32 devices in a mesh: grp: 4 (over y, core), row: 4 (over z), col: 2 (over x).
Axes of the slice: x: 2, y: 2, z: 4, core: 2. Of those that a mesh axis runs over, the one named last changes fastest.
Arguments:
- tokens: bfloat16 [16384, 2048], P(('grp', 'row', 'col')), may hold values from -6 to 6
- cotangent: bfloat16 [16384, 2048], P(('grp', 'row', 'col')), may hold values from -15 to 15
- segments: int32 [16384], P(('grp', 'row')), may hold values from 0 to 4, as said below
- positions: int32 [16384], P(('grp', 'row')), may hold values from 0 to 703, as said below
- first_gain: float32 [2048], replicated, may hold values from 0.25 to 1.75
- query_weight: bfloat16 [2048, 2048], P(None, 'col'), may hold values from -0.1875 to 0.1875
- key_matrix: bfloat16 [2048, 1024], replicated, may hold values from -0.1875 to 0.1875
- value_matrix: bfloat16 [2048, 1024], replicated, may hold values from -0.125 to 0.125
- output_weight: bfloat16 [2048, 2048], P('col'), may hold values from -1 to 1
- second_gain: float32 [2048], replicated, may hold values from 0.25 to 1.75
- gate_weight: bfloat16 [2048, 8192], P(None, ('row', 'col')), may hold values from -0.125 to 0.125
- up_weight: bfloat16 [2048, 8192], P(None, ('row', 'col')), may hold values from -0.125 to 0.125
- down_weight: bfloat16 [8192, 2048], P(('row', 'col')), may hold values from -0.09375 to 0.09375
Outputs:
- layer_out: float32 [16384, 2048], P(('grp', 'row', 'col'))
- input_grad: float32 [16384, 2048], P(('grp', 'row', 'col'))
- first_gain_grad: float32 [2048], replicated
- query_grad: float32 [2048, 2048], P(None, 'col')
- key_grad: float32 [2048, 1024], replicated
- value_grad: float32 [2048, 1024], replicated
- output_grad: float32 [2048, 2048], P('col')
- second_gain_grad: float32 [2048], replicated
- gate_grad: float32 [2048, 8192], P(None, ('row', 'col'))
- up_grad: float32 [2048, 8192], P(None, ('row', 'col'))
- down_grad: float32 [8192, 2048], P(('row', 'col'))
The draws below stay inside these ranges and needn't reach their ends.
Inputs may be any that keep to these rules, and one draw needn't show every extreme that they name: `segments`: tokens come in aligned packs of 1024: the first 512 of a pack are its prompt, segment 0; the other 512 hold its 4 continuations, numbered 1 to 4 in order, each a run of consecutive tokens of 64 to 192 tokens. A prompt's tokens have positions 0 to 511 in order; a continuation's tokens count on from 512.
All inputs are finite; a program needn't handle non-finite values.
Results may differ from the reference program's by a relative error of at most 0.02.
Values may be sent and summed in bfloat16 or wider, within the bound.
No kernel may reach another device: no remote copies, remote signals or barrier semaphores. Data moves between devices by JAX's collectives and lax.ppermute only.
A program may use at most 384 MiB of HBM per device.

```python
import math
import jax
import jax.numpy as jnp
from jax import lax

MODEL_WIDTH = 2048
QUERY_HEADS = 8
KEY_VALUE_HEADS = 4
HEAD_SIZE = 256
FF = 8192
PROMPT = 512
CONTS = 4
PACK = 1024
TOKENS = 16384
QBLOCK = 512


def pack_layout(key):
    base_key = jax.random.fold_in(key, 11)
    length_key, order_key = jax.random.split(base_key)
    pack_count = TOKENS // (2 * PROMPT)
    half_len = PROMPT // (2 * CONTS)
    pair_count = CONTS // 2
    mean_len = PROMPT // CONTS
    offsets = jax.random.randint(length_key, (pack_count, pair_count), 1, half_len + 1)
    offsets = jnp.where(jnp.arange(pair_count)[None, :] == 0, half_len, offsets)
    lengths = jnp.stack([mean_len + offsets, mean_len - offsets], axis=2).reshape(pack_count, CONTS)
    shuffle = jax.random.randint(order_key, (pack_count, CONTS), 0, 1 << 20) * CONTS + jnp.arange(CONTS)[None, :]
    permute = jnp.argsort(shuffle, axis=1)
    lengths = jnp.take_along_axis(lengths, permute, axis=1)
    run_ends = jnp.cumsum(lengths, axis=1)
    run_starts = run_ends - lengths
    offset_all = jnp.arange(PROMPT)
    run_index = jnp.sum((offset_all[None, :, None] >= run_ends[:, None, :]).astype(jnp.int32), axis=2)
    run_start = jnp.take_along_axis(run_starts, run_index, axis=1)
    cont_seg = run_index + 1
    cont_pos = PROMPT + offset_all[None, :] - run_start
    prompt_seg = jnp.zeros((pack_count, PROMPT), jnp.int32)
    prompt_pos = jnp.broadcast_to(offset_all[None, :], (pack_count, PROMPT))
    seg_all = jnp.concatenate([prompt_seg, cont_seg.astype(jnp.int32)], axis=1).reshape(-1)
    pos_all = jnp.concatenate([prompt_pos.astype(jnp.int32), cont_pos.astype(jnp.int32)], axis=1).reshape(-1)
    return (seg_all.astype(jnp.int32), pos_all.astype(jnp.int32))


def draw_segments(key, part):
    return pack_layout(key)[0]


def draw_positions(key, part):
    return pack_layout(key)[1]


def draw_cotangent(key, part):
    base_key = jax.random.fold_in(key, 5)
    rising = jnp.exp(math.log(3.0) * jnp.arange(TOKENS, dtype=jnp.float32) / (TOKENS - 1))[:, None]
    values = jnp.clip(jax.random.normal(base_key, (TOKENS, MODEL_WIDTH), jnp.float32), -5.0, 5.0) * rising
    return values.astype(jnp.bfloat16)


def level_of(key, dims, pieces, low, high):
    factor_of, own = 1.0, jax.random.fold_in(key, 6)
    for axis_at, parts in pieces:
        heights = jnp.exp(jax.random.uniform(jax.random.fold_in(own, axis_at), (parts,), jnp.float32, low / len(pieces), high / len(pieces)))
        factor_of = factor_of * jnp.repeat(heights, dims[axis_at] // parts).reshape([-1 if axis == axis_at else 1 for axis in range(len(dims))])
    return factor_of


def bell_draw(stream_key, dims, width, limit, shards=(), kind=jnp.bfloat16):
    entries = jax.random.normal(stream_key, dims, jnp.float32) * width
    if len(shards) > 0:
        entries = level_of(stream_key, dims, shards, -0.22, 0.18) * entries
    return jnp.clip(entries, min=-limit, max=limit).astype(kind)


def setup_inputs(seed: int = 0) -> dict:
    key_list = jax.random.split(jax.random.key(seed), 14)
    return {
        "tokens": bell_draw(key_list[0], (TOKENS, MODEL_WIDTH), 1.0, 6.0, ((0, 32),)),
        "cotangent": draw_cotangent(jax.random.fold_in(key_list[13], 71), 0),
        "segments": draw_segments(jax.random.fold_in(key_list[13], 71), 0),
        "positions": draw_positions(jax.random.fold_in(key_list[13], 71), 0),
        "first_gain": jnp.clip(1.0 + 0.15 * jax.random.normal(key_list[4], (MODEL_WIDTH,), jnp.float32), 0.25, 1.75),
        "query_weight": bell_draw(key_list[5], (MODEL_WIDTH, QUERY_HEADS * HEAD_SIZE), (MODEL_WIDTH // 2) ** -0.5, 0.1875, ((1, 2),)),
        "key_matrix": bell_draw(key_list[6], (MODEL_WIDTH, KEY_VALUE_HEADS * HEAD_SIZE), (MODEL_WIDTH // 2) ** -0.5, 0.1875),
        "value_matrix": bell_draw(key_list[7], (MODEL_WIDTH, KEY_VALUE_HEADS * HEAD_SIZE), MODEL_WIDTH ** -0.5, 0.125),
        "output_weight": bell_draw(key_list[8], (QUERY_HEADS * HEAD_SIZE, MODEL_WIDTH), (QUERY_HEADS * HEAD_SIZE // 64) ** -0.5, 1.0, ((0, 2),)),
        "second_gain": jnp.clip(1.0 + 0.15 * jax.random.normal(key_list[9], (MODEL_WIDTH,), jnp.float32), 0.25, 1.75),
        "gate_weight": bell_draw(key_list[10], (MODEL_WIDTH, FF), MODEL_WIDTH ** -0.5, 0.125, ((1, 8),)),
        "up_weight": bell_draw(key_list[11], (MODEL_WIDTH, FF), MODEL_WIDTH ** -0.5, 0.125, ((1, 8),)),
        "down_weight": bell_draw(key_list[12], (FF, MODEL_WIDTH), (FF // 2) ** -0.5, 0.09375, ((0, 8),)),
    }


@jax.custom_vjp
def reduced_precision(v):
    return lax.optimization_barrier(v.astype(jnp.bfloat16)).astype(jnp.float32)

@jax.custom_vjp
def reduced_precision_backward(v):
    return v

def low_keep(v):
    return (reduced_precision(v), None)

def low_pass(kept, grad):
    return (grad,)

def back_keep(v):
    return (v, None)

def back_low(kept, grad):
    return (reduced_precision(grad),)
reduced_precision.defvjp(low_keep, low_pass)
reduced_precision_backward.defvjp(back_keep, back_low)
NORM_EPSILON = 1e-06
ROPE_BASE = 1000042.0
MASKED_SCORE = -1e+30
PRECISE = lax.Precision.HIGHEST

def normalize(values, gain):
    inverse = lax.rsqrt(lax.optimization_barrier(jnp.mean(values * values, axis=-1, keepdims=True)) + NORM_EPSILON)
    return values * inverse * gain

def rope_tables(positions, head_dim):
    half_dim = head_dim // 2
    exponent = jnp.arange(half_dim, dtype=jnp.float32) * (2.0 / head_dim)
    inverse_freq = jnp.exp(-math.log(ROPE_BASE) * exponent)
    angles = positions.astype(jnp.float32)[:, None] * inverse_freq[None, :]
    return (jnp.cos(angles), jnp.sin(angles))

def rotate(values, cosine, sine):
    half_dim = values.shape[-1] // 2
    shape = (values.shape[0],) + (1,) * (values.ndim - 2) + (half_dim,)
    cosine = cosine.reshape(shape)
    sine = sine.reshape(shape)
    first_half = values[..., :half_dim]
    second_half = values[..., half_dim:]
    return jnp.concatenate([first_half * cosine - second_half * sine, second_half * cosine + first_half * sine], axis=-1)

def matrix_multiply(left, right):
    return jnp.dot(left, right, precision=PRECISE, preferred_element_type=jnp.float32)

def pack_forward(params, inputs, segments, positions):
    first_gain, query_weight, key_matrix, value_matrix, output_weight, second_gain, gate_weight, up_weight, down_weight = params
    packed_length = inputs.shape[0]
    heads_per_group = QUERY_HEADS // KEY_VALUE_HEADS
    normalized_input = reduced_precision(normalize(inputs, first_gain))
    query_lin = reduced_precision_backward(matrix_multiply(normalized_input, query_weight).reshape(packed_length, QUERY_HEADS, HEAD_SIZE))
    key_linear = reduced_precision_backward(jnp.repeat(matrix_multiply(normalized_input, key_matrix).reshape(packed_length, KEY_VALUE_HEADS, HEAD_SIZE), heads_per_group, axis=1))
    value_reduced = reduced_precision(reduced_precision_backward(jnp.repeat(matrix_multiply(normalized_input, value_matrix).reshape(packed_length, KEY_VALUE_HEADS, HEAD_SIZE), heads_per_group, axis=1)))
    cosine, sine = rope_tables(positions, HEAD_SIZE)
    query_low = reduced_precision(rotate(query_lin, cosine, sine))
    key_low = reduced_precision(rotate(key_linear, cosine, sine))
    block_count = packed_length // QBLOCK

    def attend(block):
        query_block, seg_block, pos_block = block
        raw = jnp.einsum('qhd,khd->hqk', query_block, key_low, precision=PRECISE) * HEAD_SIZE ** (-0.5)
        scores = reduced_precision_backward(raw)
        allowed = (positions[None, :] <= pos_block[:, None]) & ((segments[None, :] == 0) | (segments[None, :] == seg_block[:, None]))
        scores = jnp.where(allowed[None, :, :], scores, MASKED_SCORE)
        peak = lax.optimization_barrier(jnp.max(scores, axis=-1, keepdims=True))
        log_total = peak + jnp.log(lax.optimization_barrier(jnp.sum(jnp.exp(scores - peak), axis=-1, keepdims=True)))
        probs = reduced_precision(jnp.exp(scores - log_total))
        return jnp.einsum('hqk,khd->qhd', probs, value_reduced, precision=PRECISE)
    mixed = lax.map(jax.checkpoint(attend), (query_low.reshape(block_count, QBLOCK, QUERY_HEADS, HEAD_SIZE), segments.reshape(block_count, QBLOCK), positions.reshape(block_count, QBLOCK)))
    attn_low = reduced_precision(reduced_precision_backward(mixed.reshape(packed_length, QUERY_HEADS * HEAD_SIZE)))
    hidden_res = inputs + reduced_precision_backward(matrix_multiply(attn_low, output_weight))
    normed_mid = reduced_precision(normalize(hidden_res, second_gain))
    gate_lin = reduced_precision_backward(matrix_multiply(normed_mid, gate_weight))
    up_lin = reduced_precision_backward(matrix_multiply(normed_mid, up_weight))
    act_low = reduced_precision(jax.nn.silu(gate_lin) * up_lin)
    return hidden_res + reduced_precision_backward(matrix_multiply(act_low, down_weight))

def reference(tokens, cotangent, segments, positions, first_gain, query_weight, key_matrix, value_matrix, output_weight, second_gain, gate_weight, up_weight, down_weight):
    params = tuple((matrix.astype(jnp.float32) for matrix in (first_gain, query_weight, key_matrix, value_matrix, output_weight, second_gain, gate_weight, up_weight, down_weight)))
    pack_count = TOKENS // PACK
    inputs = tokens.astype(jnp.float32).reshape(pack_count, PACK, MODEL_WIDTH)
    out_grads = cotangent.astype(jnp.float32).reshape(pack_count, PACK, MODEL_WIDTH)
    pack_segs = segments.reshape(pack_count, PACK)
    pack_poss = positions.reshape(pack_count, PACK)

    def one_pack(totals, pack):
        pack_in, pack_cot, pack_seg, pack_pos = pack

        def forward(params_now, inputs_now):
            return pack_forward(params_now, inputs_now, pack_seg, pack_pos)
        pack_out, backward = jax.vjp(forward, params, pack_in)
        param_grads, pack_in_grad = backward(pack_cot)
        totals = jax.tree.map(jnp.add, totals, param_grads)
        return (totals, (pack_out, pack_in_grad))
    zero_grads = jax.tree.map(jnp.zeros_like, params)
    totals, (layer_out, input_grad) = lax.scan(one_pack, zero_grads, (inputs, out_grads, pack_segs, pack_poss))
    return (layer_out.reshape(TOKENS, MODEL_WIDTH), input_grad.reshape(TOKENS, MODEL_WIDTH), totals[0], totals[1], totals[2], totals[3], totals[4], totals[5], totals[6], totals[7], totals[8])
```

```python
import math

import jax
import jax.numpy as jnp
from jax import lax
from jax.sharding import PartitionSpec as P

QUERY_HEADS = 8
KEY_VALUE_HEADS = 4
HEAD_SIZE = 256
QBLOCK = 512


NORM_EPSILON = 1e-06
ROPE_BASE = 1000042.0
MASKED_SCORE = -1e30


def normalize(values, gain):
    inverse = lax.rsqrt(jnp.mean(values * values, axis=-1, keepdims=True) + NORM_EPSILON)
    return values * inverse * gain


def rope_tables(positions, head_dim):
    half_dim = head_dim // 2
    exponent = jnp.arange(half_dim, dtype=jnp.float32) * (2.0 / head_dim)
    inverse_freq = jnp.exp(-math.log(ROPE_BASE) * exponent)
    angles = positions.astype(jnp.float32)[:, None] * inverse_freq[None, :]
    return (jnp.cos(angles), jnp.sin(angles))


def rotate(values, cosine, sine):
    half_dim = values.shape[-1] // 2
    shape = (values.shape[0],) + (1,) * (values.ndim - 2) + (half_dim,)
    cosine = cosine.reshape(shape)
    sine = sine.reshape(shape)
    first_half = values[..., :half_dim]
    second_half = values[..., half_dim:]
    return jnp.concatenate(
        [first_half * cosine - second_half * sine, second_half * cosine + first_half * sine],
        axis=-1,
    )


def swap(value, axis, bit):
    count = lax.axis_size(axis)
    return lax.ppermute(value, axis, [(i, i ^ bit) for i in range(count)])


def shift(value, axis, step):
    count = lax.axis_size(axis)
    return lax.ppermute(value, axis, [(i, (i + step) % count) for i in range(count)])


def after(value, *others):
    return lax.optimization_barrier((value, *others))[0]


def ordered(first_when_zero, mine, theirs, dim):
    keep = first_when_zero == 0
    return jnp.concatenate(
        [jnp.where(keep, mine, theirs), jnp.where(keep, theirs, mine)], axis=dim
    )


def dot32(left, right):
    return jnp.dot(left, right, preferred_element_type=jnp.float32)


def dot_nt(left, right):
    return jnp.einsum("td,fd->tf", left, right, preferred_element_type=jnp.float32)


def dot_tn(left, right):
    return jnp.einsum("td,tf->df", left, right, preferred_element_type=jnp.float32)


def low(value):
    return value.astype(jnp.bfloat16)


def wide(value):
    return value.astype(jnp.float32)


def col_gather(mine):
    if lax.axis_size("col") == 2:
        return [mine, swap(mine, "col", 1)]
    return [lax.all_gather(mine, "col", axis=0, tiled=True)]


def col_scatter(product):
    if lax.axis_size("col") == 2:
        theirs = swap(low(product(1)), "col", 1)
        return product(0) + wide(theirs)
    return wide(lax.psum_scatter(low(product(0)), "col", scatter_dimension=0, tiled=True))


def butterfly(value, axes):
    for axis in axes:
        bit = 1
        while bit < lax.axis_size(axis):
            value = value + swap(value, axis, bit)
            bit *= 2
    return value


def half_rows(value, bit):
    size = value.shape[0] // 2
    return lax.dynamic_slice_in_dim(value, bit * size, size, 0)


def sum_copies(value, core, ypos, zpos):
    part = low(wide(half_rows(value, core)) + wide(swap(half_rows(value, 1 - core), "grp", 1)))
    part = low(wide(half_rows(part, ypos)) + wide(swap(half_rows(part, 1 - ypos), "grp", 2)))
    count = lax.axis_size("row")
    size = part.shape[0] // count

    def block(i):
        return lax.dynamic_slice_in_dim(part, lax.rem(zpos + i, count) * size, size, 0)

    total = wide(block(0))
    for k in range(1, count):
        total = total + wide(shift(block(k), "row", k))
    mine = low(total)
    part = jnp.zeros_like(part)
    for k in range(count):
        piece = mine if k == 0 else shift(mine, "row", k)
        part = lax.dynamic_update_slice_in_dim(
            part, piece, lax.rem(zpos - k + count, count) * size, 0
        )
    part = ordered(ypos, part, swap(part, "grp", 2), 0)
    return ordered(core, part, swap(part, "grp", 1), 0)


def pieces_of(weight, dim, core, ypos):
    size = weight.shape[dim] // 4
    mine = lax.dynamic_slice_in_dim(weight, (2 * core + ypos) * size, size, dim)
    other = lax.dynamic_slice_in_dim(weight, (2 * core + 1 - ypos) * size, size, dim)
    return mine, other


def gather_weight(weight, dim, core, ypos):
    mine, other = pieces_of(weight, dim, core, ypos)
    mines, others = [mine], [other]
    for _ in range(lax.axis_size("row") - 1):
        mines.append(shift(mines[-1], "row", 1))
        others.append(swap(mines[-1], "grp", 2))
    return jnp.concatenate(mines + others, axis=dim)


def blocks_of(value, dim, count):
    size = value.shape[dim] // count
    return [lax.slice_in_dim(value, i * size, (i + 1) * size, axis=dim) for i in range(count)]


def ring_sum(blocks):
    total = blocks[-1]
    for block in blocks[-2::-1]:
        total = low(wide(shift(total, "row", -1)) + wide(block))
    return total


def place(mine, other, dim, core, ypos):
    half = ordered(ypos, mine, other, dim)
    return wide(ordered(core, half, swap(half, "grp", 1), dim))


def sum_y_first(grad, dim, core, ypos):
    keep, give = blocks_of(grad, dim, 2)
    part = low(wide(keep) + wide(swap(give, "grp", 2)))
    mine = ring_sum(blocks_of(part, dim, lax.axis_size("row")))
    return place(mine, swap(mine, "grp", 2), dim, core, ypos)


def sum_z_first(grad, dim, core, ypos):
    keep, give = blocks_of(grad, dim, 2)
    count = lax.axis_size("row")
    mine = ring_sum(blocks_of(keep, dim, count))
    other = ring_sum(blocks_of(give, dim, count))
    mine, other = (
        low(wide(mine) + wide(swap(other, "grp", 2))),
        low(wide(other) + wide(swap(mine, "grp", 2))),
    )
    return place(mine, other, dim, core, ypos)


def per_device(
    tokens,
    cotangent,
    segments,
    positions,
    first_gain,
    query_weight,
    key_matrix,
    value_matrix,
    output_weight,
    second_gain,
    gate_weight,
    up_weight,
    down_weight,
):
    head_dim = HEAD_SIZE
    query_heads = query_weight.shape[1] // head_dim
    heads_per_group = QUERY_HEADS // KEY_VALUE_HEADS
    key_heads = max(1, query_heads // heads_per_group)
    head_share = query_heads // key_heads
    head_sharing = max(1, heads_per_group // query_heads)
    col = lax.axis_index("col")
    key_first = col * query_heads // heads_per_group
    query_cols = query_heads * head_dim
    key_cols = key_heads * head_dim
    rows, width = tokens.shape
    grp, zpos = lax.axis_index("grp"), lax.axis_index("row")
    core, ypos = lax.rem(grp, 2), lax.div(grp, 2)
    in_pairs = lax.axis_size("col") == 2

    inputs = wide(tokens)
    normalized_input, first_back = jax.vjp(normalize, inputs, first_gain)
    gathered_in = jnp.concatenate(col_gather(low(normalized_input)), axis=0)
    packed_length = gathered_in.shape[0]
    if in_pairs:
        segments = ordered(col, *blocks_of(segments, 0, 2), 0)
        positions = ordered(col, *blocks_of(positions, 0, 2), 0)

    down_all = gather_weight(down_weight, 0, core, ypos)
    gate_all = gather_weight(gate_weight, 1, core, ypos)
    up_all = gather_weight(up_weight, 1, core, ypos)

    cot_now = after(cotangent, gathered_in)
    cot_pack = jnp.concatenate(col_gather(cot_now), axis=0)
    cot_all = jnp.concatenate([cot_pack, swap(cot_pack, "grp", 1)], axis=0)

    key_slice = lax.dynamic_slice_in_dim(key_matrix, key_first * head_dim, key_cols, 1)
    value_slice = lax.dynamic_slice_in_dim(value_matrix, key_first * head_dim, key_cols, 1)
    project_in = jnp.concatenate([query_weight, key_slice, value_slice], axis=1)
    projected = dot32(gathered_in, project_in)
    cosine, sine = rope_tables(positions, head_dim)
    query_low = low(
        rotate(
            projected[:, :query_cols].reshape(packed_length, key_heads, head_share, head_dim),
            cosine,
            sine,
        )
    )
    key_low = low(
        rotate(
            projected[:, query_cols : query_cols + key_cols].reshape(
                packed_length, key_heads, head_dim
            ),
            cosine,
            sine,
        )
    )
    value_reduced = low(
        projected[:, query_cols + key_cols :].reshape(packed_length, key_heads, head_dim)
    )
    block_count = packed_length // QBLOCK
    query_blocks = query_low.reshape(block_count, QBLOCK, key_heads, head_share, head_dim)
    seg_blocks = segments.reshape(block_count, QBLOCK)
    pos_blocks = positions.reshape(block_count, QBLOCK)
    score_scale = head_dim ** (-0.5)

    def block_scores(query_block, seg_block, pos_block):
        raw = (
            jnp.einsum("qgrd,kgd->grqk", query_block, key_low, preferred_element_type=jnp.float32)
            * score_scale
        )
        allowed = (positions[None, :] <= pos_block[:, None]) & (
            (segments[None, :] == 0) | (segments[None, :] == seg_block[:, None])
        )
        return jnp.where(allowed[None, None, :, :], raw, MASKED_SCORE)

    def attend(block):
        query_block, seg_block, pos_block = block
        scores = block_scores(query_block, seg_block, pos_block)
        peak = jnp.max(scores, axis=-1, keepdims=True)
        log_total = peak + jnp.log(jnp.sum(jnp.exp(scores - peak), axis=-1, keepdims=True))
        probs_low = jnp.exp(scores - log_total).astype(jnp.bfloat16)
        mixed = jnp.einsum(
            "grqk,kgd->qgrd", probs_low, value_reduced, preferred_element_type=jnp.float32
        )
        return (mixed, log_total[..., 0])

    mixed_all, log_totals = lax.map(attend, (query_blocks, seg_blocks, pos_blocks))
    attn_low = low(mixed_all.reshape(packed_length, query_cols))
    attn_parts = blocks_of(attn_low, 0, 2) if in_pairs else [attn_low]
    hidden_res = inputs + col_scatter(lambda i: dot32(attn_parts[i], output_weight))
    normed_mid, second_back = jax.vjp(normalize, hidden_res, second_gain)

    mid_pack = jnp.concatenate(col_gather(low(normed_mid)), axis=0)
    mid_all = jnp.concatenate([mid_pack, swap(mid_pack, "grp", 1)], axis=0)
    act_grad = low(dot_nt(cot_all, down_all))
    gate_lin = low(dot32(mid_all, gate_all))
    up_lin = dot32(mid_all, up_all)
    gate32 = wide(gate_lin)
    sig = jax.nn.sigmoid(gate32)
    act_low = low(gate32 * sig * up_lin)
    gate_grad_low = low(wide(act_grad) * up_lin * sig * (1 + gate32 * (1 - sig)))
    up_grad_low = low(wide(act_grad) * gate32 * sig)
    down_wgrad = low(dot_tn(act_low, cot_all))
    down_grad = sum_z_first(down_wgrad, 0, core, ypos)
    gate_wgrad = low(dot_tn(mid_all, gate_grad_low))
    gate_grad = sum_y_first(gate_wgrad, 1, core, ypos)
    up_wgrad = low(dot_tn(mid_all, up_grad_low))
    up_grad = sum_y_first(up_wgrad, 1, core, ypos)

    def pack_sum(value):
        mine, theirs = blocks_of(value, 0, 2)
        return wide(mine) + wide(swap(low(theirs), "grp", 1))

    mid_part = pack_sum(dot_nt(gate_grad_low, gate_all) + dot_nt(up_grad_low, up_all))
    mid_parts = blocks_of(mid_part, 0, 2) if in_pairs else [mid_part]
    mid_grad = col_scatter(lambda i: mid_parts[i])
    out_part = pack_sum(dot32(act_low, down_all))
    out_parts = blocks_of(out_part, 0, 2) if in_pairs else [out_part]
    layer_out = hidden_res + col_scatter(lambda i: out_parts[i])

    res_from_mid, second_gain_part = second_back(mid_grad)
    res_grad = wide(cotangent) + res_from_mid
    shard_rows = jnp.concatenate(col_gather(low(res_grad)), axis=0)
    out_wgrad = sum_copies(low(dot_tn(attn_low, shard_rows)), core, ypos, zpos)
    mixed_low = low(dot_nt(shard_rows, output_weight)).reshape(
        block_count, QBLOCK, key_heads, head_share, head_dim
    )

    def attend_back(totals, block):
        query_block, seg_block, pos_block, mixed_block, log_block = block
        scores = block_scores(query_block, seg_block, pos_block)
        probs = jnp.exp(scores - log_block[..., None])
        probs_low = probs.astype(jnp.bfloat16)
        value_total = totals[1] + jnp.einsum(
            "grqk,qgrd->kgd", probs_low, mixed_block, preferred_element_type=jnp.float32
        )
        prob_grad = jnp.einsum(
            "qgrd,kgd->grqk", mixed_block, value_reduced, preferred_element_type=jnp.float32
        )
        row_dot = jnp.sum(probs * prob_grad, axis=-1, keepdims=True)
        score_low = (probs * (prob_grad - row_dot)).astype(jnp.bfloat16)
        query_grad_rows = (
            jnp.einsum("grqk,kgd->qgrd", score_low, key_low, preferred_element_type=jnp.float32)
            * score_scale
        )
        key_total = (
            totals[0]
            + jnp.einsum(
                "grqk,qgrd->kgd", score_low, query_block, preferred_element_type=jnp.float32
            )
            * score_scale
        )
        return ((key_total, value_total), query_grad_rows)

    zero_heads = jnp.zeros((packed_length, key_heads, head_dim), jnp.float32)
    (key_grad_rot, value_head_grad), query_grad_blocks = lax.scan(
        attend_back,
        (zero_heads, zero_heads),
        (query_blocks, seg_blocks, pos_blocks, mixed_low, log_totals),
    )
    query_grad_rot = query_grad_blocks.reshape(packed_length, key_heads, head_share, head_dim)
    query_back = low(rotate(query_grad_rot, cosine, -sine)).reshape(packed_length, query_cols)
    key_back = low(rotate(key_grad_rot, cosine, -sine)).reshape(packed_length, key_cols)
    value_back = low(value_head_grad).reshape(packed_length, key_cols)
    back_all = jnp.concatenate([query_back, key_back, value_back], axis=1)
    proj_grad = sum_copies(low(dot_tn(gathered_in, back_all)), core, ypos, zpos)
    back_parts = blocks_of(back_all, 0, 2) if in_pairs else [back_all]
    in_grad = col_scatter(lambda i: dot_nt(back_parts[i], project_in))
    res_from_in, first_gain_part = first_back(in_grad)
    input_grad = res_grad + res_from_in

    query_wgrad = wide(proj_grad[:, :query_cols])
    pair_part = proj_grad[:, query_cols:]
    if in_pairs:
        theirs = swap(pair_part, "col", 1)
        key_full = wide(ordered(col, pair_part[:, :key_cols], theirs[:, :key_cols], 1))
        value_full = wide(ordered(col, pair_part[:, key_cols:], theirs[:, key_cols:], 1))
    else:
        pair_all = wide(lax.all_gather(pair_part, "col", axis=0))
        groups = lax.axis_size("col") // head_sharing

        def spread(piece):
            piece = jnp.sum(piece.reshape(groups, head_sharing, width, key_cols), axis=1)
            return jnp.swapaxes(piece, 0, 1).reshape(width, groups * key_cols)

        key_full = spread(pair_all[..., :key_cols])
        value_full = spread(pair_all[..., key_cols:])
    axes = ("grp", "row", "col")
    first_gain_grad = butterfly(first_gain_part.reshape(8, -1), axes).reshape(-1)
    second_gain_grad = butterfly(second_gain_part.reshape(8, -1), axes).reshape(-1)
    return (
        layer_out,
        input_grad,
        first_gain_grad,
        query_wgrad,
        key_full,
        value_full,
        wide(out_wgrad),
        second_gain_grad,
        gate_grad,
        up_grad,
        down_grad,
    )


def solution(mesh):
    return jax.shard_map(
        per_device,
        mesh=mesh,
        in_specs=(
            P(("grp", "row", "col"), None),
            P(("grp", "row", "col"), None),
            P(("grp", "row")),
            P(("grp", "row")),
            P(),
            P(None, "col"),
            P(),
            P(),
            P("col", None),
            P(),
            P(None, ("row", "col")),
            P(None, ("row", "col")),
            P(("row", "col"), None),
        ),
        out_specs=(
            P(("grp", "row", "col"), None),
            P(("grp", "row", "col"), None),
            P(),
            P(None, "col"),
            P(),
            P(),
            P("col", None),
            P(),
            P(None, ("row", "col")),
            P(None, ("row", "col")),
            P(("row", "col"), None),
        ),
        check_vma=False,
    )
```

```python
import math

import jax
import jax.numpy as jnp
from jax import lax
from jax.experimental import pallas as pl
from jax.experimental.pallas import tpu as pltpu
from jax.sharding import PartitionSpec as P

QUERY_HEADS = 8
KEY_VALUE_HEADS = 4
HEAD_SIZE = 256


NORM_EPSILON = 1e-06
ROPE_BASE = 1000042.0
MASKED_SCORE = -1e30


def normalize(values, gain):
    inverse = lax.rsqrt(jnp.mean(values * values, axis=-1, keepdims=True) + NORM_EPSILON)
    return values * inverse * gain


def rope_tables(positions, head_dim):
    half_dim = head_dim // 2
    exponent = jnp.arange(half_dim, dtype=jnp.float32) * (2.0 / head_dim)
    inverse_freq = jnp.exp(-math.log(ROPE_BASE) * exponent)
    angles = positions.astype(jnp.float32)[:, None] * inverse_freq[None, :]
    return (jnp.cos(angles), jnp.sin(angles))


def turn(value, cosine, sine):
    half = value.shape[-1] // 2
    first, second = value[:, :half], value[:, half:]
    return jnp.concatenate(
        [first * cosine - second * sine, second * cosine + first * sine], axis=-1
    )


def kernel_dot(left, right, left_dim, right_dim):
    return lax.dot_general(
        left, right, (((left_dim,), (right_dim,)), ((), ())), preferred_element_type=jnp.float32
    )


def query_spans(length):
    step = length // 4
    return [(i * step, step, (i + 1) * step) for i in range(4)]


def allowed_keys(place, start, size, keys):
    pos_row, pos_col, seg_row, seg_col = place
    key_seg = seg_row[:, :keys]
    return (pos_row[:, :keys] <= pos_col[start : start + size, :]) & (
        (key_seg == 0) | (key_seg == seg_col[start : start + size, :])
    )


def stored_rows(first_ref, length):
    half = length // 2
    offsets = [first_ref[0] * half, (1 - first_ref[0]) * half]

    def rows(start, size):
        offset = pl.multiple_of(offsets[start // half] + start % half, size)
        return pl.ds(offset, size)

    return rows


def attend_kernel(
    first_ref, q_ref, k_ref, v_ref, cos_ref, sin_ref, pr_ref, pc_ref, sr_ref, sc_ref,
    out_ref, q_low_ref, k_low_ref, v_low_ref, key_ref, value_ref,
):
    length, head_dim = k_ref.shape
    rows = stored_rows(first_ref, length)
    place = (pr_ref, pc_ref, sr_ref, sc_ref)
    for start, size, _ in query_spans(length):
        span = slice(start, start + size)
        key = turn(k_ref[rows(start, size), :], cos_ref[span, :], sin_ref[span, :])
        key = key.astype(jnp.bfloat16)
        value = v_ref[rows(start, size), :].astype(jnp.bfloat16)
        key_ref[span, :] = key
        value_ref[span, :] = value
        k_low_ref[rows(start, size), :] = key
        v_low_ref[rows(start, size), :] = value
    for start, size, keys in query_spans(length):
        span = slice(start, start + size)
        allowed = allowed_keys(place, start, size, keys)
        for head in range(q_ref.shape[1] // head_dim):
            cols = slice(head * head_dim, (head + 1) * head_dim)
            query = turn(q_ref[rows(start, size), cols], cos_ref[span, :], sin_ref[span, :])
            query = query.astype(jnp.bfloat16)
            q_low_ref[rows(start, size), cols] = query
            scores = kernel_dot(query, key_ref[:keys, :], 1, 1) * head_dim**-0.5
            scores = jnp.where(allowed, scores, MASKED_SCORE)
            weights = jnp.exp(scores - jnp.max(scores, axis=1, keepdims=True))
            weights = weights * (1 / jnp.sum(weights, axis=1, keepdims=True))
            mixed = kernel_dot(weights.astype(jnp.bfloat16), value_ref[:keys, :], 1, 0)
            out_ref[rows(start, size), cols] = mixed.astype(jnp.bfloat16)


def attend_back_kernel(
    first_ref, q_ref, k_ref, v_ref, m_ref, cos_ref, sin_ref, pr_ref, pc_ref, sr_ref, sc_ref,
    q_back_ref, k_back_ref, v_back_ref, key_ref, value_ref, key_sum, value_sum,
):
    length, head_dim = k_ref.shape
    scale = head_dim**-0.5
    rows = stored_rows(first_ref, length)
    place = (pr_ref, pc_ref, sr_ref, sc_ref)
    for start, size, _ in query_spans(length):
        span = slice(start, start + size)
        key_ref[span, :] = k_ref[rows(start, size), :]
        value_ref[span, :] = v_ref[rows(start, size), :]
    key_sum[...] = jnp.zeros_like(key_sum)
    value_sum[...] = jnp.zeros_like(value_sum)
    for start, size, keys in query_spans(length):
        span = slice(start, start + size)
        allowed = allowed_keys(place, start, size, keys)
        for head in range(q_ref.shape[1] // head_dim):
            cols = slice(head * head_dim, (head + 1) * head_dim)
            query = q_ref[rows(start, size), cols]
            mixed = m_ref[rows(start, size), cols]
            scores = kernel_dot(query, key_ref[:keys, :], 1, 1) * scale
            scores = jnp.where(allowed, scores, MASKED_SCORE)
            probs = jnp.exp(scores - jnp.max(scores, axis=1, keepdims=True))
            probs = probs * (1 / jnp.sum(probs, axis=1, keepdims=True))
            value_sum[:keys, :] += kernel_dot(probs.astype(jnp.bfloat16), mixed, 0, 0)
            prob_grad = kernel_dot(mixed, value_ref[:keys, :], 1, 1)
            row_dot = jnp.sum(probs * prob_grad, axis=1, keepdims=True)
            score_low = (probs * (prob_grad - row_dot)).astype(jnp.bfloat16)
            key_sum[:keys, :] += kernel_dot(score_low, query, 0, 0)
            query_grad = kernel_dot(score_low, key_ref[:keys, :], 1, 0) * scale
            query_grad = turn(query_grad, cos_ref[span, :], -sin_ref[span, :])
            q_back_ref[rows(start, size), cols] = query_grad.astype(jnp.bfloat16)
    for start, size, _ in query_spans(length):
        span = slice(start, start + size)
        key_grad = turn(key_sum[span, :] * scale, cos_ref[span, :], -sin_ref[span, :])
        k_back_ref[rows(start, size), :] = key_grad.astype(jnp.bfloat16)
        v_back_ref[rows(start, size), :] = value_sum[span, :].astype(jnp.bfloat16)


def attention_call(kernel, name, first, heads, tables, outs, scratch, head_dim, flops):
    length = heads[0][0].shape[0]
    key_heads = flops[1]

    def head_spec(width, start):
        return pl.BlockSpec((length, width), lambda g, first_ref: (0, start + g))

    def whole_spec(shape):
        return pl.BlockSpec(shape, lambda g, first_ref: (0, 0))

    return pl.pallas_call(
        kernel,
        grid_spec=pltpu.PrefetchScalarGridSpec(
            num_scalar_prefetch=1,
            grid=(key_heads,),
            in_specs=[head_spec(width, start) for _, width, start in heads]
            + [whole_spec(table.shape) for table in tables],
            out_specs=[head_spec(width, 0) for width in outs],
            scratch_shapes=[pltpu.VMEM((length, head_dim), kind) for kind in scratch],
        ),
        out_shape=[
            jax.ShapeDtypeStruct((length, width * key_heads), jnp.bfloat16) for width in outs
        ],
        cost_estimate=pl.CostEstimate(
            flops=flops[0], bytes_accessed=flops[0] // 200, transcendentals=length * length
        ),
        name=name,
    )(first, *[array for array, _, _ in heads], *tables)


def swap(value, axis, bit):
    count = lax.axis_size(axis)
    return lax.ppermute(value, axis, [(i, i ^ bit) for i in range(count)])


def shift(value, axis, step):
    count = lax.axis_size(axis)
    return lax.ppermute(value, axis, [(i, (i + step) % count) for i in range(count)])


def tie(*values):
    return lax.optimization_barrier(values)


def ordered(first_when_zero, mine, theirs, dim):
    keep = first_when_zero == 0
    return jnp.concatenate(
        [jnp.where(keep, mine, theirs), jnp.where(keep, theirs, mine)], axis=dim
    )


def dot32(left, right):
    return jnp.dot(left, right, preferred_element_type=jnp.float32)


def dot_nt(left, right):
    return jnp.einsum("td,fd->tf", left, right, preferred_element_type=jnp.float32)


def dot_tn(left, right):
    return jnp.einsum("td,tf->df", left, right, preferred_element_type=jnp.float32)


def low(value):
    return value.astype(jnp.bfloat16)


def wide(value):
    return value.astype(jnp.float32)


def col_gather(mine):
    if lax.axis_size("col") == 2:
        return [mine, swap(mine, "col", 1)]
    return [lax.all_gather(mine, "col", axis=0, tiled=True)]


def col_scatter(product):
    if lax.axis_size("col") == 2:
        theirs = swap(low(product(1)), "col", 1)
        return product(0) + wide(theirs)
    return wide(lax.psum_scatter(low(product(0)), "col", scatter_dimension=0, tiled=True))


def blocks_of(value, dim, count):
    size = value.shape[dim] // count
    return [lax.slice_in_dim(value, i * size, (i + 1) * size, axis=dim) for i in range(count)]


def butterfly(value, axes):
    for axis in axes:
        bit = 1
        while bit < lax.axis_size(axis):
            value = value + swap(value, axis, bit)
            bit *= 2
    return value


def half_rows(value, bit):
    size = value.shape[0] // 2
    return lax.dynamic_slice_in_dim(value, bit * size, size, 0)


def row_gather(value):
    return lax.all_gather(value, "row", axis=0, tiled=True)


def row_scatter(value):
    return lax.psum_scatter(value, "row", scatter_dimension=0, tiled=True)


def sum_quarters(value, core, ypos):
    part = low(wide(half_rows(value, core)) + wide(swap(half_rows(value, 1 - core), "grp", 1)))
    part = low(wide(half_rows(part, ypos)) + wide(swap(half_rows(part, 1 - ypos), "grp", 2)))
    return row_gather(row_scatter(part))


def spread_y(part, ypos):
    return ordered(ypos, part, swap(part, "grp", 2), 0)


def spread_core(part, core):
    return ordered(core, part, swap(part, "grp", 1), 0)


def own_quarters(weight, core, ypos):
    size = weight.shape[0] // 4
    mine = lax.dynamic_slice_in_dim(weight, (2 * core + ypos) * size, size, 0)
    other = lax.dynamic_slice_in_dim(weight, (2 * core + 1 - ypos) * size, size, 0)
    return mine, other


def other_quarters(mines, other, zpos):
    count = lax.axis_size("row")
    size = other.shape[0]
    turned = jnp.concatenate(
        [
            lax.dynamic_slice_in_dim(mines, lax.rem(zpos + k, count) * size, size, 0)
            for k in range(1, count)
        ],
        axis=0,
    )
    theirs = swap(turned, "grp", 2)
    others = lax.dynamic_update_slice_in_dim(jnp.zeros_like(mines), other, zpos * size, 0)
    for k in range(1, count):
        others = lax.dynamic_update_slice_in_dim(
            others,
            lax.slice_in_dim(theirs, (k - 1) * size, k * size, axis=0),
            lax.rem(zpos + k, count) * size,
            0,
        )
    return others


def sum_y_first(keep, give, core, ypos):
    part = low(wide(keep) + wide(swap(give, "grp", 2)))
    mine = row_scatter(part)
    return spread_core(spread_y(mine, ypos), core)


def sum_z_first(keep, give, core, ypos):
    mine, other = row_scatter(keep), row_scatter(give)
    mine, other = (
        low(wide(mine) + wide(swap(other, "grp", 2))),
        low(wide(other) + wide(swap(mine, "grp", 2))),
    )
    return spread_core(ordered(ypos, mine, other, 0), core)


def per_device(
    tokens,
    cotangent,
    segments,
    positions,
    first_gain,
    query_weight,
    key_matrix,
    value_matrix,
    output_weight,
    second_gain,
    gate_weight,
    up_weight,
    down_weight,
):
    head_dim = HEAD_SIZE
    query_heads = query_weight.shape[1] // head_dim
    heads_per_group = QUERY_HEADS // KEY_VALUE_HEADS
    key_heads = max(1, query_heads // heads_per_group)
    head_share = query_heads // key_heads
    head_sharing = max(1, heads_per_group // query_heads)
    col = lax.axis_index("col")
    key_first = col * query_heads // heads_per_group
    query_cols = query_heads * head_dim
    key_cols = key_heads * head_dim
    rows, width = tokens.shape
    grp, zpos = lax.axis_index("grp"), lax.axis_index("row")
    core, ypos = lax.rem(grp, 2), lax.div(grp, 2)
    in_pairs = lax.axis_size("col") == 2

    inputs = wide(tokens)
    normalized_input, first_back = jax.vjp(normalize, inputs, first_gain)
    gathered_in = jnp.concatenate(col_gather(low(normalized_input)), axis=0)
    packed_length = gathered_in.shape[0]

    down_mine, down_other = own_quarters(down_weight, core, ypos)
    gate_mine, gate_other = own_quarters(gate_weight.T, core, ypos)
    up_mine, up_other = own_quarters(up_weight.T, core, ypos)
    down_mines, gate_mines, up_mines = [row_gather(m) for m in (down_mine, gate_mine, up_mine)]

    gathered_in, cot_now = tie(gathered_in, cotangent)
    cot_pack = jnp.concatenate(col_gather(cot_now), axis=0)
    cot_all = jnp.concatenate([cot_pack, swap(cot_pack, "grp", 1)], axis=0)

    key_slice = lax.dynamic_slice_in_dim(key_matrix, key_first * head_dim, key_cols, 1)
    value_slice = lax.dynamic_slice_in_dim(value_matrix, key_first * head_dim, key_cols, 1)
    project_in = jnp.concatenate([query_weight, key_slice, value_slice], axis=1)
    projected = dot32(gathered_in, project_in)
    cosine, sine = rope_tables(positions, head_dim)
    tables = (cosine, sine, positions[None], positions[:, None], segments[None], segments[:, None])
    first = (col if in_pairs else jnp.zeros_like(col)).astype(jnp.int32).reshape(1)
    group_cols = head_share * head_dim
    score_flops = query_cols * packed_length * packed_length
    attn_low, query_low, key_low, value_low = attention_call(
        attend_kernel,
        "attend",
        first,
        [
            (projected, group_cols, 0),
            (projected, head_dim, query_heads),
            (projected, head_dim, query_heads + key_heads),
        ],
        tables,
        (group_cols, group_cols, head_dim, head_dim),
        (jnp.bfloat16, jnp.bfloat16),
        head_dim,
        (3 * score_flops, key_heads),
    )
    attn_low, down_mines = tie(attn_low, down_mines)
    down_all = [down_mines, other_quarters(down_mines, down_other, zpos)]
    attn_parts = blocks_of(attn_low, 0, 2) if in_pairs else [attn_low]
    hidden_res = inputs + col_scatter(lambda i: dot32(attn_parts[i], output_weight))
    normed_mid, second_back = jax.vjp(normalize, hidden_res, second_gain)

    mid_pack = jnp.concatenate(col_gather(low(normed_mid)), axis=0)
    mid_pack, gate_mines = tie(mid_pack, gate_mines)
    gate_all = [gate_mines, other_quarters(gate_mines, gate_other, zpos)]
    up_all = [up_mines, other_quarters(up_mines, up_other, zpos)]
    mid_all = jnp.concatenate([mid_pack, swap(mid_pack, "grp", 1)], axis=0)
    acts, gate_backs, up_backs = [], [], []
    for gate_rows, up_rows, down_rows in zip(gate_all, up_all, down_all):
        act_grad = low(dot_nt(cot_all, down_rows))
        gate32 = wide(low(dot_nt(mid_all, gate_rows)))
        up_lin = dot_nt(mid_all, up_rows)
        sig = jax.nn.sigmoid(gate32)
        acts.append(low(gate32 * sig * up_lin))
        gate_backs.append(low(wide(act_grad) * up_lin * sig * (1 + gate32 * (1 - sig))))
        up_backs.append(low(wide(act_grad) * gate32 * sig))
    down_parts = [low(dot_tn(act, cot_all)) for act in acts]
    gate_parts = [low(dot_tn(back, mid_all)) for back in gate_backs]
    up_parts = [low(dot_tn(back, mid_all)) for back in up_backs]

    def token_sum(product):
        both = mid_all.shape[0]
        pack = both // 2
        from_core = wide(swap(low(product(pack, both)), "grp", 1))
        if not in_pairs:
            return col_scatter(lambda i: product(0, pack) + from_core)
        half = pack // 2
        parts = blocks_of(from_core, 0, 2)
        return col_scatter(lambda i: product(i * half, (i + 1) * half) + parts[i])

    def over_hidden(a, b, *pairs):
        return sum(dot32(left[a:b], right) for lefts, rights in pairs for left, right in zip(lefts, rights))

    mid_grad = token_sum(
        lambda a, b: over_hidden(a, b, (gate_backs, gate_all), (up_backs, up_all))
    )
    layer_out = hidden_res + token_sum(lambda a, b: over_hidden(a, b, (acts, down_all)))

    res_from_mid, second_gain_part = second_back(mid_grad)
    res_grad = wide(cotangent) + res_from_mid
    shard_rows = jnp.concatenate(col_gather(low(res_grad)), axis=0)
    shard_rows, *parts = tie(shard_rows, *down_parts, *gate_parts, *up_parts)
    down_grad = sum_z_first(*parts[:2], core, ypos)
    gate_grad = sum_y_first(*parts[2:4], core, ypos)
    up_grad = sum_y_first(*parts[4:], core, ypos)
    out_wgrad = sum_quarters(low(dot_tn(attn_low, shard_rows)), core, ypos)
    out_wgrad = spread_core(spread_y(out_wgrad, ypos), core)
    mixed_low = low(dot_nt(shard_rows, output_weight))
    query_back, key_back, value_back = attention_call(
        attend_back_kernel,
        "attend_back",
        first,
        [
            (query_low, group_cols, 0),
            (key_low, head_dim, 0),
            (value_low, head_dim, 0),
            (mixed_low, group_cols, 0),
        ],
        tables,
        (group_cols, head_dim, head_dim),
        (jnp.bfloat16, jnp.bfloat16, jnp.float32, jnp.float32),
        head_dim,
        (7 * score_flops, key_heads),
    )
    pair_back = jnp.concatenate([key_back, value_back], axis=1)
    back_all = jnp.concatenate([query_back, pair_back], axis=1)
    query_part = sum_quarters(low(dot_tn(gathered_in, query_back)), core, ypos)
    pair_part = sum_quarters(low(dot_tn(gathered_in, pair_back)), core, ypos)
    back_parts = blocks_of(back_all, 0, 2) if in_pairs else [back_all]
    in_grad = col_scatter(lambda i: dot_nt(back_parts[i], project_in))
    res_from_in, _ = first_back(in_grad)
    input_grad = res_grad + res_from_in

    query_wgrad = wide(spread_core(spread_y(query_part, ypos), core))
    pair_part = spread_y(pair_part, ypos)
    if in_pairs:
        theirs = swap(pair_part, "col", 1)
        key_part = ordered(col, pair_part[:, :key_cols], theirs[:, :key_cols], 1)
        value_part = ordered(col, pair_part[:, key_cols:], theirs[:, key_cols:], 1)
        key_full = wide(spread_core(key_part, core))
        value_full = wide(spread_core(value_part, core))
    else:
        pair_part = spread_core(pair_part, core)
        pair_all = wide(lax.all_gather(pair_part, "col", axis=0))
        groups = lax.axis_size("col") // head_sharing

        def spread(piece):
            piece = jnp.sum(piece.reshape(groups, head_sharing, width, key_cols), axis=1)
            return jnp.swapaxes(piece, 0, 1).reshape(width, groups * key_cols)

        key_full = spread(pair_all[..., :key_cols])
        value_full = spread(pair_all[..., key_cols:])
    query_term = jnp.sum(query_wgrad * wide(query_weight), axis=1)
    pair_term = jnp.sum(key_full * wide(key_matrix) + value_full * wide(value_matrix), axis=1)
    query_term = butterfly(query_term.reshape(8, -1), ("col",)).reshape(-1)
    first_gain_grad = (query_term + pair_term) / first_gain
    axes = ("grp", "row", "col")
    second_gain_grad = butterfly(second_gain_part.reshape(8, -1), axes).reshape(-1)
    return (
        layer_out,
        input_grad,
        first_gain_grad,
        query_wgrad,
        key_full,
        value_full,
        wide(out_wgrad),
        second_gain_grad,
        wide(gate_grad).T,
        wide(up_grad).T,
        wide(down_grad),
    )


def solution(mesh):
    return jax.shard_map(
        per_device,
        mesh=mesh,
        in_specs=(
            P(("grp", "row", "col"), None),
            P(("grp", "row", "col"), None),
            P(("grp", "row")),
            P(("grp", "row")),
            P(),
            P(None, "col"),
            P(),
            P(),
            P("col", None),
            P(),
            P(None, ("row", "col")),
            P(None, ("row", "col")),
            P(("row", "col"), None),
        ),
        out_specs=(
            P(("grp", "row", "col"), None),
            P(("grp", "row", "col"), None),
            P(),
            P(None, "col"),
            P(),
            P(),
            P("col", None),
            P(),
            P(None, ("row", "col")),
            P(None, ("row", "col")),
            P(("row", "col"), None),
        ),
        check_vma=False,
    )
```

```python
import math

import jax
import jax.numpy as jnp
from jax import lax
from jax.experimental import pallas as pl
from jax.experimental.pallas import tpu as pltpu
from jax.sharding import PartitionSpec as P

QUERY_HEADS = 8
KEY_VALUE_HEADS = 4
HEAD_SIZE = 256


NORM_EPSILON = 1e-06
ROPE_BASE = 1000042.0
MASKED_SCORE = -1e30


def normalize(values, gain):
    inverse = lax.rsqrt(jnp.mean(values * values, axis=-1, keepdims=True) + NORM_EPSILON)
    return values * inverse * gain


def rope_tables(positions, head_dim):
    half_dim = head_dim // 2
    exponent = jnp.arange(half_dim, dtype=jnp.float32) * (2.0 / head_dim)
    inverse_freq = jnp.exp(-math.log(ROPE_BASE) * exponent)
    angles = positions.astype(jnp.float32)[:, None] * inverse_freq[None, :]
    return (jnp.cos(angles), jnp.sin(angles))


def turn(value, cosine, sine):
    half = value.shape[-1] // 2
    first, second = value[:, :half], value[:, half:]
    return jnp.concatenate(
        [first * cosine - second * sine, second * cosine + first * sine], axis=-1
    )


def kernel_dot(left, right, left_dim, right_dim):
    return lax.dot_general(
        left, right, (((left_dim,), (right_dim,)), ((), ())), preferred_element_type=jnp.float32
    )


def query_spans(length):
    step = length // 4
    return [(i * step, step, (i + 1) * step) for i in range(4)]


def allowed_keys(place, start, size, keys):
    pos_row, pos_col, seg_row, seg_col = place
    key_seg = seg_row[:, :keys]
    return (pos_row[:, :keys] <= pos_col[start : start + size, :]) & (
        (key_seg == 0) | (key_seg == seg_col[start : start + size, :])
    )


def stored_rows(first_ref, length):
    half = length // 2
    offsets = [first_ref[0] * half, (1 - first_ref[0]) * half]

    def rows(start, size):
        offset = pl.multiple_of(offsets[start // half] + start % half, size)
        return pl.ds(offset, size)

    return rows


def attend_kernel(
    first_ref, q_ref, k_ref, v_ref, cos_ref, sin_ref, pr_ref, pc_ref, sr_ref, sc_ref,
    out_ref, q_low_ref, k_low_ref, v_low_ref, key_ref, value_ref,
):
    length, head_dim = k_ref.shape
    rows = stored_rows(first_ref, length)
    place = (pr_ref, pc_ref, sr_ref, sc_ref)
    for start, size, _ in query_spans(length):
        span = slice(start, start + size)
        key = turn(k_ref[rows(start, size), :], cos_ref[span, :], sin_ref[span, :])
        key = key.astype(jnp.bfloat16)
        value = v_ref[rows(start, size), :].astype(jnp.bfloat16)
        key_ref[span, :] = key
        value_ref[span, :] = value
        k_low_ref[rows(start, size), :] = key
        v_low_ref[rows(start, size), :] = value
    for start, size, keys in query_spans(length):
        span = slice(start, start + size)
        allowed = allowed_keys(place, start, size, keys)
        for head in range(q_ref.shape[1] // head_dim):
            cols = slice(head * head_dim, (head + 1) * head_dim)
            query = turn(q_ref[rows(start, size), cols], cos_ref[span, :], sin_ref[span, :])
            query = query.astype(jnp.bfloat16)
            q_low_ref[rows(start, size), cols] = query
            scores = kernel_dot(query, key_ref[:keys, :], 1, 1) * head_dim**-0.5
            scores = jnp.where(allowed, scores, MASKED_SCORE)
            weights = jnp.exp(scores - jnp.max(scores, axis=1, keepdims=True))
            weights = weights * (1 / jnp.sum(weights, axis=1, keepdims=True))
            mixed = kernel_dot(weights.astype(jnp.bfloat16), value_ref[:keys, :], 1, 0)
            out_ref[rows(start, size), cols] = mixed.astype(jnp.bfloat16)


def attend_back_kernel(
    first_ref, q_ref, k_ref, v_ref, m_ref, cos_ref, sin_ref, pr_ref, pc_ref, sr_ref, sc_ref,
    q_back_ref, k_back_ref, v_back_ref, key_ref, value_ref, key_sum, value_sum,
):
    length, head_dim = k_ref.shape
    scale = head_dim**-0.5
    rows = stored_rows(first_ref, length)
    place = (pr_ref, pc_ref, sr_ref, sc_ref)
    for start, size, _ in query_spans(length):
        span = slice(start, start + size)
        key_ref[span, :] = k_ref[rows(start, size), :]
        value_ref[span, :] = v_ref[rows(start, size), :]
    key_sum[...] = jnp.zeros_like(key_sum)
    value_sum[...] = jnp.zeros_like(value_sum)
    for start, size, keys in query_spans(length):
        span = slice(start, start + size)
        allowed = allowed_keys(place, start, size, keys)
        for head in range(q_ref.shape[1] // head_dim):
            cols = slice(head * head_dim, (head + 1) * head_dim)
            query = q_ref[rows(start, size), cols]
            mixed = m_ref[rows(start, size), cols]
            scores = kernel_dot(query, key_ref[:keys, :], 1, 1) * scale
            scores = jnp.where(allowed, scores, MASKED_SCORE)
            probs = jnp.exp(scores - jnp.max(scores, axis=1, keepdims=True))
            probs = probs * (1 / jnp.sum(probs, axis=1, keepdims=True))
            value_sum[:keys, :] += kernel_dot(probs.astype(jnp.bfloat16), mixed, 0, 0)
            prob_grad = kernel_dot(mixed, value_ref[:keys, :], 1, 1)
            row_dot = jnp.sum(probs * prob_grad, axis=1, keepdims=True)
            score_low = (probs * (prob_grad - row_dot)).astype(jnp.bfloat16)
            key_sum[:keys, :] += kernel_dot(score_low, query, 0, 0)
            query_grad = kernel_dot(score_low, key_ref[:keys, :], 1, 0) * scale
            query_grad = turn(query_grad, cos_ref[span, :], -sin_ref[span, :])
            q_back_ref[rows(start, size), cols] = query_grad.astype(jnp.bfloat16)
    for start, size, _ in query_spans(length):
        span = slice(start, start + size)
        key_grad = turn(key_sum[span, :] * scale, cos_ref[span, :], -sin_ref[span, :])
        k_back_ref[rows(start, size), :] = key_grad.astype(jnp.bfloat16)
        v_back_ref[rows(start, size), :] = value_sum[span, :].astype(jnp.bfloat16)


def attention_call(kernel, name, first, heads, tables, outs, scratch, head_dim, flops):
    length = heads[0][0].shape[0]
    key_heads = flops[1]

    def head_spec(width, start):
        return pl.BlockSpec((length, width), lambda g, first_ref: (0, start + g))

    def whole_spec(shape):
        return pl.BlockSpec(shape, lambda g, first_ref: (0, 0))

    return pl.pallas_call(
        kernel,
        grid_spec=pltpu.PrefetchScalarGridSpec(
            num_scalar_prefetch=1,
            grid=(key_heads,),
            in_specs=[head_spec(width, start) for _, width, start in heads]
            + [whole_spec(table.shape) for table in tables],
            out_specs=[head_spec(width, 0) for width in outs],
            scratch_shapes=[pltpu.VMEM((length, head_dim), kind) for kind in scratch],
        ),
        out_shape=[
            jax.ShapeDtypeStruct((length, width * key_heads), jnp.bfloat16) for width in outs
        ],
        cost_estimate=pl.CostEstimate(
            flops=flops[0], bytes_accessed=flops[0] // 200, transcendentals=length * length
        ),
        name=name,
    )(first, *[array for array, _, _ in heads], *tables)


def swap(value, axis, bit):
    count = lax.axis_size(axis)
    return lax.ppermute(value, axis, [(i, i ^ bit) for i in range(count)])


def shift(value, axis, step):
    count = lax.axis_size(axis)
    return lax.ppermute(value, axis, [(i, (i + step) % count) for i in range(count)])


def tie(*values):
    return lax.optimization_barrier(values)


def ordered(first_when_zero, mine, theirs, dim):
    keep = first_when_zero == 0
    return jnp.concatenate(
        [jnp.where(keep, mine, theirs), jnp.where(keep, theirs, mine)], axis=dim
    )


def dot32(left, right):
    return jnp.dot(left, right, preferred_element_type=jnp.float32)


def dot_nt(left, right):
    return jnp.einsum("td,fd->tf", left, right, preferred_element_type=jnp.float32)


def dot_tn(left, right):
    return jnp.einsum("td,tf->df", left, right, preferred_element_type=jnp.float32)


def low(value):
    return value.astype(jnp.bfloat16)


def wide(value):
    return value.astype(jnp.float32)


def col_gather(mine):
    if lax.axis_size("col") == 2:
        return [mine, swap(mine, "col", 1)]
    return [lax.all_gather(mine, "col", axis=0, tiled=True)]


def col_scatter(product):
    if lax.axis_size("col") == 2:
        theirs = swap(low(product(1)), "col", 1)
        return product(0) + wide(theirs)
    return wide(lax.psum_scatter(low(product(0)), "col", scatter_dimension=0, tiled=True))


def blocks_of(value, dim, count):
    size = value.shape[dim] // count
    return [lax.slice_in_dim(value, i * size, (i + 1) * size, axis=dim) for i in range(count)]


def square_gather(for_x, for_y):
    if lax.axis_size("col") == 2:
        over_y = swap(for_y, "grp", 2)
        over_x = swap(for_x, "col", 1)
        half = for_x.shape[0] // 2
        across_first = swap(over_x[:half], "grp", 2)
        across_second = swap(over_y[half:], "col", 1)
        near = jnp.concatenate([for_x, over_x], axis=0)
        return near, jnp.concatenate([over_y, across_first, across_second], axis=0)
    near = lax.all_gather(for_x, "col", axis=0, tiled=True)
    return near, swap(near, "grp", 2)


def square_scatter(near, far):
    size = far.shape[0]
    if lax.axis_size("col") == 2:
        half, part = size // 2, size // 4
        across_first = swap(far[half : half + part], "grp", 2)
        across_second = swap(far[half + part :], "col", 1)
        rest = jnp.zeros_like(across_first)
        to_y = low(wide(far[:half]) + wide(jnp.concatenate([rest, across_second], axis=0)))
        to_x = low(near(half, size) + wide(jnp.concatenate([across_first, rest], axis=0)))
        from_y = swap(to_y, "grp", 2)
        from_x = swap(to_x, "col", 1)
        return near(0, half) + wide(from_x) + wide(from_y)
    total = low(near(0, size) + wide(swap(far, "grp", 2)))
    return wide(lax.psum_scatter(total, "col", scatter_dimension=0, tiled=True))


def butterfly(value, axes):
    for axis in axes:
        bit = 1
        while bit < lax.axis_size(axis):
            value = value + swap(value, axis, bit)
            bit *= 2
    return value


def half_rows(value, bit):
    size = value.shape[0] // 2
    return lax.dynamic_slice_in_dim(value, bit * size, size, 0)


def row_gather(value):
    return lax.all_gather(value, "row", axis=0, tiled=True)


def row_scatter(value):
    return lax.psum_scatter(value, "row", scatter_dimension=0, tiled=True)


def sum_quarters(value, core, ypos):
    part = low(wide(half_rows(value, core)) + wide(swap(half_rows(value, 1 - core), "grp", 1)))
    part = low(wide(half_rows(part, ypos)) + wide(swap(half_rows(part, 1 - ypos), "grp", 2)))
    return row_gather(row_scatter(part))


def spread_y(part, ypos):
    return ordered(ypos, part, swap(part, "grp", 2), 0)


def spread_core(part, core):
    return ordered(core, part, swap(part, "grp", 1), 0)


def own_quarter(weight, core, ypos):
    size = weight.shape[0] // 4
    return lax.dynamic_slice_in_dim(weight, (2 * core + ypos) * size, size, 0)


def spread_quarters(part, core, ypos, dim):
    half = ordered(ypos, part, swap(part, "grp", 2), dim)
    return wide(ordered(core, half, swap(half, "grp", 1), dim))


def per_device(
    tokens,
    cotangent,
    segments,
    positions,
    first_gain,
    query_weight,
    key_matrix,
    value_matrix,
    output_weight,
    second_gain,
    gate_weight,
    up_weight,
    down_weight,
):
    head_dim = HEAD_SIZE
    query_heads = query_weight.shape[1] // head_dim
    heads_per_group = QUERY_HEADS // KEY_VALUE_HEADS
    key_heads = max(1, query_heads // heads_per_group)
    head_share = query_heads // key_heads
    head_sharing = max(1, heads_per_group // query_heads)
    col = lax.axis_index("col")
    key_first = col * query_heads // heads_per_group
    query_cols = query_heads * head_dim
    key_cols = key_heads * head_dim
    rows, width = tokens.shape
    grp, zpos = lax.axis_index("grp"), lax.axis_index("row")
    core, ypos = lax.rem(grp, 2), lax.div(grp, 2)
    in_pairs = lax.axis_size("col") == 2

    inputs = wide(tokens)
    normalized_input, first_back = jax.vjp(normalize, inputs, first_gain)
    gathered_in = jnp.concatenate(col_gather(low(normalized_input)), axis=0)
    packed_length = gathered_in.shape[0]

    down_rows, gate_rows, up_rows = [
        row_gather(own_quarter(weight, core, ypos))
        for weight in (down_weight, gate_weight.T, up_weight.T)
    ]

    gathered_in, cot_now = tie(gathered_in, cotangent)
    cot_sets = [
        jnp.concatenate([pack, swap(pack, "grp", 1)], axis=0)
        for pack in square_gather(cot_now, cotangent)
    ]

    key_slice = lax.dynamic_slice_in_dim(key_matrix, key_first * head_dim, key_cols, 1)
    value_slice = lax.dynamic_slice_in_dim(value_matrix, key_first * head_dim, key_cols, 1)
    project_in = jnp.concatenate([query_weight, key_slice, value_slice], axis=1)
    projected = dot32(gathered_in, project_in)
    cosine, sine = rope_tables(positions, head_dim)
    tables = (cosine, sine, positions[None], positions[:, None], segments[None], segments[:, None])
    first = (col if in_pairs else jnp.zeros_like(col)).astype(jnp.int32).reshape(1)
    group_cols = head_share * head_dim
    score_flops = query_cols * packed_length * packed_length
    attn_low, query_low, key_low, value_low = attention_call(
        attend_kernel,
        "attend",
        first,
        [
            (projected, group_cols, 0),
            (projected, head_dim, query_heads),
            (projected, head_dim, query_heads + key_heads),
        ],
        tables,
        (group_cols, group_cols, head_dim, head_dim),
        (jnp.bfloat16, jnp.bfloat16),
        head_dim,
        (3 * score_flops, key_heads),
    )
    attn_low, down_rows = tie(attn_low, down_rows)
    act_grads = [low(dot_nt(cot, down_rows)) for cot in cot_sets]
    attn_parts = blocks_of(attn_low, 0, 2) if in_pairs else [attn_low]
    hidden_res = inputs + col_scatter(lambda i: dot32(attn_parts[i], output_weight))
    normed_mid, second_back = jax.vjp(normalize, hidden_res, second_gain)

    normed_low = low(normed_mid)
    mid_sets = [
        jnp.concatenate([pack, swap(pack, "grp", 1)], axis=0)
        for pack in square_gather(normed_low, normed_low)
    ]
    acts, gate_backs, up_backs = [], [], []
    for mid, act_grad in zip(mid_sets, act_grads):
        gate32 = wide(low(dot_nt(mid, gate_rows)))
        up_lin = dot_nt(mid, up_rows)
        sig = jax.nn.sigmoid(gate32)
        acts.append(low(gate32 * sig * up_lin))
        gate_backs.append(low(wide(act_grad) * up_lin * sig * (1 + gate32 * (1 - sig))))
        up_backs.append(low(wide(act_grad) * gate32 * sig))

    def token_sum(product):
        pack = packed_length
        far = low(
            product(1, 0, pack) + wide(swap(low(product(1, pack, 2 * pack)), "grp", 1))
        )
        from_core = wide(swap(low(product(0, pack, 2 * pack)), "grp", 1))
        return square_scatter(
            lambda first, last: product(0, first, last) + from_core[first:last], far
        )

    mid_grad = token_sum(
        lambda i, a, b: dot32(gate_backs[i][a:b], gate_rows) + dot32(up_backs[i][a:b], up_rows)
    )

    def weight_part(lefts, rights):
        return row_scatter(low(sum(dot_tn(left, right) for left, right in zip(lefts, rights))))

    down_part = weight_part(acts, cot_sets)
    gate_part = weight_part(gate_backs, mid_sets)
    up_part = weight_part(up_backs, mid_sets)
    layer_out = hidden_res + token_sum(lambda i, a, b: dot32(acts[i][a:b], down_rows))

    res_from_mid, second_gain_part = second_back(mid_grad)
    res_grad = wide(cotangent) + res_from_mid
    shard_rows = jnp.concatenate(col_gather(low(res_grad)), axis=0)
    shard_rows, down_part = tie(shard_rows, down_part)
    out_part = sum_quarters(low(dot_tn(attn_low, shard_rows)), core, ypos)
    mixed_low = low(dot_nt(shard_rows, output_weight))
    query_back, key_back, value_back = attention_call(
        attend_back_kernel,
        "attend_back",
        first,
        [
            (query_low, group_cols, 0),
            (key_low, head_dim, 0),
            (value_low, head_dim, 0),
            (mixed_low, group_cols, 0),
        ],
        tables,
        (group_cols, head_dim, head_dim),
        (jnp.bfloat16, jnp.bfloat16, jnp.float32, jnp.float32),
        head_dim,
        (7 * score_flops, key_heads),
    )
    pair_back = jnp.concatenate([key_back, value_back], axis=1)
    back_all = jnp.concatenate([query_back, pair_back], axis=1)
    query_part = sum_quarters(low(dot_tn(gathered_in, query_back)), core, ypos)
    pair_part = sum_quarters(low(dot_tn(gathered_in, pair_back)), core, ypos)
    back_parts = blocks_of(back_all, 0, 2) if in_pairs else [back_all]
    in_grad = col_scatter(lambda i: dot_nt(back_parts[i], project_in))
    in_grad, gate_part = tie(in_grad, gate_part)
    res_from_in, _ = first_back(in_grad)
    input_grad = res_grad + res_from_in

    down_grad = spread_quarters(down_part, core, ypos, 0)
    gate_grad = spread_quarters(gate_part.T, core, ypos, 1)
    up_grad = spread_quarters(up_part.T, core, ypos, 1)
    out_wgrad = spread_quarters(out_part, core, ypos, 0)
    query_wgrad = spread_quarters(query_part, core, ypos, 0)
    pair_part = ordered(ypos, pair_part, swap(pair_part, "grp", 2), 0)
    if in_pairs:
        theirs = swap(pair_part, "col", 1)
        key_part = ordered(col, pair_part[:, :key_cols], theirs[:, :key_cols], 1)
        value_part = ordered(col, pair_part[:, key_cols:], theirs[:, key_cols:], 1)
        key_full = wide(ordered(core, key_part, swap(key_part, "grp", 1), 0))
        value_full = wide(ordered(core, value_part, swap(value_part, "grp", 1), 0))
    else:
        pair_part = ordered(core, pair_part, swap(pair_part, "grp", 1), 0)
        pair_all = wide(lax.all_gather(pair_part, "col", axis=0))
        groups = lax.axis_size("col") // head_sharing

        def spread(piece):
            piece = jnp.sum(piece.reshape(groups, head_sharing, width, key_cols), axis=1)
            return jnp.swapaxes(piece, 0, 1).reshape(width, groups * key_cols)

        key_full = spread(pair_all[..., :key_cols])
        value_full = spread(pair_all[..., key_cols:])
    query_term = jnp.sum(query_wgrad * wide(query_weight), axis=1)
    pair_term = jnp.sum(key_full * wide(key_matrix) + value_full * wide(value_matrix), axis=1)
    query_term = butterfly(query_term.reshape(8, -1), ("col",)).reshape(-1)
    first_gain_grad = (query_term + pair_term) / first_gain
    axes = ("grp", "row", "col")
    second_gain_grad = butterfly(second_gain_part.reshape(8, -1), axes).reshape(-1)
    return (
        layer_out,
        input_grad,
        first_gain_grad,
        query_wgrad,
        key_full,
        value_full,
        out_wgrad,
        second_gain_grad,
        gate_grad,
        up_grad,
        down_grad,
    )


def solution(mesh):
    return jax.shard_map(
        per_device,
        mesh=mesh,
        in_specs=(
            P(("grp", "row", "col"), None),
            P(("grp", "row", "col"), None),
            P(("grp", "row")),
            P(("grp", "row")),
            P(),
            P(None, "col"),
            P(),
            P(),
            P("col", None),
            P(),
            P(None, ("row", "col")),
            P(None, ("row", "col")),
            P(("row", "col"), None),
        ),
        out_specs=(
            P(("grp", "row", "col"), None),
            P(("grp", "row", "col"), None),
            P(),
            P(None, "col"),
            P(),
            P(),
            P("col", None),
            P(),
            P(None, ("row", "col")),
            P(None, ("row", "col")),
            P(("row", "col"), None),
        ),
        check_vma=False,
    )
```

```python
import math

import jax
import jax.numpy as jnp
from jax import lax
from jax.experimental import pallas as pl
from jax.experimental.pallas import tpu as pltpu
from jax.sharding import PartitionSpec as P

QUERY_HEADS = 8
KEY_VALUE_HEADS = 4
HEAD_SIZE = 256


NORM_EPSILON = 1e-06
ROPE_BASE = 1000042.0
MASKED_SCORE = -1e30


def normalize(values, gain):
    inverse = lax.rsqrt(jnp.mean(values * values, axis=-1, keepdims=True) + NORM_EPSILON)
    return values * inverse * gain


def rope_tables(positions, head_dim):
    half_dim = head_dim // 2
    exponent = jnp.arange(half_dim, dtype=jnp.float32) * (2.0 / head_dim)
    inverse_freq = jnp.exp(-math.log(ROPE_BASE) * exponent)
    angles = positions.astype(jnp.float32)[:, None] * inverse_freq[None, :]
    return (jnp.cos(angles), jnp.sin(angles))


def turn(value, cosine, sine):
    half = value.shape[-1] // 2
    first, second = value[:, :half], value[:, half:]
    return jnp.concatenate(
        [first * cosine - second * sine, second * cosine + first * sine], axis=-1
    )


def kernel_dot(left, right, left_dim, right_dim):
    return lax.dot_general(
        left, right, (((left_dim,), (right_dim,)), ((), ())), preferred_element_type=jnp.float32
    )


def query_spans(length):
    step = length // 4
    return [(i * step, step, (i + 1) * step) for i in range(4)]


def allowed_keys(place, start, size, keys):
    pos_row, pos_col, seg_row, seg_col = place
    key_seg = seg_row[:, :keys]
    return (pos_row[:, :keys] <= pos_col[start : start + size, :]) & (
        (key_seg == 0) | (key_seg == seg_col[start : start + size, :])
    )


def stored_rows(first_ref, length):
    half = length // 2
    offsets = [first_ref[0] * half, (1 - first_ref[0]) * half]

    def rows(start, size):
        offset = pl.multiple_of(offsets[start // half] + start % half, size)
        return pl.ds(offset, size)

    return rows


def attend_kernel(
    first_ref, q_ref, k_ref, v_ref, cos_ref, sin_ref, pr_ref, pc_ref, sr_ref, sc_ref,
    out_ref, q_low_ref, k_low_ref, v_low_ref, key_ref, value_ref,
):
    length, head_dim = k_ref.shape
    rows = stored_rows(first_ref, length)
    place = (pr_ref, pc_ref, sr_ref, sc_ref)
    for start, size, _ in query_spans(length):
        span = slice(start, start + size)
        key = turn(k_ref[rows(start, size), :], cos_ref[span, :], sin_ref[span, :])
        key = key.astype(jnp.bfloat16)
        value = v_ref[rows(start, size), :].astype(jnp.bfloat16)
        key_ref[span, :] = key
        value_ref[span, :] = value
        k_low_ref[rows(start, size), :] = key
        v_low_ref[rows(start, size), :] = value
    for start, size, keys in query_spans(length):
        span = slice(start, start + size)
        allowed = allowed_keys(place, start, size, keys)
        for head in range(q_ref.shape[1] // head_dim):
            cols = slice(head * head_dim, (head + 1) * head_dim)
            query = turn(q_ref[rows(start, size), cols], cos_ref[span, :], sin_ref[span, :])
            query = query.astype(jnp.bfloat16)
            q_low_ref[rows(start, size), cols] = query
            scores = kernel_dot(query, key_ref[:keys, :], 1, 1) * head_dim**-0.5
            scores = jnp.where(allowed, scores, MASKED_SCORE)
            weights = jnp.exp(scores - jnp.max(scores, axis=1, keepdims=True))
            weights = weights * (1 / jnp.sum(weights, axis=1, keepdims=True))
            mixed = kernel_dot(weights.astype(jnp.bfloat16), value_ref[:keys, :], 1, 0)
            out_ref[rows(start, size), cols] = mixed.astype(jnp.bfloat16)


def attend_back_kernel(
    first_ref, q_ref, k_ref, v_ref, m_ref, cos_ref, sin_ref, pr_ref, pc_ref, sr_ref, sc_ref,
    q_back_ref, k_back_ref, v_back_ref, key_ref, value_ref, key_sum, value_sum,
):
    length, head_dim = k_ref.shape
    scale = head_dim**-0.5
    rows = stored_rows(first_ref, length)
    place = (pr_ref, pc_ref, sr_ref, sc_ref)
    for start, size, _ in query_spans(length):
        span = slice(start, start + size)
        key_ref[span, :] = k_ref[rows(start, size), :]
        value_ref[span, :] = v_ref[rows(start, size), :]
    key_sum[...] = jnp.zeros_like(key_sum)
    value_sum[...] = jnp.zeros_like(value_sum)
    for start, size, keys in query_spans(length):
        span = slice(start, start + size)
        allowed = allowed_keys(place, start, size, keys)
        for head in range(q_ref.shape[1] // head_dim):
            cols = slice(head * head_dim, (head + 1) * head_dim)
            query = q_ref[rows(start, size), cols]
            mixed = m_ref[rows(start, size), cols]
            scores = kernel_dot(query, key_ref[:keys, :], 1, 1) * scale
            scores = jnp.where(allowed, scores, MASKED_SCORE)
            probs = jnp.exp(scores - jnp.max(scores, axis=1, keepdims=True))
            probs = probs * (1 / jnp.sum(probs, axis=1, keepdims=True))
            value_sum[:keys, :] += kernel_dot(probs.astype(jnp.bfloat16), mixed, 0, 0)
            prob_grad = kernel_dot(mixed, value_ref[:keys, :], 1, 1)
            row_dot = jnp.sum(probs * prob_grad, axis=1, keepdims=True)
            score_low = (probs * (prob_grad - row_dot)).astype(jnp.bfloat16)
            key_sum[:keys, :] += kernel_dot(score_low, query, 0, 0)
            query_grad = kernel_dot(score_low, key_ref[:keys, :], 1, 0) * scale
            query_grad = turn(query_grad, cos_ref[span, :], -sin_ref[span, :])
            q_back_ref[rows(start, size), cols] = query_grad.astype(jnp.bfloat16)
    for start, size, _ in query_spans(length):
        span = slice(start, start + size)
        key_grad = turn(key_sum[span, :] * scale, cos_ref[span, :], -sin_ref[span, :])
        k_back_ref[rows(start, size), :] = key_grad.astype(jnp.bfloat16)
        v_back_ref[rows(start, size), :] = value_sum[span, :].astype(jnp.bfloat16)


def attention_call(kernel, name, first, heads, tables, outs, scratch, head_dim, flops):
    length = heads[0][0].shape[0]
    key_heads = flops[1]

    def head_spec(width, start):
        return pl.BlockSpec((length, width), lambda g, first_ref: (0, start + g))

    def whole_spec(shape):
        return pl.BlockSpec(shape, lambda g, first_ref: (0, 0))

    return pl.pallas_call(
        kernel,
        grid_spec=pltpu.PrefetchScalarGridSpec(
            num_scalar_prefetch=1,
            grid=(key_heads,),
            in_specs=[head_spec(width, start) for _, width, start in heads]
            + [whole_spec(table.shape) for table in tables],
            out_specs=[head_spec(width, 0) for width in outs],
            scratch_shapes=[pltpu.VMEM((length, head_dim), kind) for kind in scratch],
        ),
        out_shape=[
            jax.ShapeDtypeStruct((length, width * key_heads), jnp.bfloat16) for width in outs
        ],
        cost_estimate=pl.CostEstimate(
            flops=flops[0], bytes_accessed=flops[0] // 200, transcendentals=length * length
        ),
        name=name,
    )(first, *[array for array, _, _ in heads], *tables)


def swap(value, axis, bit):
    count = lax.axis_size(axis)
    return lax.ppermute(value, axis, [(i, i ^ bit) for i in range(count)])


def shift(value, axis, step):
    count = lax.axis_size(axis)
    return lax.ppermute(value, axis, [(i, (i + step) % count) for i in range(count)])


def tie(*values):
    return lax.optimization_barrier(values)


def ordered(first_when_zero, mine, theirs, dim):
    keep = first_when_zero == 0
    return jnp.concatenate(
        [jnp.where(keep, mine, theirs), jnp.where(keep, theirs, mine)], axis=dim
    )


def dot32(left, right):
    return jnp.dot(left, right, preferred_element_type=jnp.float32)


def dot_nt(left, right):
    return jnp.einsum("td,fd->tf", left, right, preferred_element_type=jnp.float32)


def dot_tn(left, right):
    return jnp.einsum("td,tf->df", left, right, preferred_element_type=jnp.float32)


def low(value):
    return value.astype(jnp.bfloat16)


def wide(value):
    return value.astype(jnp.float32)


def col_gather(mine):
    if lax.axis_size("col") == 2:
        return [mine, swap(mine, "col", 1)]
    return [lax.all_gather(mine, "col", axis=0, tiled=True)]


def col_scatter(product, beside=None):
    if lax.axis_size("col") == 2:
        theirs = swap(low(product(1)), "col", 1)
        if beside is not None:
            theirs, beside = tie(theirs, beside)
            return product(0) + wide(theirs), beside
        return product(0) + wide(theirs)
    if beside is not None:
        return col_scatter(product), beside
    return wide(lax.psum_scatter(low(product(0)), "col", scatter_dimension=0, tiled=True))


def blocks_of(value, dim, count):
    size = value.shape[dim] // count
    return [lax.slice_in_dim(value, i * size, (i + 1) * size, axis=dim) for i in range(count)]


def square_gather(mine):
    if lax.axis_size("col") == 2:
        over_x = swap(mine, "col", 1)
        over_y = swap(mine, "grp", 2)
        half = mine.shape[0] // 2
        across_first = swap(over_x[:half], "grp", 2)
        across_second = swap(over_y[half:], "col", 1)
        near = jnp.concatenate([mine, over_x], axis=0)
        return near, jnp.concatenate([over_y, across_first, across_second], axis=0)
    near = lax.all_gather(mine, "col", axis=0, tiled=True)
    return near, swap(near, "grp", 2)


def with_core(pack):
    return jnp.concatenate([pack, swap(pack, "grp", 1)], axis=0)


def square_scatter(near, far):
    size = far.shape[0]
    if lax.axis_size("col") == 2:
        half, part = size // 2, size // 4
        across_first = swap(far[half : half + part], "grp", 2)
        across_second = swap(far[half + part :], "col", 1)
        rest = jnp.zeros_like(across_first)
        to_y = low(wide(far[:half]) + wide(jnp.concatenate([rest, across_second], axis=0)))
        to_x = low(near(half, size) + wide(jnp.concatenate([across_first, rest], axis=0)))
        from_y = swap(to_y, "grp", 2)
        from_x = swap(to_x, "col", 1)
        return near(0, half) + wide(from_x) + wide(from_y)
    total = low(near(0, size) + wide(swap(far, "grp", 2)))
    return wide(lax.psum_scatter(total, "col", scatter_dimension=0, tiled=True))


def butterfly(value, axes):
    for axis in axes:
        bit = 1
        while bit < lax.axis_size(axis):
            value = value + swap(value, axis, bit)
            bit *= 2
    return value


def half_rows(value, bit):
    size = value.shape[0] // 2
    return lax.dynamic_slice_in_dim(value, bit * size, size, 0)


def row_gather(value):
    return lax.all_gather(value, "row", axis=0, tiled=True)


def row_scatter(value):
    return lax.psum_scatter(value, "row", scatter_dimension=0, tiled=True)


def sum_quarters(value, core, ypos):
    return sum_y(sum_cores(value, core), ypos)


def sum_cores(value, core):
    return low(wide(half_rows(value, core)) + wide(swap(half_rows(value, 1 - core), "grp", 1)))


def sum_y(part, ypos):
    part = low(wide(half_rows(part, ypos)) + wide(swap(half_rows(part, 1 - ypos), "grp", 2)))
    return part


def spread_y(part, ypos):
    return ordered(ypos, part, swap(part, "grp", 2), 0)


def spread_core(part, core):
    return ordered(core, part, swap(part, "grp", 1), 0)


def own_quarter(weight, core, ypos):
    size = weight.shape[0] // 4
    return lax.dynamic_slice_in_dim(weight, (2 * core + ypos) * size, size, 0)


def spread_quarters(part, core, ypos, dim):
    half = ordered(ypos, part, swap(part, "grp", 2), dim)
    return wide(ordered(core, half, swap(half, "grp", 1), dim))


def per_device(
    tokens,
    cotangent,
    segments,
    positions,
    first_gain,
    query_weight,
    key_matrix,
    value_matrix,
    output_weight,
    second_gain,
    gate_weight,
    up_weight,
    down_weight,
):
    head_dim = HEAD_SIZE
    query_heads = query_weight.shape[1] // head_dim
    heads_per_group = QUERY_HEADS // KEY_VALUE_HEADS
    key_heads = max(1, query_heads // heads_per_group)
    head_share = query_heads // key_heads
    head_sharing = max(1, heads_per_group // query_heads)
    col = lax.axis_index("col")
    key_first = col * query_heads // heads_per_group
    query_cols = query_heads * head_dim
    key_cols = key_heads * head_dim
    rows, width = tokens.shape
    grp, zpos = lax.axis_index("grp"), lax.axis_index("row")
    core, ypos = lax.rem(grp, 2), lax.div(grp, 2)
    in_pairs = lax.axis_size("col") == 2

    inputs = wide(tokens)
    normalized_input, first_back = jax.vjp(normalize, inputs, first_gain)
    gathered_in = jnp.concatenate(col_gather(low(normalized_input)), axis=0)
    packed_length = gathered_in.shape[0]

    down_own, gate_own, up_own = [
        own_quarter(weight, core, ypos) for weight in (down_weight, gate_weight.T, up_weight.T)
    ]
    down_rows = row_gather(down_own)
    gate_up = lax.all_gather(jnp.stack([gate_own, up_own]), "row", axis=0)

    gathered_in, cot_now = tie(gathered_in, cotangent)
    cot_near = col_gather(cot_now)
    if in_pairs:
        cot_far = [swap(cotangent, "grp", 2), swap(cot_near[1], "grp", 2)]
    else:
        cot_far = [swap(cot_near[0], "grp", 2)]
    cot_sets = [with_core(jnp.concatenate(pack, axis=0)) for pack in (cot_near, cot_far)]

    key_slice = lax.dynamic_slice_in_dim(key_matrix, key_first * head_dim, key_cols, 1)
    value_slice = lax.dynamic_slice_in_dim(value_matrix, key_first * head_dim, key_cols, 1)
    project_in = jnp.concatenate([query_weight, key_slice, value_slice], axis=1)
    projected = dot32(gathered_in, project_in)
    cosine, sine = rope_tables(positions, head_dim)
    tables = (cosine, sine, positions[None], positions[:, None], segments[None], segments[:, None])
    first = (col if in_pairs else jnp.zeros_like(col)).astype(jnp.int32).reshape(1)
    group_cols = head_share * head_dim
    score_flops = query_cols * packed_length * packed_length
    attn_low, query_low, key_low, value_low = attention_call(
        attend_kernel,
        "attend",
        first,
        [
            (projected, group_cols, 0),
            (projected, head_dim, query_heads),
            (projected, head_dim, query_heads + key_heads),
        ],
        tables,
        (group_cols, group_cols, head_dim, head_dim),
        (jnp.bfloat16, jnp.bfloat16),
        head_dim,
        (3 * score_flops, key_heads),
    )
    attn_low, down_rows = tie(attn_low, down_rows)
    act_near = low(dot_nt(cot_sets[0], down_rows))
    act_far = low(dot_nt(cot_sets[1], down_rows))
    attn_parts = blocks_of(attn_low, 0, 2) if in_pairs else [attn_low]
    from_attention, act_near = col_scatter(
        lambda i: dot32(attn_parts[i], output_weight), act_near
    )
    hidden_res = inputs + from_attention
    normed_mid, second_back = jax.vjp(normalize, hidden_res, second_gain)

    mid_near, mid_far = square_gather(low(normed_mid))
    mid_near, act_far = tie(mid_near, act_far)
    mid_sets = [with_core(mid_near), with_core(mid_far)]
    act_grads = [act_near, act_far]
    gate_rows, up_rows = [gate_up[:, i].reshape(-1, width) for i in range(2)]
    acts, gate_backs, up_backs = [], [], []
    for mid, act_grad in zip(mid_sets, act_grads):
        gate32 = wide(low(dot_nt(mid, gate_rows)))
        up_lin = dot_nt(mid, up_rows)
        sig = jax.nn.sigmoid(gate32)
        acts.append(low(gate32 * sig * up_lin))
        gate_backs.append(low(wide(act_grad) * up_lin * sig * (1 + gate32 * (1 - sig))))
        up_backs.append(low(wide(act_grad) * gate32 * sig))

    def weight_sum(lefts, rights):
        return low(sum(dot_tn(left, right) for left, right in zip(lefts, rights)))

    def far_sum(product):
        pack = packed_length
        theirs = swap(low(product(1, pack, 2 * pack)), "grp", 1)
        return low(product(1, 0, pack) + wide(theirs))

    def near_sum(product):
        pack = packed_length
        return wide(swap(low(product(0, pack, 2 * pack)), "grp", 1))

    def mid_product(i, a, b):
        return dot32(gate_backs[i][a:b], gate_rows) + dot32(up_backs[i][a:b], up_rows)

    def out_product(i, a, b):
        return dot32(acts[i][a:b], down_rows)

    down_low = weight_sum(acts, cot_sets)
    down_low, gate_backs[1], up_backs[1] = tie(down_low, gate_backs[1], up_backs[1])
    down_part = row_scatter(down_low)
    mid_far_sum = far_sum(mid_product)
    mid_from_core = near_sum(mid_product)
    mid_grad = square_scatter(
        lambda first, last: mid_product(0, first, last) + mid_from_core[first:last], mid_far_sum
    )
    gate_low = weight_sum(gate_backs, mid_sets)
    up_low = weight_sum(up_backs, mid_sets)

    res_from_mid, second_gain_part = second_back(mid_grad)
    res_grad = wide(cotangent) + res_from_mid
    gate_part = row_scatter(gate_low)
    up_part = row_scatter(up_low)
    res_low, down_part = tie(low(res_grad), down_part)
    shard_rows = jnp.concatenate(col_gather(res_low), axis=0)

    out_far = far_sum(out_product)
    shard_rows, gate_part, out_far = tie(shard_rows, gate_part, out_far)
    out_from_core = near_sum(out_product) + wide(swap(out_far, "grp", 2))
    half_pack = packed_length // 2
    if in_pairs:
        layer_rows = col_scatter(
            lambda i: out_product(0, i * half_pack, (i + 1) * half_pack)
            + out_from_core[i * half_pack : (i + 1) * half_pack]
        )
    else:
        layer_rows = col_scatter(lambda i: out_product(0, 0, packed_length) + out_from_core)
    layer_out = hidden_res + layer_rows

    mixed_low = low(dot_nt(shard_rows, output_weight))
    out_low = low(dot_tn(attn_low, shard_rows))
    mixed_low, out_low = tie(mixed_low, sum_cores(out_low, core))
    out_part, up_part = tie(sum_y(out_low, ypos), up_part)
    out_part = row_gather(row_scatter(out_part))
    query_back, key_back, value_back = attention_call(
        attend_back_kernel,
        "attend_back",
        first,
        [
            (query_low, group_cols, 0),
            (key_low, head_dim, 0),
            (value_low, head_dim, 0),
            (mixed_low, group_cols, 0),
        ],
        tables,
        (group_cols, head_dim, head_dim),
        (jnp.bfloat16, jnp.bfloat16, jnp.float32, jnp.float32),
        head_dim,
        (7 * score_flops, key_heads),
    )
    pair_back = jnp.concatenate([key_back, value_back], axis=1)
    back_all = jnp.concatenate([query_back, pair_back], axis=1)
    query_part = sum_quarters(low(dot_tn(gathered_in, query_back)), core, ypos)
    pair_part = sum_quarters(low(dot_tn(gathered_in, pair_back)), core, ypos)
    query_part, pair_part, down_part, gate_part = tie(query_part, pair_part, down_part, gate_part)
    query_part = row_gather(row_scatter(query_part))
    pair_part = row_gather(row_scatter(pair_part))
    back_parts = blocks_of(back_all, 0, 2) if in_pairs else [back_all]
    in_grad = col_scatter(lambda i: dot_nt(back_parts[i], project_in))
    res_from_in, _ = first_back(in_grad)
    input_grad = res_grad + res_from_in

    down_grad = spread_quarters(down_part, core, ypos, 0)
    gate_grad = spread_quarters(gate_part.T, core, ypos, 1)
    up_grad = spread_quarters(up_part.T, core, ypos, 1)
    out_wgrad = spread_quarters(out_part, core, ypos, 0)
    query_wgrad = spread_quarters(query_part, core, ypos, 0)
    if in_pairs:
        over_x, over_y = swap(pair_part, "col", 1), swap(pair_part, "grp", 2)
        half = pair_part.shape[0] // 2
        across = jnp.concatenate(
            [swap(over_x[:half], "grp", 2), swap(over_y[half:], "col", 1)], axis=0
        )
        pair_part = ordered(ypos, pair_part, over_y, 0)
        theirs = ordered(ypos, over_x, across, 0)
        key_part = ordered(col, pair_part[:, :key_cols], theirs[:, :key_cols], 1)
        value_part = ordered(col, pair_part[:, key_cols:], theirs[:, key_cols:], 1)
        key_full = wide(ordered(core, key_part, swap(key_part, "grp", 1), 0))
        value_full = wide(ordered(core, value_part, swap(value_part, "grp", 1), 0))
    else:
        pair_part = ordered(ypos, pair_part, swap(pair_part, "grp", 2), 0)
        pair_part = ordered(core, pair_part, swap(pair_part, "grp", 1), 0)
        pair_all = wide(lax.all_gather(pair_part, "col", axis=0))
        groups = lax.axis_size("col") // head_sharing

        def spread(piece):
            piece = jnp.sum(piece.reshape(groups, head_sharing, width, key_cols), axis=1)
            return jnp.swapaxes(piece, 0, 1).reshape(width, groups * key_cols)

        key_full = spread(pair_all[..., :key_cols])
        value_full = spread(pair_all[..., key_cols:])
    query_term = jnp.sum(query_wgrad * wide(query_weight), axis=1)
    pair_term = jnp.sum(key_full * wide(key_matrix) + value_full * wide(value_matrix), axis=1)
    query_term = butterfly(query_term.reshape(8, -1), ("col",)).reshape(-1)
    first_gain_grad = (query_term + pair_term) / first_gain
    axes = ("grp", "row", "col")
    second_gain_grad = butterfly(second_gain_part.reshape(8, -1), axes).reshape(-1)
    return (
        layer_out,
        input_grad,
        first_gain_grad,
        query_wgrad,
        key_full,
        value_full,
        out_wgrad,
        second_gain_grad,
        gate_grad,
        up_grad,
        down_grad,
    )


def solution(mesh):
    return jax.shard_map(
        per_device,
        mesh=mesh,
        in_specs=(
            P(("grp", "row", "col"), None),
            P(("grp", "row", "col"), None),
            P(("grp", "row")),
            P(("grp", "row")),
            P(),
            P(None, "col"),
            P(),
            P(),
            P("col", None),
            P(),
            P(None, ("row", "col")),
            P(None, ("row", "col")),
            P(("row", "col"), None),
        ),
        out_specs=(
            P(("grp", "row", "col"), None),
            P(("grp", "row", "col"), None),
            P(),
            P(None, "col"),
            P(),
            P(),
            P("col", None),
            P(),
            P(None, ("row", "col")),
            P(None, ("row", "col")),
            P(("row", "col"), None),
        ),
        check_vma=False,
    )
```

```python
import math

import jax
import jax.numpy as jnp
from jax import lax
from jax.experimental import pallas as pl
from jax.experimental.pallas import tpu as pltpu
from jax.sharding import PartitionSpec as P

QUERY_HEADS = 8
KEY_VALUE_HEADS = 4
HEAD_SIZE = 256


NORM_EPSILON = 1e-06
ROPE_BASE = 1000042.0
MASKED_SCORE = -1e30


def normalize(values, gain):
    inverse = lax.rsqrt(jnp.mean(values * values, axis=-1, keepdims=True) + NORM_EPSILON)
    return values * inverse * gain


def rope_tables(positions, head_dim):
    half_dim = head_dim // 2
    exponent = jnp.arange(half_dim, dtype=jnp.float32) * (2.0 / head_dim)
    inverse_freq = jnp.exp(-math.log(ROPE_BASE) * exponent)
    angles = positions.astype(jnp.float32)[:, None] * inverse_freq[None, :]
    return (jnp.cos(angles), jnp.sin(angles))


def turn(value, cosine, sine):
    half = value.shape[-1] // 2
    first, second = value[:, :half], value[:, half:]
    return jnp.concatenate(
        [first * cosine - second * sine, second * cosine + first * sine], axis=-1
    )


def kernel_dot(left, right, left_dim, right_dim):
    return lax.dot_general(
        left, right, (((left_dim,), (right_dim,)), ((), ())), preferred_element_type=jnp.float32
    )


def query_spans(length):
    step = length // 4
    return [(i * step, step, (i + 1) * step) for i in range(4)]


def allowed_keys(place, start, size, keys):
    pos_row, pos_col, seg_row, seg_col = place
    key_seg = seg_row[:, :keys]
    return (pos_row[:, :keys] <= pos_col[start : start + size, :]) & (
        (key_seg == 0) | (key_seg == seg_col[start : start + size, :])
    )


def stored_rows(first_ref, length):
    half = length // 2
    offsets = [first_ref[0] * half, (1 - first_ref[0]) * half]

    def rows(start, size):
        offset = pl.multiple_of(offsets[start // half] + start % half, size)
        return pl.ds(offset, size)

    return rows


def attend_kernel(
    first_ref, q_ref, k_ref, v_ref, cos_ref, sin_ref, pr_ref, pc_ref, sr_ref, sc_ref,
    out_ref, q_low_ref, k_low_ref, v_low_ref, key_ref, value_ref,
):
    length, head_dim = k_ref.shape
    rows = stored_rows(first_ref, length)
    place = (pr_ref, pc_ref, sr_ref, sc_ref)
    for start, size, _ in query_spans(length):
        span = slice(start, start + size)
        key = turn(k_ref[rows(start, size), :], cos_ref[span, :], sin_ref[span, :])
        key = key.astype(jnp.bfloat16)
        value = v_ref[rows(start, size), :].astype(jnp.bfloat16)
        key_ref[span, :] = key
        value_ref[span, :] = value
        k_low_ref[rows(start, size), :] = key
        v_low_ref[rows(start, size), :] = value
    for start, size, keys in query_spans(length):
        span = slice(start, start + size)
        allowed = allowed_keys(place, start, size, keys)
        for head in range(q_ref.shape[1] // head_dim):
            cols = slice(head * head_dim, (head + 1) * head_dim)
            query = turn(q_ref[rows(start, size), cols], cos_ref[span, :], sin_ref[span, :])
            query = query.astype(jnp.bfloat16)
            q_low_ref[rows(start, size), cols] = query
            scores = kernel_dot(query, key_ref[:keys, :], 1, 1) * head_dim**-0.5
            scores = jnp.where(allowed, scores, MASKED_SCORE)
            weights = jnp.exp(scores - jnp.max(scores, axis=1, keepdims=True))
            weights = weights * (1 / jnp.sum(weights, axis=1, keepdims=True))
            mixed = kernel_dot(weights.astype(jnp.bfloat16), value_ref[:keys, :], 1, 0)
            out_ref[rows(start, size), cols] = mixed.astype(jnp.bfloat16)


def attend_back_kernel(
    first_ref, q_ref, k_ref, v_ref, m_ref, cos_ref, sin_ref, pr_ref, pc_ref, sr_ref, sc_ref,
    q_back_ref, k_back_ref, v_back_ref, key_ref, value_ref, key_sum, value_sum,
):
    length, head_dim = k_ref.shape
    scale = head_dim**-0.5
    rows = stored_rows(first_ref, length)
    place = (pr_ref, pc_ref, sr_ref, sc_ref)
    for start, size, _ in query_spans(length):
        span = slice(start, start + size)
        key_ref[span, :] = k_ref[rows(start, size), :]
        value_ref[span, :] = v_ref[rows(start, size), :]
    key_sum[...] = jnp.zeros_like(key_sum)
    value_sum[...] = jnp.zeros_like(value_sum)
    for start, size, keys in query_spans(length):
        span = slice(start, start + size)
        allowed = allowed_keys(place, start, size, keys)
        for head in range(q_ref.shape[1] // head_dim):
            cols = slice(head * head_dim, (head + 1) * head_dim)
            query = q_ref[rows(start, size), cols]
            mixed = m_ref[rows(start, size), cols]
            scores = kernel_dot(query, key_ref[:keys, :], 1, 1) * scale
            scores = jnp.where(allowed, scores, MASKED_SCORE)
            probs = jnp.exp(scores - jnp.max(scores, axis=1, keepdims=True))
            probs = probs * (1 / jnp.sum(probs, axis=1, keepdims=True))
            value_sum[:keys, :] += kernel_dot(probs.astype(jnp.bfloat16), mixed, 0, 0)
            prob_grad = kernel_dot(mixed, value_ref[:keys, :], 1, 1)
            row_dot = jnp.sum(probs * prob_grad, axis=1, keepdims=True)
            score_low = (probs * (prob_grad - row_dot)).astype(jnp.bfloat16)
            key_sum[:keys, :] += kernel_dot(score_low, query, 0, 0)
            query_grad = kernel_dot(score_low, key_ref[:keys, :], 1, 0) * scale
            query_grad = turn(query_grad, cos_ref[span, :], -sin_ref[span, :])
            q_back_ref[rows(start, size), cols] = query_grad.astype(jnp.bfloat16)
    for start, size, _ in query_spans(length):
        span = slice(start, start + size)
        key_grad = turn(key_sum[span, :] * scale, cos_ref[span, :], -sin_ref[span, :])
        k_back_ref[rows(start, size), :] = key_grad.astype(jnp.bfloat16)
        v_back_ref[rows(start, size), :] = value_sum[span, :].astype(jnp.bfloat16)


def attention_call(kernel, name, first, heads, tables, outs, scratch, head_dim, flops):
    length = heads[0][0].shape[0]
    key_heads = flops[1]

    def head_spec(width, start):
        return pl.BlockSpec((length, width), lambda g, first_ref: (0, start + g))

    def whole_spec(shape):
        return pl.BlockSpec(shape, lambda g, first_ref: (0, 0))

    return pl.pallas_call(
        kernel,
        grid_spec=pltpu.PrefetchScalarGridSpec(
            num_scalar_prefetch=1,
            grid=(key_heads,),
            in_specs=[head_spec(width, start) for _, width, start in heads]
            + [whole_spec(table.shape) for table in tables],
            out_specs=[head_spec(width, 0) for width in outs],
            scratch_shapes=[pltpu.VMEM((length, head_dim), kind) for kind in scratch],
        ),
        out_shape=[
            jax.ShapeDtypeStruct((length, width * key_heads), jnp.bfloat16) for width in outs
        ],
        cost_estimate=pl.CostEstimate(
            flops=flops[0], bytes_accessed=flops[0] // 200, transcendentals=length * length
        ),
        name=name,
    )(first, *[array for array, _, _ in heads], *tables)


def swap(value, axis, bit):
    count = lax.axis_size(axis)
    return lax.ppermute(value, axis, [(i, i ^ bit) for i in range(count)])


def shift(value, axis, step):
    count = lax.axis_size(axis)
    return lax.ppermute(value, axis, [(i, (i + step) % count) for i in range(count)])


def tie(*values):
    return lax.optimization_barrier(values)


def ordered(first_when_zero, mine, theirs, dim):
    keep = first_when_zero == 0
    return jnp.concatenate(
        [jnp.where(keep, mine, theirs), jnp.where(keep, theirs, mine)], axis=dim
    )


def dot32(left, right):
    return jnp.dot(left, right, preferred_element_type=jnp.float32)


def dot_nt(left, right):
    return jnp.einsum("td,fd->tf", left, right, preferred_element_type=jnp.float32)


def dot_tn(left, right):
    return jnp.einsum("td,tf->df", left, right, preferred_element_type=jnp.float32)


def low(value):
    return value.astype(jnp.bfloat16)


def wide(value):
    return value.astype(jnp.float32)


def col_gather(mine):
    if lax.axis_size("col") == 2:
        return [mine, swap(mine, "col", 1)]
    return [lax.all_gather(mine, "col", axis=0, tiled=True)]


def col_scatter(product, beside=None):
    if lax.axis_size("col") == 2:
        theirs = swap(low(product(1)), "col", 1)
        if beside is not None:
            theirs, beside = tie(theirs, beside)
            return product(0) + wide(theirs), beside
        return product(0) + wide(theirs)
    if beside is not None:
        return col_scatter(product), beside
    return wide(lax.psum_scatter(low(product(0)), "col", scatter_dimension=0, tiled=True))


def blocks_of(value, dim, count):
    size = value.shape[dim] // count
    return [lax.slice_in_dim(value, i * size, (i + 1) * size, axis=dim) for i in range(count)]


def square_gather(mine):
    if lax.axis_size("col") == 2:
        over_x = swap(mine, "col", 1)
        over_y = swap(mine, "grp", 2)
        half = mine.shape[0] // 2
        across_first = swap(over_x[:half], "grp", 2)
        across_second = swap(over_y[half:], "col", 1)
        near = jnp.concatenate([mine, over_x], axis=0)
        return near, jnp.concatenate([over_y, across_first, across_second], axis=0)
    near = lax.all_gather(mine, "col", axis=0, tiled=True)
    return near, swap(near, "grp", 2)


def with_core(pack):
    return jnp.concatenate([pack, swap(pack, "grp", 1)], axis=0)


def square_scatter(near, far):
    size = far.shape[0]
    if lax.axis_size("col") == 2:
        half, part = size // 2, size // 4
        across_first = swap(far[half : half + part], "grp", 2)
        across_second = swap(far[half + part :], "col", 1)
        rest = jnp.zeros_like(across_first)
        to_y = low(wide(far[:half]) + wide(jnp.concatenate([rest, across_second], axis=0)))
        to_x = low(near(half, size) + wide(jnp.concatenate([across_first, rest], axis=0)))
        from_y = swap(to_y, "grp", 2)
        from_x = swap(to_x, "col", 1)
        return near(0, half) + wide(from_x) + wide(from_y)
    total = low(near(0, size) + wide(swap(far, "grp", 2)))
    return wide(lax.psum_scatter(total, "col", scatter_dimension=0, tiled=True))


def butterfly(value, axes):
    for axis in axes:
        bit = 1
        while bit < lax.axis_size(axis):
            value = value + swap(value, axis, bit)
            bit *= 2
    return value


def half_rows(value, bit):
    size = value.shape[0] // 2
    return lax.dynamic_slice_in_dim(value, bit * size, size, 0)


def row_gather(value):
    return lax.all_gather(value, "row", axis=0, tiled=True)


def row_scatter(value):
    return lax.psum_scatter(value, "row", scatter_dimension=0, tiled=True)


def sum_quarters(value, core, ypos):
    return sum_y(sum_cores(value, core), ypos)


def sum_cores(value, core):
    return low(wide(half_rows(value, core)) + wide(swap(half_rows(value, 1 - core), "grp", 1)))


def sum_y(part, ypos):
    part = low(wide(half_rows(part, ypos)) + wide(swap(half_rows(part, 1 - ypos), "grp", 2)))
    return part


def spread_y(part, ypos):
    return ordered(ypos, part, swap(part, "grp", 2), 0)


def spread_core(part, core):
    return ordered(core, part, swap(part, "grp", 1), 0)


def own_quarter(weight, core, ypos):
    size = weight.shape[0] // 4
    return lax.dynamic_slice_in_dim(weight, (2 * core + ypos) * size, size, 0)


def spread_quarters(part, core, ypos, dim):
    half = ordered(ypos, part, swap(part, "grp", 2), dim)
    return wide(ordered(core, half, swap(half, "grp", 1), dim))


def per_device(
    tokens,
    cotangent,
    segments,
    positions,
    first_gain,
    query_weight,
    key_matrix,
    value_matrix,
    output_weight,
    second_gain,
    gate_weight,
    up_weight,
    down_weight,
):
    head_dim = HEAD_SIZE
    query_heads = query_weight.shape[1] // head_dim
    heads_per_group = QUERY_HEADS // KEY_VALUE_HEADS
    key_heads = max(1, query_heads // heads_per_group)
    head_share = query_heads // key_heads
    head_sharing = max(1, heads_per_group // query_heads)
    col = lax.axis_index("col")
    key_first = col * query_heads // heads_per_group
    query_cols = query_heads * head_dim
    key_cols = key_heads * head_dim
    rows, width = tokens.shape
    grp, zpos = lax.axis_index("grp"), lax.axis_index("row")
    core, ypos = lax.rem(grp, 2), lax.div(grp, 2)
    in_pairs = lax.axis_size("col") == 2

    inputs = wide(tokens)
    normalized_input, first_back = jax.vjp(normalize, inputs, first_gain)
    gathered_in = jnp.concatenate(col_gather(low(normalized_input)), axis=0)
    packed_length = gathered_in.shape[0]

    down_own, gate_own, up_own = [
        own_quarter(weight, core, ypos) for weight in (down_weight, gate_weight.T, up_weight.T)
    ]
    down_rows = row_gather(down_own)
    gate_up = lax.all_gather(jnp.stack([gate_own, up_own]), "row", axis=0)

    cot_far = []
    if in_pairs:
        gathered_in, cot_now, cot_over_y = tie(
            gathered_in, cotangent, swap(cotangent, "grp", 2)
        )
        cot_far.append(cot_over_y)
    else:
        gathered_in, cot_now = tie(gathered_in, cotangent)
    cot_near = col_gather(cot_now)

    key_slice = lax.dynamic_slice_in_dim(key_matrix, key_first * head_dim, key_cols, 1)
    value_slice = lax.dynamic_slice_in_dim(value_matrix, key_first * head_dim, key_cols, 1)
    project_in = jnp.concatenate([query_weight, key_slice, value_slice], axis=1)
    projected = dot32(gathered_in, project_in)
    cosine, sine = rope_tables(positions, head_dim)
    tables = (cosine, sine, positions[None], positions[:, None], segments[None], segments[:, None])
    first = (col if in_pairs else jnp.zeros_like(col)).astype(jnp.int32).reshape(1)
    group_cols = head_share * head_dim
    score_flops = query_cols * packed_length * packed_length
    attn_low, query_low, key_low, value_low = attention_call(
        attend_kernel,
        "attend",
        first,
        [
            (projected, group_cols, 0),
            (projected, head_dim, query_heads),
            (projected, head_dim, query_heads + key_heads),
        ],
        tables,
        (group_cols, group_cols, head_dim, head_dim),
        (jnp.bfloat16, jnp.bfloat16),
        head_dim,
        (3 * score_flops, key_heads),
    )
    attn_low, down_rows, cot_near[-1] = tie(attn_low, down_rows, cot_near[-1])
    cot_far.append(swap(cot_near[-1], "grp", 2))
    cot_sets = [with_core(jnp.concatenate(pack, axis=0)) for pack in (cot_near, cot_far)]
    act_near = low(dot_nt(cot_sets[0], down_rows))
    act_far = low(dot_nt(cot_sets[1], down_rows))
    attn_parts = blocks_of(attn_low, 0, 2) if in_pairs else [attn_low]
    from_attention, act_near = col_scatter(
        lambda i: dot32(attn_parts[i], output_weight), act_near
    )
    hidden_res = inputs + from_attention
    normed_mid, second_back = jax.vjp(normalize, hidden_res, second_gain)

    mid_near, mid_far = square_gather(low(normed_mid))
    mid_near, act_far = tie(mid_near, act_far)
    gate_rows, up_rows = [gate_up[:, i].reshape(-1, width) for i in range(2)]
    mid_near = with_core(mid_near)
    gate_near, mid_far = tie(low(dot_nt(mid_near, gate_rows)), mid_far)
    mid_sets = [mid_near, with_core(mid_far)]
    gate_lins = [gate_near, low(dot_nt(mid_sets[1], gate_rows))]
    act_grads = [act_near, act_far]
    acts, gate_backs, up_backs = [], [], []
    for mid, act_grad, gate_lin in zip(mid_sets, act_grads, gate_lins):
        gate32 = wide(gate_lin)
        up_lin = dot_nt(mid, up_rows)
        sig = jax.nn.sigmoid(gate32)
        acts.append(low(gate32 * sig * up_lin))
        gate_backs.append(low(wide(act_grad) * up_lin * sig * (1 + gate32 * (1 - sig))))
        up_backs.append(low(wide(act_grad) * gate32 * sig))

    def weight_sum(lefts, rights):
        return low(sum(dot_tn(left, right) for left, right in zip(lefts, rights)))

    def far_sum(product):
        pack = packed_length
        theirs = swap(low(product(1, pack, 2 * pack)), "grp", 1)
        return low(product(1, 0, pack) + wide(theirs))

    def near_sum(product):
        pack = packed_length
        return swap(low(product(0, pack, 2 * pack)), "grp", 1)

    def mid_product(i, a, b):
        return dot32(gate_backs[i][a:b], gate_rows) + dot32(up_backs[i][a:b], up_rows)

    def out_product(i, a, b):
        return dot32(acts[i][a:b], down_rows)

    down_low = weight_sum(acts, cot_sets)
    down_low, gate_backs[1], up_backs[1] = tie(down_low, gate_backs[1], up_backs[1])
    down_part = row_scatter(down_low)
    mid_from_core = near_sum(mid_product)
    mid_far_sum = far_sum(mid_product)
    mid_far_sum, gate_backs[0], up_backs[0], gate_backs[1] = tie(
        mid_far_sum, gate_backs[0], up_backs[0], gate_backs[1]
    )
    mid_grad = square_scatter(
        lambda first, last: mid_product(0, first, last) + wide(mid_from_core[first:last]),
        mid_far_sum,
    )
    gate_low = weight_sum(gate_backs, mid_sets)
    gate_part = row_scatter(gate_low)
    out_far = far_sum(out_product)
    out_far, up_backs[1] = tie(out_far, up_backs[1])
    out_over_y = swap(out_far, "grp", 2)
    up_part = row_scatter(weight_sum(up_backs, mid_sets))

    res_from_mid, second_gain_part = second_back(mid_grad)
    res_grad = wide(cotangent) + res_from_mid
    res_low, down_part = tie(low(res_grad), down_part)
    shard_rows = jnp.concatenate(col_gather(res_low), axis=0)
    shard_rows, gate_part = tie(shard_rows, gate_part)

    mixed_low = low(dot_nt(shard_rows, output_weight))
    out_low = low(dot_tn(attn_low, shard_rows))
    mixed_low, out_low = tie(mixed_low, sum_cores(out_low, core))
    out_part, up_part = tie(sum_y(out_low, ypos), up_part)
    out_part = row_scatter(out_part)
    query_back, key_back, value_back = attention_call(
        attend_back_kernel,
        "attend_back",
        first,
        [
            (query_low, group_cols, 0),
            (key_low, head_dim, 0),
            (value_low, head_dim, 0),
            (mixed_low, group_cols, 0),
        ],
        tables,
        (group_cols, head_dim, head_dim),
        (jnp.bfloat16, jnp.bfloat16, jnp.float32, jnp.float32),
        head_dim,
        (7 * score_flops, key_heads),
    )
    query_back, out_over_y, acts[0] = tie(query_back, out_over_y, acts[0])
    pair_back = jnp.concatenate([key_back, value_back], axis=1)
    back_all = jnp.concatenate([query_back, pair_back], axis=1)
    query_part = sum_quarters(low(dot_tn(gathered_in, query_back)), core, ypos)
    pair_part = sum_quarters(low(dot_tn(gathered_in, pair_back)), core, ypos)
    query_part, pair_part, down_part, gate_part, second_gain_part, acts[0] = tie(
        query_part, pair_part, down_part, gate_part, second_gain_part, acts[0]
    )
    out_part, query_part, pair_part = tie(
        out_part, row_scatter(query_part), row_scatter(pair_part)
    )
    pair_part, query_part, out_part = [row_gather(p) for p in (pair_part, query_part, out_part)]
    back_parts = blocks_of(back_all, 0, 2) if in_pairs else [back_all]
    in_grad = col_scatter(lambda i: dot_nt(back_parts[i], project_in))

    out_from_core = near_sum(out_product)
    piece = packed_length // 2 if in_pairs else packed_length

    def out_rows(i):
        part = slice(i * piece, (i + 1) * piece)
        return out_product(0, part.start, part.stop) + wide(out_from_core[part]) + wide(out_over_y[part])

    layer_out = hidden_res + col_scatter(out_rows)
    res_from_in, _ = first_back(in_grad)
    input_grad = res_grad + res_from_in

    down_grad = spread_quarters(down_part, core, ypos, 0)
    gate_grad = spread_quarters(gate_part.T, core, ypos, 1)
    up_grad = spread_quarters(up_part.T, core, ypos, 1)
    out_wgrad = spread_quarters(out_part, core, ypos, 0)
    query_wgrad = spread_quarters(query_part, core, ypos, 0)
    if in_pairs:
        over_x, over_y = swap(pair_part, "col", 1), swap(pair_part, "grp", 2)
        half = pair_part.shape[0] // 2
        across = jnp.concatenate(
            [swap(over_x[:half], "grp", 2), swap(over_y[half:], "col", 1)], axis=0
        )
        pair_part = ordered(ypos, pair_part, over_y, 0)
        theirs = ordered(ypos, over_x, across, 0)
        key_part = ordered(col, pair_part[:, :key_cols], theirs[:, :key_cols], 1)
        value_part = ordered(col, pair_part[:, key_cols:], theirs[:, key_cols:], 1)
        key_full = wide(ordered(core, key_part, swap(key_part, "grp", 1), 0))
        value_full = wide(ordered(core, value_part, swap(value_part, "grp", 1), 0))
    else:
        pair_part = ordered(ypos, pair_part, swap(pair_part, "grp", 2), 0)
        pair_part = ordered(core, pair_part, swap(pair_part, "grp", 1), 0)
        pair_all = wide(lax.all_gather(pair_part, "col", axis=0))
        groups = lax.axis_size("col") // head_sharing

        def spread(piece):
            piece = jnp.sum(piece.reshape(groups, head_sharing, width, key_cols), axis=1)
            return jnp.swapaxes(piece, 0, 1).reshape(width, groups * key_cols)

        key_full = spread(pair_all[..., :key_cols])
        value_full = spread(pair_all[..., key_cols:])
    query_term = jnp.sum(query_wgrad * wide(query_weight), axis=1)
    pair_term = jnp.sum(key_full * wide(key_matrix) + value_full * wide(value_matrix), axis=1)
    query_term = butterfly(query_term.reshape(8, -1), ("col",)).reshape(-1)
    first_gain_grad = (query_term + pair_term) / first_gain
    axes = ("grp", "row", "col")
    second_gain_grad = butterfly(second_gain_part.reshape(8, -1), axes).reshape(-1)
    return (
        layer_out,
        input_grad,
        first_gain_grad,
        query_wgrad,
        key_full,
        value_full,
        out_wgrad,
        second_gain_grad,
        gate_grad,
        up_grad,
        down_grad,
    )


def solution(mesh):
    return jax.shard_map(
        per_device,
        mesh=mesh,
        in_specs=(
            P(("grp", "row", "col"), None),
            P(("grp", "row", "col"), None),
            P(("grp", "row")),
            P(("grp", "row")),
            P(),
            P(None, "col"),
            P(),
            P(),
            P("col", None),
            P(),
            P(None, ("row", "col")),
            P(None, ("row", "col")),
            P(("row", "col"), None),
        ),
        out_specs=(
            P(("grp", "row", "col"), None),
            P(("grp", "row", "col"), None),
            P(),
            P(None, "col"),
            P(),
            P(),
            P("col", None),
            P(),
            P(None, ("row", "col")),
            P(None, ("row", "col")),
            P(("row", "col"), None),
        ),
        check_vma=False,
    )
```

```python
import math

import jax
import jax.numpy as jnp
from jax import lax
from jax.experimental import pallas as pl
from jax.experimental.pallas import tpu as pltpu
from jax.sharding import PartitionSpec as P

QUERY_HEADS = 8
KEY_VALUE_HEADS = 4
HEAD_SIZE = 256


NORM_EPSILON = 1e-06
ROPE_BASE = 1000042.0
MASKED_SCORE = -1e30


def normalize(values, gain):
    inverse = lax.rsqrt(jnp.mean(values * values, axis=-1, keepdims=True) + NORM_EPSILON)
    return values * inverse * gain


def rope_tables(positions, head_dim):
    half_dim = head_dim // 2
    exponent = jnp.arange(half_dim, dtype=jnp.float32) * (2.0 / head_dim)
    inverse_freq = jnp.exp(-math.log(ROPE_BASE) * exponent)
    angles = positions.astype(jnp.float32)[:, None] * inverse_freq[None, :]
    return (jnp.cos(angles), jnp.sin(angles))


def turn(value, cosine, sine):
    half = value.shape[-1] // 2
    first, second = value[:, :half], value[:, half:]
    return jnp.concatenate(
        [first * cosine - second * sine, second * cosine + first * sine], axis=-1
    )


def kernel_dot(left, right, left_dim, right_dim):
    return lax.dot_general(
        left, right, (((left_dim,), (right_dim,)), ((), ())), preferred_element_type=jnp.float32
    )


def query_spans(length):
    step = length // 4
    return [(i * step, step, (i + 1) * step) for i in range(4)]


def allowed_keys(place, start, size, keys):
    pos_row, pos_col, seg_row, seg_col = place
    key_seg = seg_row[:, :keys]
    return (pos_row[:, :keys] <= pos_col[start : start + size, :]) & (
        (key_seg == 0) | (key_seg == seg_col[start : start + size, :])
    )


def stored_rows(first_ref, length):
    half = length // 2
    offsets = [first_ref[0] * half, (1 - first_ref[0]) * half]

    def rows(start, size):
        offset = pl.multiple_of(offsets[start // half] + start % half, size)
        return pl.ds(offset, size)

    return rows


def attend_kernel(
    first_ref, q_ref, k_ref, v_ref, cos_ref, sin_ref, pr_ref, pc_ref, sr_ref, sc_ref,
    out_ref, q_low_ref, k_low_ref, v_low_ref, key_ref, value_ref,
):
    length, head_dim = k_ref.shape
    rows = stored_rows(first_ref, length)
    place = (pr_ref, pc_ref, sr_ref, sc_ref)
    for start, size, _ in query_spans(length):
        span = slice(start, start + size)
        key = turn(k_ref[rows(start, size), :], cos_ref[span, :], sin_ref[span, :])
        key = key.astype(jnp.bfloat16)
        value = v_ref[rows(start, size), :].astype(jnp.bfloat16)
        key_ref[span, :] = key
        value_ref[span, :] = value
        k_low_ref[rows(start, size), :] = key
        v_low_ref[rows(start, size), :] = value
    for start, size, keys in query_spans(length):
        span = slice(start, start + size)
        allowed = allowed_keys(place, start, size, keys)
        for head in range(q_ref.shape[1] // head_dim):
            cols = slice(head * head_dim, (head + 1) * head_dim)
            query = turn(q_ref[rows(start, size), cols], cos_ref[span, :], sin_ref[span, :])
            query = query.astype(jnp.bfloat16)
            q_low_ref[rows(start, size), cols] = query
            scores = kernel_dot(query, key_ref[:keys, :], 1, 1) * head_dim**-0.5
            scores = jnp.where(allowed, scores, MASKED_SCORE)
            weights = jnp.exp(scores - jnp.max(scores, axis=1, keepdims=True))
            weights = weights * (1 / jnp.sum(weights, axis=1, keepdims=True))
            mixed = kernel_dot(weights.astype(jnp.bfloat16), value_ref[:keys, :], 1, 0)
            out_ref[rows(start, size), cols] = mixed.astype(jnp.bfloat16)


def attend_back_kernel(
    first_ref, q_ref, k_ref, v_ref, m_ref, cos_ref, sin_ref, pr_ref, pc_ref, sr_ref, sc_ref,
    q_back_ref, k_back_ref, v_back_ref, key_ref, value_ref, key_sum, value_sum,
):
    length, head_dim = k_ref.shape
    scale = head_dim**-0.5
    rows = stored_rows(first_ref, length)
    place = (pr_ref, pc_ref, sr_ref, sc_ref)
    for start, size, _ in query_spans(length):
        span = slice(start, start + size)
        key_ref[span, :] = k_ref[rows(start, size), :]
        value_ref[span, :] = v_ref[rows(start, size), :]
    key_sum[...] = jnp.zeros_like(key_sum)
    value_sum[...] = jnp.zeros_like(value_sum)
    for start, size, keys in query_spans(length):
        span = slice(start, start + size)
        allowed = allowed_keys(place, start, size, keys)
        for head in range(q_ref.shape[1] // head_dim):
            cols = slice(head * head_dim, (head + 1) * head_dim)
            query = q_ref[rows(start, size), cols]
            mixed = m_ref[rows(start, size), cols]
            scores = kernel_dot(query, key_ref[:keys, :], 1, 1) * scale
            scores = jnp.where(allowed, scores, MASKED_SCORE)
            probs = jnp.exp(scores - jnp.max(scores, axis=1, keepdims=True))
            probs = probs * (1 / jnp.sum(probs, axis=1, keepdims=True))
            value_sum[:keys, :] += kernel_dot(probs.astype(jnp.bfloat16), mixed, 0, 0)
            prob_grad = kernel_dot(mixed, value_ref[:keys, :], 1, 1)
            row_dot = jnp.sum(probs * prob_grad, axis=1, keepdims=True)
            score_low = (probs * (prob_grad - row_dot)).astype(jnp.bfloat16)
            key_sum[:keys, :] += kernel_dot(score_low, query, 0, 0)
            query_grad = kernel_dot(score_low, key_ref[:keys, :], 1, 0) * scale
            query_grad = turn(query_grad, cos_ref[span, :], -sin_ref[span, :])
            q_back_ref[rows(start, size), cols] = query_grad.astype(jnp.bfloat16)
    for start, size, _ in query_spans(length):
        span = slice(start, start + size)
        key_grad = turn(key_sum[span, :] * scale, cos_ref[span, :], -sin_ref[span, :])
        k_back_ref[rows(start, size), :] = key_grad.astype(jnp.bfloat16)
        v_back_ref[rows(start, size), :] = value_sum[span, :].astype(jnp.bfloat16)


def attention_call(kernel, name, first, heads, tables, outs, scratch, head_dim, flops):
    length = heads[0][0].shape[0]
    key_heads = flops[1]

    def head_spec(width, start):
        return pl.BlockSpec((length, width), lambda g, first_ref: (0, start + g))

    def whole_spec(shape):
        return pl.BlockSpec(shape, lambda g, first_ref: (0, 0))

    return pl.pallas_call(
        kernel,
        grid_spec=pltpu.PrefetchScalarGridSpec(
            num_scalar_prefetch=1,
            grid=(key_heads,),
            in_specs=[head_spec(width, start) for _, width, start in heads]
            + [whole_spec(table.shape) for table in tables],
            out_specs=[head_spec(width, 0) for width in outs],
            scratch_shapes=[pltpu.VMEM((length, head_dim), kind) for kind in scratch],
        ),
        out_shape=[
            jax.ShapeDtypeStruct((length, width * key_heads), jnp.bfloat16) for width in outs
        ],
        cost_estimate=pl.CostEstimate(
            flops=flops[0], bytes_accessed=flops[0] // 200, transcendentals=length * length
        ),
        name=name,
    )(first, *[array for array, _, _ in heads], *tables)


def swap(value, axis, bit):
    count = lax.axis_size(axis)
    return lax.ppermute(value, axis, [(i, i ^ bit) for i in range(count)])


def shift(value, axis, step):
    count = lax.axis_size(axis)
    return lax.ppermute(value, axis, [(i, (i + step) % count) for i in range(count)])


def tie(*values):
    return lax.optimization_barrier(values)


def ordered(first_when_zero, mine, theirs, dim):
    keep = first_when_zero == 0
    return jnp.concatenate(
        [jnp.where(keep, mine, theirs), jnp.where(keep, theirs, mine)], axis=dim
    )


def dot32(left, right):
    return jnp.dot(left, right, preferred_element_type=jnp.float32)


def dot_nt(left, right):
    return jnp.einsum("td,fd->tf", left, right, preferred_element_type=jnp.float32)


def dot_tn(left, right):
    return jnp.einsum("td,tf->df", left, right, preferred_element_type=jnp.float32)


def low(value):
    return value.astype(jnp.bfloat16)


def wide(value):
    return value.astype(jnp.float32)


def col_gather(mine):
    if lax.axis_size("col") == 2:
        return [mine, swap(mine, "col", 1)]
    return [lax.all_gather(mine, "col", axis=0, tiled=True)]


def col_scatter(product):
    if lax.axis_size("col") == 2:
        theirs = swap(low(product(1)), "col", 1)
        return product(0) + wide(theirs)
    return wide(lax.psum_scatter(low(product(0)), "col", scatter_dimension=0, tiled=True))


def blocks_of(value, dim, count):
    size = value.shape[dim] // count
    return [lax.slice_in_dim(value, i * size, (i + 1) * size, axis=dim) for i in range(count)]


def square_gather(mine, beside_first, beside_second):
    if lax.axis_size("col") == 2:
        over_x, over_y, beside_first = tie(
            swap(mine, "col", 1), swap(mine, "grp", 2), beside_first
        )
        half = mine.shape[0] // 2
        across_first, across_second, beside_second = tie(
            swap(over_x[:half], "grp", 2), swap(over_y[half:], "col", 1), beside_second
        )
        near = jnp.concatenate([mine, over_x], axis=0)
        far = jnp.concatenate([over_y, across_first, across_second], axis=0)
        return near, far, beside_first, beside_second
    near = lax.all_gather(mine, "col", axis=0, tiled=True)
    return near, swap(near, "grp", 2), beside_first, beside_second


def with_core(pack):
    return jnp.concatenate([pack, swap(pack, "grp", 1)], axis=0)


def square_scatter(near, far, later):
    size = far.shape[0]
    if lax.axis_size("col") == 2:
        half, part = size // 2, size // 4
        across_first = swap(far[half : half + part], "grp", 2)
        across_second = swap(far[half + part :], "col", 1)
        rest = jnp.zeros_like(across_first)
        to_y = low(wide(far[:half]) + wide(jnp.concatenate([rest, across_second], axis=0)))
        to_x = low(near(half, size) + wide(jnp.concatenate([across_first, rest], axis=0)))
        to_y, to_x, *later = tie(to_y, to_x, *later)
        from_y = swap(to_y, "grp", 2)
        from_x = swap(to_x, "col", 1)
        return near(0, half) + wide(from_x) + wide(from_y), later
    total = low(near(0, size) + wide(swap(far, "grp", 2)))
    return wide(lax.psum_scatter(total, "col", scatter_dimension=0, tiled=True)), later


def butterfly(value, axes):
    for axis in axes:
        bit = 1
        while bit < lax.axis_size(axis):
            value = value + swap(value, axis, bit)
            bit *= 2
    return value


def half_rows(value, bit):
    size = value.shape[0] // 2
    return lax.dynamic_slice_in_dim(value, bit * size, size, 0)


def row_gather(value):
    return lax.all_gather(value, "row", axis=0, tiled=True)


def row_scatter(value):
    return lax.psum_scatter(value, "row", scatter_dimension=0, tiled=True)


def sum_quarters(value, core, ypos):
    return sum_y(sum_cores(value, core), ypos)


def sum_cores(value, core):
    return low(wide(half_rows(value, core)) + wide(swap(half_rows(value, 1 - core), "grp", 1)))


def sum_y(part, ypos):
    part = low(wide(half_rows(part, ypos)) + wide(swap(half_rows(part, 1 - ypos), "grp", 2)))
    return part


def spread_y(part, ypos):
    return ordered(ypos, part, swap(part, "grp", 2), 0)


def spread_core(part, core):
    return ordered(core, part, swap(part, "grp", 1), 0)


def own_quarter(weight, core, ypos):
    size = weight.shape[0] // 4
    return lax.dynamic_slice_in_dim(weight, (2 * core + ypos) * size, size, 0)


def spread_quarters(part, core, ypos, dim):
    half = ordered(ypos, part, swap(part, "grp", 2), dim)
    return wide(ordered(core, half, swap(half, "grp", 1), dim))


def per_device(
    tokens,
    cotangent,
    segments,
    positions,
    first_gain,
    query_weight,
    key_matrix,
    value_matrix,
    output_weight,
    second_gain,
    gate_weight,
    up_weight,
    down_weight,
):
    head_dim = HEAD_SIZE
    query_heads = query_weight.shape[1] // head_dim
    heads_per_group = QUERY_HEADS // KEY_VALUE_HEADS
    key_heads = max(1, query_heads // heads_per_group)
    head_share = query_heads // key_heads
    head_sharing = max(1, heads_per_group // query_heads)
    col = lax.axis_index("col")
    key_first = col * query_heads // heads_per_group
    query_cols = query_heads * head_dim
    key_cols = key_heads * head_dim
    rows, width = tokens.shape
    grp, zpos = lax.axis_index("grp"), lax.axis_index("row")
    core, ypos = lax.rem(grp, 2), lax.div(grp, 2)
    in_pairs = lax.axis_size("col") == 2

    inputs = wide(tokens)
    normalized_input, first_back = jax.vjp(normalize, inputs, first_gain)
    gathered_in = jnp.concatenate(col_gather(low(normalized_input)), axis=0)
    packed_length = gathered_in.shape[0]

    down_rows, gate_rows, up_rows = [
        row_gather(own_quarter(weight, core, ypos))
        for weight in (down_weight, gate_weight.T, up_weight.T)
    ]

    gathered_in, cot_now = tie(gathered_in, cotangent)
    cot_near = col_gather(cot_now)
    cot_far = [swap(cotangent, "grp", 2)] if in_pairs else []
    cot_far.append(swap(cot_near[-1], "grp", 2))
    cot_sets = [with_core(jnp.concatenate(pack, axis=0)) for pack in (cot_near, cot_far)]

    key_slice = lax.dynamic_slice_in_dim(key_matrix, key_first * head_dim, key_cols, 1)
    value_slice = lax.dynamic_slice_in_dim(value_matrix, key_first * head_dim, key_cols, 1)
    project_in = jnp.concatenate([query_weight, key_slice, value_slice], axis=1)
    projected = dot32(gathered_in, project_in)
    cosine, sine = rope_tables(positions, head_dim)
    tables = (cosine, sine, positions[None], positions[:, None], segments[None], segments[:, None])
    first = (col if in_pairs else jnp.zeros_like(col)).astype(jnp.int32).reshape(1)
    group_cols = head_share * head_dim
    score_flops = query_cols * packed_length * packed_length
    attn_low, query_low, key_low, value_low = attention_call(
        attend_kernel,
        "attend",
        first,
        [
            (projected, group_cols, 0),
            (projected, head_dim, query_heads),
            (projected, head_dim, query_heads + key_heads),
        ],
        tables,
        (group_cols, group_cols, head_dim, head_dim),
        (jnp.bfloat16, jnp.bfloat16),
        head_dim,
        (3 * score_flops, key_heads),
    )
    attn_low, down_rows = tie(attn_low, down_rows)
    act_near = low(dot_nt(cot_sets[0], down_rows))
    act_far = low(dot_nt(cot_sets[1], down_rows))
    attn_parts = blocks_of(attn_low, 0, 2) if in_pairs else [attn_low]
    hidden_res = inputs + col_scatter(lambda i: dot32(attn_parts[i], output_weight))
    normed_mid, second_back = jax.vjp(normalize, hidden_res, second_gain)

    mid_near, mid_far, act_near, act_far = square_gather(low(normed_mid), act_near, act_far)
    mid_sets = [with_core(mid_near), with_core(mid_far)]
    gate_lins = [low(dot_nt(mid, gate_rows)) for mid in mid_sets]
    act_grads = [act_near, act_far]
    acts, gate_backs, up_backs = [], [], []
    for mid, act_grad, gate_lin in zip(mid_sets, act_grads, gate_lins):
        gate32 = wide(gate_lin)
        up_lin = dot_nt(mid, up_rows)
        sig = jax.nn.sigmoid(gate32)
        acts.append(low(gate32 * sig * up_lin))
        gate_backs.append(low(wide(act_grad) * up_lin * sig * (1 + gate32 * (1 - sig))))
        up_backs.append(low(wide(act_grad) * gate32 * sig))

    def weight_sum(lefts, rights):
        return low(sum(dot_tn(left, right) for left, right in zip(lefts, rights)))

    def far_sum(product):
        pack = packed_length
        theirs = swap(low(product(1, pack, 2 * pack)), "grp", 1)
        return low(product(1, 0, pack) + wide(theirs))

    def near_sum(product):
        pack = packed_length
        return swap(low(product(0, pack, 2 * pack)), "grp", 1)

    def mid_product(i, a, b):
        return dot32(gate_backs[i][a:b], gate_rows) + dot32(up_backs[i][a:b], up_rows)

    def out_product(i, a, b):
        return dot32(acts[i][a:b], down_rows)

    down_low = weight_sum(acts, cot_sets)
    down_low, gate_backs[1], up_backs[1] = tie(down_low, gate_backs[1], up_backs[1])
    down_part = row_scatter(down_low)
    mid_from_core = near_sum(mid_product)
    mid_far_sum = far_sum(mid_product)
    mid_far_sum, gate_backs[0], up_backs[0] = tie(mid_far_sum, gate_backs[0], up_backs[0])
    mid_grad, (gate_backs[1], acts[1]) = square_scatter(
        lambda first, last: mid_product(0, first, last) + wide(mid_from_core[first:last]),
        mid_far_sum,
        [gate_backs[1], acts[1]],
    )
    gate_part = row_scatter(weight_sum(gate_backs, mid_sets))
    out_far = far_sum(out_product)
    out_far, up_backs[1] = tie(out_far, up_backs[1])
    out_first, out_second = blocks_of(out_far, 0, 2)
    out_first = swap(out_first, "grp", 2)
    up_part = row_scatter(weight_sum(up_backs, mid_sets))

    res_from_mid, second_gain_part = second_back(mid_grad)
    res_grad = wide(cotangent) + res_from_mid
    res_low, down_part = tie(low(res_grad), down_part)
    shard_rows = jnp.concatenate(col_gather(res_low), axis=0)
    shard_rows, gate_part = tie(shard_rows, gate_part)

    mixed_low = low(dot_nt(shard_rows, output_weight))
    out_low = low(dot_tn(attn_low, shard_rows))
    mixed_low, out_low, out_first = tie(mixed_low, sum_cores(out_low, core), out_first)
    out_low = sum_y(out_low, ypos)
    query_back, key_back, value_back = attention_call(
        attend_back_kernel,
        "attend_back",
        first,
        [
            (query_low, group_cols, 0),
            (key_low, head_dim, 0),
            (value_low, head_dim, 0),
            (mixed_low, group_cols, 0),
        ],
        tables,
        (group_cols, head_dim, head_dim),
        (jnp.bfloat16, jnp.bfloat16, jnp.float32, jnp.float32),
        head_dim,
        (7 * score_flops, key_heads),
    )
    query_back, out_low = tie(query_back, out_low)
    out_part, up_part = tie(out_low, up_part)
    out_part = row_gather(row_scatter(out_part))
    pair_back = jnp.concatenate([key_back, value_back], axis=1)
    back_all = jnp.concatenate([query_back, pair_back], axis=1)
    query_low_grad = low(dot_tn(gathered_in, query_back))
    pair_low_grad = low(dot_tn(gathered_in, pair_back))
    query_low_grad, pair_low_grad, acts[0] = tie(query_low_grad, pair_low_grad, acts[0])
    query_part = sum_quarters(query_low_grad, core, ypos)
    pair_part = sum_quarters(pair_low_grad, core, ypos)
    query_part, pair_part, down_part, gate_part, second_gain_part, out_second = tie(
        query_part, pair_part, down_part, gate_part, second_gain_part, out_second
    )
    both_part = row_gather(row_scatter(jnp.concatenate([query_part, pair_part], axis=1)))
    query_part, pair_part = both_part[:, :query_cols], both_part[:, query_cols:]
    back_parts = blocks_of(back_all, 0, 2) if in_pairs else [back_all]
    in_grad = col_scatter(lambda i: dot_nt(back_parts[i], project_in))

    out_over_y = jnp.concatenate([out_first, swap(out_second, "grp", 2)], axis=0)
    out_from_core = near_sum(out_product)
    piece = packed_length // 2 if in_pairs else packed_length

    def out_rows(i):
        part = slice(i * piece, (i + 1) * piece)
        return out_product(0, part.start, part.stop) + wide(out_from_core[part]) + wide(out_over_y[part])

    layer_out = hidden_res + col_scatter(out_rows)
    res_from_in, _ = first_back(in_grad)
    input_grad = res_grad + res_from_in

    down_grad = spread_quarters(down_part, core, ypos, 0)
    gate_grad = spread_quarters(gate_part.T, core, ypos, 1)
    up_grad = spread_quarters(up_part.T, core, ypos, 1)
    out_wgrad = spread_quarters(out_part, core, ypos, 0)
    query_wgrad = spread_quarters(query_part, core, ypos, 0)
    if in_pairs:
        over_x, over_y = swap(pair_part, "col", 1), swap(pair_part, "grp", 2)
        half = pair_part.shape[0] // 2
        across = jnp.concatenate(
            [swap(over_x[:half], "grp", 2), swap(over_y[half:], "col", 1)], axis=0
        )
        pair_part = ordered(ypos, pair_part, over_y, 0)
        theirs = ordered(ypos, over_x, across, 0)
        key_part = ordered(col, pair_part[:, :key_cols], theirs[:, :key_cols], 1)
        value_part = ordered(col, pair_part[:, key_cols:], theirs[:, key_cols:], 1)
        key_full = wide(ordered(core, key_part, swap(key_part, "grp", 1), 0))
        value_full = wide(ordered(core, value_part, swap(value_part, "grp", 1), 0))
    else:
        pair_part = ordered(ypos, pair_part, swap(pair_part, "grp", 2), 0)
        pair_part = ordered(core, pair_part, swap(pair_part, "grp", 1), 0)
        pair_all = wide(lax.all_gather(pair_part, "col", axis=0))
        groups = lax.axis_size("col") // head_sharing

        def spread(piece):
            piece = jnp.sum(piece.reshape(groups, head_sharing, width, key_cols), axis=1)
            return jnp.swapaxes(piece, 0, 1).reshape(width, groups * key_cols)

        key_full = spread(pair_all[..., :key_cols])
        value_full = spread(pair_all[..., key_cols:])
    query_term = jnp.sum(query_wgrad * wide(query_weight), axis=1)
    pair_term = jnp.sum(key_full * wide(key_matrix) + value_full * wide(value_matrix), axis=1)
    query_term = butterfly(query_term.reshape(8, -1), ("col",)).reshape(-1)
    first_gain_grad = (query_term + pair_term) / first_gain
    axes = ("grp", "row", "col")
    second_gain_grad = butterfly(second_gain_part.reshape(8, -1), axes).reshape(-1)
    return (
        layer_out,
        input_grad,
        first_gain_grad,
        query_wgrad,
        key_full,
        value_full,
        out_wgrad,
        second_gain_grad,
        gate_grad,
        up_grad,
        down_grad,
    )


def solution(mesh):
    return jax.shard_map(
        per_device,
        mesh=mesh,
        in_specs=(
            P(("grp", "row", "col"), None),
            P(("grp", "row", "col"), None),
            P(("grp", "row")),
            P(("grp", "row")),
            P(),
            P(None, "col"),
            P(),
            P(),
            P("col", None),
            P(),
            P(None, ("row", "col")),
            P(None, ("row", "col")),
            P(("row", "col"), None),
        ),
        out_specs=(
            P(("grp", "row", "col"), None),
            P(("grp", "row", "col"), None),
            P(),
            P(None, "col"),
            P(),
            P(),
            P("col", None),
            P(),
            P(None, ("row", "col")),
            P(None, ("row", "col")),
            P(("row", "col"), None),
        ),
        check_vma=False,
    )
```

```python
import math

import jax
import jax.numpy as jnp
from jax import lax
from jax.experimental import pallas as pl
from jax.experimental.pallas import tpu as pltpu
from jax.sharding import PartitionSpec as P

QUERY_HEADS = 8
KEY_VALUE_HEADS = 4
HEAD_SIZE = 256


NORM_EPSILON = 1e-06
ROPE_BASE = 1000042.0
MASKED_SCORE = -1e30


def normalize(values, gain):
    inverse = lax.rsqrt(jnp.mean(values * values, axis=-1, keepdims=True) + NORM_EPSILON)
    return values * inverse * gain


def rope_tables(positions, head_dim):
    half_dim = head_dim // 2
    exponent = jnp.arange(half_dim, dtype=jnp.float32) * (2.0 / head_dim)
    inverse_freq = jnp.exp(-math.log(ROPE_BASE) * exponent)
    angles = positions.astype(jnp.float32)[:, None] * inverse_freq[None, :]
    return (jnp.cos(angles), jnp.sin(angles))


def turn(value, cosine, sine):
    half = value.shape[-1] // 2
    first, second = value[:, :half], value[:, half:]
    return jnp.concatenate(
        [first * cosine - second * sine, second * cosine + first * sine], axis=-1
    )


def kernel_dot(left, right, left_dim, right_dim):
    return lax.dot_general(
        left, right, (((left_dim,), (right_dim,)), ((), ())), preferred_element_type=jnp.float32
    )


def query_spans(length):
    step = length // 4
    return [(i * step, step, (i + 1) * step) for i in range(4)]


def allowed_keys(place, start, size, keys):
    pos_row, pos_col, seg_row, seg_col = place
    key_seg = seg_row[:, :keys]
    return (pos_row[:, :keys] <= pos_col[start : start + size, :]) & (
        (key_seg == 0) | (key_seg == seg_col[start : start + size, :])
    )


def stored_rows(first_ref, length):
    half = length // 2
    offsets = [first_ref[0] * half, (1 - first_ref[0]) * half]

    def rows(start, size):
        offset = pl.multiple_of(offsets[start // half] + start % half, size)
        return pl.ds(offset, size)

    return rows


def attend_kernel(
    first_ref, q_ref, k_ref, v_ref, cos_ref, sin_ref, pr_ref, pc_ref, sr_ref, sc_ref,
    out_ref, q_low_ref, k_low_ref, v_low_ref, key_ref, value_ref,
):
    length, head_dim = k_ref.shape
    rows = stored_rows(first_ref, length)
    place = (pr_ref, pc_ref, sr_ref, sc_ref)
    for start, size, _ in query_spans(length):
        span = slice(start, start + size)
        key = turn(k_ref[rows(start, size), :], cos_ref[span, :], sin_ref[span, :])
        key = key.astype(jnp.bfloat16)
        value = v_ref[rows(start, size), :].astype(jnp.bfloat16)
        key_ref[span, :] = key
        value_ref[span, :] = value
        k_low_ref[rows(start, size), :] = key
        v_low_ref[rows(start, size), :] = value
    for start, size, keys in query_spans(length):
        span = slice(start, start + size)
        allowed = allowed_keys(place, start, size, keys)
        for head in range(q_ref.shape[1] // head_dim):
            cols = slice(head * head_dim, (head + 1) * head_dim)
            query = turn(q_ref[rows(start, size), cols], cos_ref[span, :], sin_ref[span, :])
            query = query.astype(jnp.bfloat16)
            q_low_ref[rows(start, size), cols] = query
            scores = kernel_dot(query, key_ref[:keys, :], 1, 1) * head_dim**-0.5
            scores = jnp.where(allowed, scores, MASKED_SCORE)
            weights = jnp.exp(scores - jnp.max(scores, axis=1, keepdims=True))
            weights = weights * (1 / jnp.sum(weights, axis=1, keepdims=True))
            mixed = kernel_dot(weights.astype(jnp.bfloat16), value_ref[:keys, :], 1, 0)
            out_ref[rows(start, size), cols] = mixed.astype(jnp.bfloat16)


def attend_back_kernel(
    first_ref, q_ref, k_ref, v_ref, m_ref, cos_ref, sin_ref, pr_ref, pc_ref, sr_ref, sc_ref,
    q_back_ref, k_back_ref, v_back_ref, key_ref, value_ref, key_sum, value_sum,
):
    length, head_dim = k_ref.shape
    scale = head_dim**-0.5
    rows = stored_rows(first_ref, length)
    place = (pr_ref, pc_ref, sr_ref, sc_ref)
    for start, size, _ in query_spans(length):
        span = slice(start, start + size)
        key_ref[span, :] = k_ref[rows(start, size), :]
        value_ref[span, :] = v_ref[rows(start, size), :]
    key_sum[...] = jnp.zeros_like(key_sum)
    value_sum[...] = jnp.zeros_like(value_sum)
    for start, size, keys in query_spans(length):
        span = slice(start, start + size)
        allowed = allowed_keys(place, start, size, keys)
        for head in range(q_ref.shape[1] // head_dim):
            cols = slice(head * head_dim, (head + 1) * head_dim)
            query = q_ref[rows(start, size), cols]
            mixed = m_ref[rows(start, size), cols]
            scores = kernel_dot(query, key_ref[:keys, :], 1, 1) * scale
            scores = jnp.where(allowed, scores, MASKED_SCORE)
            probs = jnp.exp(scores - jnp.max(scores, axis=1, keepdims=True))
            probs = probs * (1 / jnp.sum(probs, axis=1, keepdims=True))
            value_sum[:keys, :] += kernel_dot(probs.astype(jnp.bfloat16), mixed, 0, 0)
            prob_grad = kernel_dot(mixed, value_ref[:keys, :], 1, 1)
            row_dot = jnp.sum(probs * prob_grad, axis=1, keepdims=True)
            score_low = (probs * (prob_grad - row_dot)).astype(jnp.bfloat16)
            key_sum[:keys, :] += kernel_dot(score_low, query, 0, 0)
            query_grad = kernel_dot(score_low, key_ref[:keys, :], 1, 0) * scale
            query_grad = turn(query_grad, cos_ref[span, :], -sin_ref[span, :])
            q_back_ref[rows(start, size), cols] = query_grad.astype(jnp.bfloat16)
    for start, size, _ in query_spans(length):
        span = slice(start, start + size)
        key_grad = turn(key_sum[span, :] * scale, cos_ref[span, :], -sin_ref[span, :])
        k_back_ref[rows(start, size), :] = key_grad.astype(jnp.bfloat16)
        v_back_ref[rows(start, size), :] = value_sum[span, :].astype(jnp.bfloat16)


def attention_call(kernel, name, first, heads, tables, outs, scratch, head_dim, flops):
    length = heads[0][0].shape[0]
    key_heads = flops[1]

    def head_spec(width, start):
        return pl.BlockSpec((length, width), lambda g, first_ref: (0, start + g))

    def whole_spec(shape):
        return pl.BlockSpec(shape, lambda g, first_ref: (0, 0))

    return pl.pallas_call(
        kernel,
        grid_spec=pltpu.PrefetchScalarGridSpec(
            num_scalar_prefetch=1,
            grid=(key_heads,),
            in_specs=[head_spec(width, start) for _, width, start in heads]
            + [whole_spec(table.shape) for table in tables],
            out_specs=[head_spec(width, 0) for width in outs],
            scratch_shapes=[pltpu.VMEM((length, head_dim), kind) for kind in scratch],
        ),
        out_shape=[
            jax.ShapeDtypeStruct((length, width * key_heads), jnp.bfloat16) for width in outs
        ],
        cost_estimate=pl.CostEstimate(
            flops=flops[0], bytes_accessed=flops[0] // 200, transcendentals=length * length
        ),
        name=name,
    )(first, *[array for array, _, _ in heads], *tables)


def swap(value, axis, bit):
    count = lax.axis_size(axis)
    return lax.ppermute(value, axis, [(i, i ^ bit) for i in range(count)])


def shift(value, axis, step):
    count = lax.axis_size(axis)
    return lax.ppermute(value, axis, [(i, (i + step) % count) for i in range(count)])


def tie(*values):
    return lax.optimization_barrier(values)


def ordered(first_when_zero, mine, theirs, dim):
    keep = first_when_zero == 0
    return jnp.concatenate(
        [jnp.where(keep, mine, theirs), jnp.where(keep, theirs, mine)], axis=dim
    )


def dot32(left, right):
    return jnp.dot(left, right, preferred_element_type=jnp.float32)


def dot_nt(left, right):
    return jnp.einsum("td,fd->tf", left, right, preferred_element_type=jnp.float32)


def dot_tn(left, right):
    return jnp.einsum("td,tf->df", left, right, preferred_element_type=jnp.float32)


def low(value):
    return value.astype(jnp.bfloat16)


def wide(value):
    return value.astype(jnp.float32)


def col_gather(mine):
    if lax.axis_size("col") == 2:
        return [mine, swap(mine, "col", 1)]
    return [lax.all_gather(mine, "col", axis=0, tiled=True)]


def col_scatter(product):
    if lax.axis_size("col") == 2:
        theirs = swap(low(product(1)), "col", 1)
        return product(0) + wide(theirs)
    return wide(lax.psum_scatter(low(product(0)), "col", scatter_dimension=0, tiled=True))


def blocks_of(value, dim, count):
    size = value.shape[dim] // count
    return [lax.slice_in_dim(value, i * size, (i + 1) * size, axis=dim) for i in range(count)]


def square_gather(mine, beside_first, beside_second):
    if lax.axis_size("col") == 2:
        over_x, over_y, beside_first = tie(
            swap(mine, "col", 1), swap(mine, "grp", 2), beside_first
        )
        half = mine.shape[0] // 2
        across_first, across_second, beside_second = tie(
            swap(over_x[:half], "grp", 2), swap(over_y[half:], "col", 1), beside_second
        )
        near = jnp.concatenate([mine, over_x], axis=0)
        far = jnp.concatenate([over_y, across_first, across_second], axis=0)
        return near, far, beside_first, beside_second
    near = lax.all_gather(mine, "col", axis=0, tiled=True)
    return near, swap(near, "grp", 2), beside_first, beside_second


def with_core(pack):
    return jnp.concatenate([pack, swap(pack, "grp", 1)], axis=0)


def square_scatter(near, far, later):
    size = far.shape[0]
    if lax.axis_size("col") == 2:
        half, part = size // 2, size // 4
        across_first = swap(far[half : half + part], "grp", 2)
        across_second = swap(far[half + part :], "col", 1)
        rest = jnp.zeros_like(across_first)
        to_y = low(wide(far[:half]) + wide(jnp.concatenate([rest, across_second], axis=0)))
        to_x = low(near(half, size) + wide(jnp.concatenate([across_first, rest], axis=0)))
        to_y, to_x, *later = tie(to_y, to_x, *later)
        from_y = swap(to_y, "grp", 2)
        from_x = swap(to_x, "col", 1)
        return near(0, half) + wide(from_x) + wide(from_y), later
    total = low(near(0, size) + wide(swap(far, "grp", 2)))
    return wide(lax.psum_scatter(total, "col", scatter_dimension=0, tiled=True)), later


def butterfly(value, axes):
    for axis in axes:
        bit = 1
        while bit < lax.axis_size(axis):
            value = value + swap(value, axis, bit)
            bit *= 2
    return value


def half_rows(value, bit):
    size = value.shape[0] // 2
    return lax.dynamic_slice_in_dim(value, bit * size, size, 0)


def row_gather(value):
    return lax.all_gather(value, "row", axis=0, tiled=True)


def row_scatter(value):
    return lax.psum_scatter(value, "row", scatter_dimension=0, tiled=True)


def sum_cores(value, core):
    return low(wide(half_rows(value, core)) + wide(swap(half_rows(value, 1 - core), "grp", 1)))


def sum_y(part, ypos):
    part = low(wide(half_rows(part, ypos)) + wide(swap(half_rows(part, 1 - ypos), "grp", 2)))
    return part


def spread_y(part, ypos):
    return ordered(ypos, part, swap(part, "grp", 2), 0)


def spread_core(part, core):
    return ordered(core, part, swap(part, "grp", 1), 0)


def own_quarter(weight, core, ypos):
    size = weight.shape[0] // 4
    return lax.dynamic_slice_in_dim(weight, (2 * core + ypos) * size, size, 0)


def spread_quarters(part, over_y, core, ypos, dim):
    half = ordered(ypos, part, over_y, dim)
    return wide(ordered(core, half, swap(half, "grp", 1), dim))


def per_device(
    tokens,
    cotangent,
    segments,
    positions,
    first_gain,
    query_weight,
    key_matrix,
    value_matrix,
    output_weight,
    second_gain,
    gate_weight,
    up_weight,
    down_weight,
):
    head_dim = HEAD_SIZE
    query_heads = query_weight.shape[1] // head_dim
    heads_per_group = QUERY_HEADS // KEY_VALUE_HEADS
    key_heads = max(1, query_heads // heads_per_group)
    head_share = query_heads // key_heads
    head_sharing = max(1, heads_per_group // query_heads)
    col = lax.axis_index("col")
    key_first = col * query_heads // heads_per_group
    query_cols = query_heads * head_dim
    key_cols = key_heads * head_dim
    rows, width = tokens.shape
    grp, zpos = lax.axis_index("grp"), lax.axis_index("row")
    core, ypos = lax.rem(grp, 2), lax.div(grp, 2)
    in_pairs = lax.axis_size("col") == 2

    inputs = wide(tokens)
    normalized_input, first_back = jax.vjp(normalize, inputs, first_gain)
    gathered_in = jnp.concatenate(col_gather(low(normalized_input)), axis=0)
    packed_length = gathered_in.shape[0]

    down_rows, gate_rows, up_rows = [
        row_gather(own_quarter(weight, core, ypos))
        for weight in (down_weight, gate_weight.T, up_weight.T)
    ]

    gathered_in, cot_now = tie(gathered_in, cotangent)
    cot_near = col_gather(cot_now)
    cot_far = [swap(cotangent, "grp", 2)] if in_pairs else []
    cot_far.append(swap(cot_near[-1], "grp", 2))
    cot_sets = [with_core(jnp.concatenate(pack, axis=0)) for pack in (cot_near, cot_far)]

    key_slice = lax.dynamic_slice_in_dim(key_matrix, key_first * head_dim, key_cols, 1)
    value_slice = lax.dynamic_slice_in_dim(value_matrix, key_first * head_dim, key_cols, 1)
    project_in = jnp.concatenate([query_weight, key_slice, value_slice], axis=1)
    projected = dot32(gathered_in, project_in)
    cosine, sine = rope_tables(positions, head_dim)
    tables = (cosine, sine, positions[None], positions[:, None], segments[None], segments[:, None])
    first = (col if in_pairs else jnp.zeros_like(col)).astype(jnp.int32).reshape(1)
    group_cols = head_share * head_dim
    score_flops = query_cols * packed_length * packed_length
    attn_low, query_low, key_low, value_low = attention_call(
        attend_kernel,
        "attend",
        first,
        [
            (projected, group_cols, 0),
            (projected, head_dim, query_heads),
            (projected, head_dim, query_heads + key_heads),
        ],
        tables,
        (group_cols, group_cols, head_dim, head_dim),
        (jnp.bfloat16, jnp.bfloat16),
        head_dim,
        (3 * score_flops, key_heads),
    )
    attn_low, down_rows = tie(attn_low, down_rows)
    act_near = low(dot_nt(cot_sets[0], down_rows))
    act_far = low(dot_nt(cot_sets[1], down_rows))
    attn_parts = blocks_of(attn_low, 0, 2) if in_pairs else [attn_low]
    hidden_res = inputs + col_scatter(lambda i: dot32(attn_parts[i], output_weight))
    normed_mid, second_back = jax.vjp(normalize, hidden_res, second_gain)

    mid_near, mid_far, act_near, act_far = square_gather(low(normed_mid), act_near, act_far)
    mid_sets = [with_core(mid_near), with_core(mid_far)]
    gate_lins = [low(dot_nt(mid, gate_rows)) for mid in mid_sets]
    act_grads = [act_near, act_far]
    acts, gate_backs, up_backs = [], [], []
    for mid, act_grad, gate_lin in zip(mid_sets, act_grads, gate_lins):
        gate32 = wide(gate_lin)
        up_lin = dot_nt(mid, up_rows)
        sig = jax.nn.sigmoid(gate32)
        acts.append(low(gate32 * sig * up_lin))
        gate_backs.append(low(wide(act_grad) * up_lin * sig * (1 + gate32 * (1 - sig))))
        up_backs.append(low(wide(act_grad) * gate32 * sig))

    def weight_sum(lefts, rights):
        return low(sum(dot_tn(left, right) for left, right in zip(lefts, rights)))

    def far_sum(product):
        pack = packed_length
        theirs = swap(low(product(1, pack, 2 * pack)), "grp", 1)
        return low(product(1, 0, pack) + wide(theirs))

    def near_sum(product):
        pack = packed_length
        return swap(low(product(0, pack, 2 * pack)), "grp", 1)

    def mid_product(i, a, b):
        return dot32(gate_backs[i][a:b], gate_rows) + dot32(up_backs[i][a:b], up_rows)

    def out_product(i, a, b):
        return dot32(acts[i][a:b], down_rows)

    down_low = weight_sum(acts, cot_sets)
    down_low, gate_backs[1], up_backs[1] = tie(down_low, gate_backs[1], up_backs[1])
    down_part = row_scatter(down_low)
    mid_from_core = near_sum(mid_product)
    mid_far_sum = far_sum(mid_product)
    mid_far_sum, gate_backs[0], up_backs[0] = tie(mid_far_sum, gate_backs[0], up_backs[0])
    mid_grad, (gate_backs[1],) = square_scatter(
        lambda first, last: mid_product(0, first, last) + wide(mid_from_core[first:last]),
        mid_far_sum,
        [gate_backs[1]],
    )
    gate_part = row_scatter(weight_sum(gate_backs, mid_sets))
    up_part = row_scatter(weight_sum(up_backs, mid_sets))

    res_from_mid, second_gain_part = second_back(mid_grad)
    res_grad = wide(cotangent) + res_from_mid
    res_low, down_part = tie(low(res_grad), down_part)
    shard_rows = jnp.concatenate(col_gather(res_low), axis=0)
    down_over_y = swap(down_part, "grp", 2)
    shard_rows, gate_part, down_over_y = tie(shard_rows, gate_part, down_over_y)
    gate_part = gate_part.T
    gate_over_y = swap(gate_part, "grp", 2)

    mixed_low = low(dot_nt(shard_rows, output_weight))
    out_low = low(dot_tn(attn_low, shard_rows))
    mixed_low, out_low = tie(mixed_low, sum_cores(out_low, core))
    out_low = sum_y(out_low, ypos)
    query_back, key_back, value_back = attention_call(
        attend_back_kernel,
        "attend_back",
        first,
        [
            (query_low, group_cols, 0),
            (key_low, head_dim, 0),
            (value_low, head_dim, 0),
            (mixed_low, group_cols, 0),
        ],
        tables,
        (group_cols, head_dim, head_dim),
        (jnp.bfloat16, jnp.bfloat16, jnp.float32, jnp.float32),
        head_dim,
        (7 * score_flops, key_heads),
    )
    query_back, out_low = tie(query_back, out_low)
    out_part, up_part = tie(out_low, up_part)
    out_part = row_gather(row_scatter(out_part))
    pair_back = jnp.concatenate([key_back, value_back], axis=1)
    back_all = jnp.concatenate([query_back, pair_back], axis=1)
    query_low_grad = low(dot_tn(gathered_in, query_back))
    pair_low_grad = low(dot_tn(gathered_in, pair_back))
    query_low_grad, pair_low_grad, *acts = tie(query_low_grad, pair_low_grad, *acts)
    query_part, pair_part, gate_over_y = tie(
        sum_cores(query_low_grad, core), sum_cores(pair_low_grad, core), gate_over_y
    )
    back_parts = blocks_of(back_all, 0, 2) if in_pairs else [back_all]
    in_grad = col_scatter(lambda i: dot_nt(back_parts[i], project_in))
    query_part, pair_part, out_part, up_part, second_gain_part, in_grad = tie(
        sum_y(query_part, ypos),
        sum_y(pair_part, ypos),
        out_part,
        up_part,
        second_gain_part,
        in_grad,
    )
    both_part = row_scatter(jnp.concatenate([query_part, pair_part], axis=1))
    up_part = up_part.T
    up_over_y = swap(up_part, "grp", 2)
    out_over_y = swap(out_part, "grp", 2)
    out_from_core = near_sum(out_product)
    layer_rows, (both_part, up_over_y) = square_scatter(
        lambda first, last: out_product(0, first, last) + wide(out_from_core[first:last]),
        far_sum(out_product),
        [both_part, up_over_y],
    )
    layer_out = hidden_res + layer_rows
    res_from_in, _ = first_back(in_grad)
    input_grad = res_grad + res_from_in

    both_part, layer_out, input_grad, out_over_y = tie(
        row_gather(both_part), layer_out, input_grad, out_over_y
    )
    size = both_part.shape[0]
    project_rows = lax.dynamic_slice_in_dim(project_in, (2 * core + ypos) * size, size, 0)
    term = jnp.sum(wide(both_part) * wide(project_rows), axis=1)
    term = butterfly(term.reshape(8, -1), ("col",)).reshape(-1)
    term = ordered(ypos, term, swap(term, "grp", 2), 0)
    first_gain_grad = ordered(core, term, swap(term, "grp", 1), 0) / first_gain
    query_part, pair_part = both_part[:, :query_cols], both_part[:, query_cols:]
    down_grad = spread_quarters(down_part, down_over_y, core, ypos, 0)
    gate_grad = spread_quarters(gate_part, gate_over_y, core, ypos, 1)
    up_grad = spread_quarters(up_part, up_over_y, core, ypos, 1)
    out_wgrad = spread_quarters(out_part, out_over_y, core, ypos, 0)
    query_wgrad = spread_quarters(query_part, swap(query_part, "grp", 2), core, ypos, 0)
    if in_pairs:
        over_x, over_y = swap(pair_part, "col", 1), swap(pair_part, "grp", 2)
        half = pair_part.shape[0] // 2
        across = jnp.concatenate(
            [swap(over_x[:half], "grp", 2), swap(over_y[half:], "col", 1)], axis=0
        )
        pair_part = ordered(ypos, pair_part, over_y, 0)
        theirs = ordered(ypos, over_x, across, 0)
        key_part = ordered(col, pair_part[:, :key_cols], theirs[:, :key_cols], 1)
        value_part = ordered(col, pair_part[:, key_cols:], theirs[:, key_cols:], 1)
        key_full = wide(ordered(core, key_part, swap(key_part, "grp", 1), 0))
        value_full = wide(ordered(core, value_part, swap(value_part, "grp", 1), 0))
    else:
        pair_part = ordered(ypos, pair_part, swap(pair_part, "grp", 2), 0)
        pair_part = ordered(core, pair_part, swap(pair_part, "grp", 1), 0)
        pair_all = wide(lax.all_gather(pair_part, "col", axis=0))
        groups = lax.axis_size("col") // head_sharing

        def spread(piece):
            piece = jnp.sum(piece.reshape(groups, head_sharing, width, key_cols), axis=1)
            return jnp.swapaxes(piece, 0, 1).reshape(width, groups * key_cols)

        key_full = spread(pair_all[..., :key_cols])
        value_full = spread(pair_all[..., key_cols:])
    axes = ("grp", "row", "col")
    second_gain_grad = butterfly(second_gain_part.reshape(8, -1), axes).reshape(-1)
    return (
        layer_out,
        input_grad,
        first_gain_grad,
        query_wgrad,
        key_full,
        value_full,
        out_wgrad,
        second_gain_grad,
        gate_grad,
        up_grad,
        down_grad,
    )


def solution(mesh):
    return jax.shard_map(
        per_device,
        mesh=mesh,
        in_specs=(
            P(("grp", "row", "col"), None),
            P(("grp", "row", "col"), None),
            P(("grp", "row")),
            P(("grp", "row")),
            P(),
            P(None, "col"),
            P(),
            P(),
            P("col", None),
            P(),
            P(None, ("row", "col")),
            P(None, ("row", "col")),
            P(("row", "col"), None),
        ),
        out_specs=(
            P(("grp", "row", "col"), None),
            P(("grp", "row", "col"), None),
            P(),
            P(None, "col"),
            P(),
            P(),
            P("col", None),
            P(),
            P(None, ("row", "col")),
            P(None, ("row", "col")),
            P(("row", "col"), None),
        ),
        check_vma=False,
    )
```

```python
import math

import jax
import jax.numpy as jnp
from jax import lax
from jax.experimental import pallas as pl
from jax.experimental.pallas import tpu as pltpu
from jax.sharding import PartitionSpec as P

QUERY_HEADS = 8
KEY_VALUE_HEADS = 4
HEAD_SIZE = 256


NORM_EPSILON = 1e-06
ROPE_BASE = 1000042.0
MASKED_SCORE = -1e30


def normalize(values, gain):
    inverse = lax.rsqrt(jnp.mean(values * values, axis=-1, keepdims=True) + NORM_EPSILON)
    return values * inverse * gain


def rope_tables(positions, head_dim):
    half_dim = head_dim // 2
    exponent = jnp.arange(half_dim, dtype=jnp.float32) * (2.0 / head_dim)
    inverse_freq = jnp.exp(-math.log(ROPE_BASE) * exponent)
    angles = positions.astype(jnp.float32)[:, None] * inverse_freq[None, :]
    return (jnp.cos(angles), jnp.sin(angles))


def turn(value, cosine, sine):
    half = value.shape[-1] // 2
    first, second = value[:, :half], value[:, half:]
    return jnp.concatenate(
        [first * cosine - second * sine, second * cosine + first * sine], axis=-1
    )


def kernel_dot(left, right, left_dim, right_dim):
    return lax.dot_general(
        left, right, (((left_dim,), (right_dim,)), ((), ())), preferred_element_type=jnp.float32
    )


def query_spans(length):
    step = length // 4
    return [(i * step, step, (i + 1) * step) for i in range(4)]


def allowed_keys(place, start, size, keys):
    pos_row, pos_col, seg_row, seg_col = place
    key_seg = seg_row[:, :keys]
    return (pos_row[:, :keys] <= pos_col[start : start + size, :]) & (
        (key_seg == 0) | (key_seg == seg_col[start : start + size, :])
    )


def stored_rows(first_ref, length):
    half = length // 2
    offsets = [first_ref[0] * half, (1 - first_ref[0]) * half]

    def rows(start, size):
        offset = pl.multiple_of(offsets[start // half] + start % half, size)
        return pl.ds(offset, size)

    return rows


def attend_kernel(
    first_ref, q_ref, k_ref, v_ref, cos_ref, sin_ref, pr_ref, pc_ref, sr_ref, sc_ref,
    out_ref, q_low_ref, k_low_ref, v_low_ref, key_ref, value_ref,
):
    length, head_dim = k_ref.shape
    rows = stored_rows(first_ref, length)
    place = (pr_ref, pc_ref, sr_ref, sc_ref)
    for start, size, _ in query_spans(length):
        span = slice(start, start + size)
        key = turn(k_ref[rows(start, size), :], cos_ref[span, :], sin_ref[span, :])
        key = key.astype(jnp.bfloat16)
        value = v_ref[rows(start, size), :].astype(jnp.bfloat16)
        key_ref[span, :] = key
        value_ref[span, :] = value
        k_low_ref[rows(start, size), :] = key
        v_low_ref[rows(start, size), :] = value
    for start, size, keys in query_spans(length):
        span = slice(start, start + size)
        allowed = allowed_keys(place, start, size, keys)
        for head in range(q_ref.shape[1] // head_dim):
            cols = slice(head * head_dim, (head + 1) * head_dim)
            query = turn(q_ref[rows(start, size), cols], cos_ref[span, :], sin_ref[span, :])
            query = query.astype(jnp.bfloat16)
            q_low_ref[rows(start, size), cols] = query
            scores = kernel_dot(query, key_ref[:keys, :], 1, 1) * head_dim**-0.5
            scores = jnp.where(allowed, scores, MASKED_SCORE)
            weights = jnp.exp(scores - jnp.max(scores, axis=1, keepdims=True))
            weights = weights * (1 / jnp.sum(weights, axis=1, keepdims=True))
            mixed = kernel_dot(weights.astype(jnp.bfloat16), value_ref[:keys, :], 1, 0)
            out_ref[rows(start, size), cols] = mixed.astype(jnp.bfloat16)


def attend_back_kernel(
    first_ref, q_ref, k_ref, v_ref, m_ref, cos_ref, sin_ref, pr_ref, pc_ref, sr_ref, sc_ref,
    q_back_ref, k_back_ref, v_back_ref, key_ref, value_ref, key_sum, value_sum,
):
    length, head_dim = k_ref.shape
    scale = head_dim**-0.5
    rows = stored_rows(first_ref, length)
    place = (pr_ref, pc_ref, sr_ref, sc_ref)
    for start, size, _ in query_spans(length):
        span = slice(start, start + size)
        key_ref[span, :] = k_ref[rows(start, size), :]
        value_ref[span, :] = v_ref[rows(start, size), :]
    key_sum[...] = jnp.zeros_like(key_sum)
    value_sum[...] = jnp.zeros_like(value_sum)
    for start, size, keys in query_spans(length):
        span = slice(start, start + size)
        allowed = allowed_keys(place, start, size, keys)
        for head in range(q_ref.shape[1] // head_dim):
            cols = slice(head * head_dim, (head + 1) * head_dim)
            query = q_ref[rows(start, size), cols]
            mixed = m_ref[rows(start, size), cols]
            scores = kernel_dot(query, key_ref[:keys, :], 1, 1) * scale
            scores = jnp.where(allowed, scores, MASKED_SCORE)
            probs = jnp.exp(scores - jnp.max(scores, axis=1, keepdims=True))
            probs = probs * (1 / jnp.sum(probs, axis=1, keepdims=True))
            value_sum[:keys, :] += kernel_dot(probs.astype(jnp.bfloat16), mixed, 0, 0)
            prob_grad = kernel_dot(mixed, value_ref[:keys, :], 1, 1)
            row_dot = jnp.sum(probs * prob_grad, axis=1, keepdims=True)
            score_low = (probs * (prob_grad - row_dot)).astype(jnp.bfloat16)
            key_sum[:keys, :] += kernel_dot(score_low, query, 0, 0)
            query_grad = kernel_dot(score_low, key_ref[:keys, :], 1, 0) * scale
            query_grad = turn(query_grad, cos_ref[span, :], -sin_ref[span, :])
            q_back_ref[rows(start, size), cols] = query_grad.astype(jnp.bfloat16)
    for start, size, _ in query_spans(length):
        span = slice(start, start + size)
        key_grad = turn(key_sum[span, :] * scale, cos_ref[span, :], -sin_ref[span, :])
        k_back_ref[rows(start, size), :] = key_grad.astype(jnp.bfloat16)
        v_back_ref[rows(start, size), :] = value_sum[span, :].astype(jnp.bfloat16)


def attention_call(kernel, name, first, heads, tables, outs, scratch, head_dim, flops):
    length = heads[0][0].shape[0]
    key_heads = flops[1]

    def head_spec(width, start):
        return pl.BlockSpec((length, width), lambda g, first_ref: (0, start + g))

    def whole_spec(shape):
        return pl.BlockSpec(shape, lambda g, first_ref: (0, 0))

    return pl.pallas_call(
        kernel,
        grid_spec=pltpu.PrefetchScalarGridSpec(
            num_scalar_prefetch=1,
            grid=(key_heads,),
            in_specs=[head_spec(width, start) for _, width, start in heads]
            + [whole_spec(table.shape) for table in tables],
            out_specs=[head_spec(width, 0) for width in outs],
            scratch_shapes=[pltpu.VMEM((length, head_dim), kind) for kind in scratch],
        ),
        out_shape=[
            jax.ShapeDtypeStruct((length, width * key_heads), jnp.bfloat16) for width in outs
        ],
        cost_estimate=pl.CostEstimate(
            flops=flops[0], bytes_accessed=flops[0] // 200, transcendentals=length * length
        ),
        name=name,
    )(first, *[array for array, _, _ in heads], *tables)


def swap(value, axis, bit):
    count = lax.axis_size(axis)
    return lax.ppermute(value, axis, [(i, i ^ bit) for i in range(count)])


def shift(value, axis, step):
    count = lax.axis_size(axis)
    return lax.ppermute(value, axis, [(i, (i + step) % count) for i in range(count)])


def tie(*values):
    return lax.optimization_barrier(values)


def ordered(first_when_zero, mine, theirs, dim):
    keep = first_when_zero == 0
    return jnp.concatenate(
        [jnp.where(keep, mine, theirs), jnp.where(keep, theirs, mine)], axis=dim
    )


def dot32(left, right):
    return jnp.dot(left, right, preferred_element_type=jnp.float32)


def dot_nt(left, right):
    return jnp.einsum("td,fd->tf", left, right, preferred_element_type=jnp.float32)


def dot_tn(left, right):
    return jnp.einsum("td,tf->df", left, right, preferred_element_type=jnp.float32)


def low(value):
    return value.astype(jnp.bfloat16)


def wide(value):
    return value.astype(jnp.float32)


def col_gather(mine):
    if lax.axis_size("col") == 2:
        return [mine, swap(mine, "col", 1)]
    return [lax.all_gather(mine, "col", axis=0, tiled=True)]


def col_scatter(product):
    if lax.axis_size("col") == 2:
        theirs = swap(low(product(1)), "col", 1)
        return product(0) + wide(theirs)
    return wide(lax.psum_scatter(low(product(0)), "col", scatter_dimension=0, tiled=True))


def blocks_of(value, dim, count):
    size = value.shape[dim] // count
    return [lax.slice_in_dim(value, i * size, (i + 1) * size, axis=dim) for i in range(count)]


def square_gather(mine, beside_first, beside_second):
    if lax.axis_size("col") == 2:
        over_x, over_y, beside_first = tie(
            swap(mine, "col", 1), swap(mine, "grp", 2), beside_first
        )
        half = mine.shape[0] // 2
        across_first, across_second, beside_second = tie(
            swap(over_x[:half], "grp", 2), swap(over_y[half:], "col", 1), beside_second
        )
        near = jnp.concatenate([mine, over_x], axis=0)
        far = jnp.concatenate([over_y, across_first, across_second], axis=0)
        return near, far, beside_first, beside_second
    near = lax.all_gather(mine, "col", axis=0, tiled=True)
    return near, swap(near, "grp", 2), beside_first, beside_second


def with_core(pack):
    return jnp.concatenate([pack, swap(pack, "grp", 1)], axis=0)


def square_scatter(near, far, later):
    size = far.shape[0]
    if lax.axis_size("col") == 2:
        half, part = size // 2, size // 4
        across_first = swap(far[half : half + part], "grp", 2)
        across_second = swap(far[half + part :], "col", 1)
        rest = jnp.zeros_like(across_first)
        to_y = low(wide(far[:half]) + wide(jnp.concatenate([rest, across_second], axis=0)))
        to_x = low(near(half, size) + wide(jnp.concatenate([across_first, rest], axis=0)))
        to_y, to_x, *later = tie(to_y, to_x, *later)
        from_y = swap(to_y, "grp", 2)
        from_x = swap(to_x, "col", 1)
        return near(0, half) + wide(from_x) + wide(from_y), later
    total = low(near(0, size) + wide(swap(far, "grp", 2)))
    return wide(lax.psum_scatter(total, "col", scatter_dimension=0, tiled=True)), later


def butterfly(value, axes):
    for axis in axes:
        bit = 1
        while bit < lax.axis_size(axis):
            value = value + swap(value, axis, bit)
            bit *= 2
    return value


def half_rows(value, bit):
    size = value.shape[0] // 2
    return lax.dynamic_slice_in_dim(value, bit * size, size, 0)


def row_gather(value):
    return lax.all_gather(value, "row", axis=0, tiled=True)


def row_scatter(value):
    return lax.psum_scatter(value, "row", scatter_dimension=0, tiled=True)


def sum_cores(value, core):
    return low(wide(half_rows(value, core)) + wide(swap(half_rows(value, 1 - core), "grp", 1)))


def sum_y(part, ypos):
    part = low(wide(half_rows(part, ypos)) + wide(swap(half_rows(part, 1 - ypos), "grp", 2)))
    return part


def spread_y(part, ypos):
    return ordered(ypos, part, swap(part, "grp", 2), 0)


def spread_core(part, core):
    return ordered(core, part, swap(part, "grp", 1), 0)


def own_quarter(weight, core, ypos):
    size = weight.shape[0] // 4
    return lax.dynamic_slice_in_dim(weight, (2 * core + ypos) * size, size, 0)


def spread_quarters(part, over_y, core, ypos, dim):
    half = ordered(ypos, part, over_y, dim)
    return wide(ordered(core, half, swap(half, "grp", 1), dim))


def per_device(
    tokens,
    cotangent,
    segments,
    positions,
    first_gain,
    query_weight,
    key_matrix,
    value_matrix,
    output_weight,
    second_gain,
    gate_weight,
    up_weight,
    down_weight,
):
    head_dim = HEAD_SIZE
    query_heads = query_weight.shape[1] // head_dim
    heads_per_group = QUERY_HEADS // KEY_VALUE_HEADS
    key_heads = max(1, query_heads // heads_per_group)
    head_share = query_heads // key_heads
    head_sharing = max(1, heads_per_group // query_heads)
    col = lax.axis_index("col")
    key_first = col * query_heads // heads_per_group
    query_cols = query_heads * head_dim
    key_cols = key_heads * head_dim
    rows, width = tokens.shape
    grp, zpos = lax.axis_index("grp"), lax.axis_index("row")
    core, ypos = lax.rem(grp, 2), lax.div(grp, 2)
    in_pairs = lax.axis_size("col") == 2

    inputs = wide(tokens)
    normalized_input, first_back = jax.vjp(normalize, inputs, first_gain)
    gathered_in = jnp.concatenate(col_gather(low(normalized_input)), axis=0)
    packed_length = gathered_in.shape[0]

    down_rows, gate_rows, up_rows = [
        row_gather(own_quarter(weight, core, ypos))
        for weight in (down_weight, gate_weight.T, up_weight.T)
    ]

    gathered_in, cot_now = tie(gathered_in, cotangent)
    cot_near = col_gather(cot_now)
    cot_far = [swap(cotangent, "grp", 2)] if in_pairs else []
    cot_far.append(swap(cot_near[-1], "grp", 2))
    cot_sets = [with_core(jnp.concatenate(pack, axis=0)) for pack in (cot_near, cot_far)]

    key_slice = lax.dynamic_slice_in_dim(key_matrix, key_first * head_dim, key_cols, 1)
    value_slice = lax.dynamic_slice_in_dim(value_matrix, key_first * head_dim, key_cols, 1)
    project_in = jnp.concatenate([query_weight, key_slice, value_slice], axis=1)
    projected = dot32(gathered_in, project_in)
    cosine, sine = rope_tables(positions, head_dim)
    tables = (cosine, sine, positions[None], positions[:, None], segments[None], segments[:, None])
    first = (col if in_pairs else jnp.zeros_like(col)).astype(jnp.int32).reshape(1)
    group_cols = head_share * head_dim
    score_flops = query_cols * packed_length * packed_length
    attn_low, query_low, key_low, value_low = attention_call(
        attend_kernel,
        "attend",
        first,
        [
            (projected, group_cols, 0),
            (projected, head_dim, query_heads),
            (projected, head_dim, query_heads + key_heads),
        ],
        tables,
        (group_cols, group_cols, head_dim, head_dim),
        (jnp.bfloat16, jnp.bfloat16),
        head_dim,
        (3 * score_flops, key_heads),
    )
    attn_low, down_rows = tie(attn_low, down_rows)
    act_near = low(dot_nt(cot_sets[0], down_rows))
    act_far = low(dot_nt(cot_sets[1], down_rows))
    attn_parts = blocks_of(attn_low, 0, 2) if in_pairs else [attn_low]
    hidden_res = inputs + col_scatter(lambda i: dot32(attn_parts[i], output_weight))
    normed_mid, second_back = jax.vjp(normalize, hidden_res, second_gain)

    mid_near, mid_far, act_near, act_far = square_gather(low(normed_mid), act_near, act_far)
    mid_sets = [with_core(mid_near), with_core(mid_far)]
    gate_lins = [low(dot_nt(mid, gate_rows)) for mid in mid_sets]
    act_grads = [act_near, act_far]
    acts, gate_backs, up_backs = [], [], []
    for mid, act_grad, gate_lin in zip(mid_sets, act_grads, gate_lins):
        gate32 = wide(gate_lin)
        up_lin = dot_nt(mid, up_rows)
        sig = jax.nn.sigmoid(gate32)
        acts.append(low(gate32 * sig * up_lin))
        gate_backs.append(low(wide(act_grad) * up_lin * sig * (1 + gate32 * (1 - sig))))
        up_backs.append(low(wide(act_grad) * gate32 * sig))

    def weight_sum(lefts, rights):
        return low(sum(dot_tn(left, right) for left, right in zip(lefts, rights)))

    def far_sum(product):
        pack = packed_length
        theirs = swap(low(product(1, pack, 2 * pack)), "grp", 1)
        return low(product(1, 0, pack) + wide(theirs))

    def near_sum(product):
        pack = packed_length
        return swap(low(product(0, pack, 2 * pack)), "grp", 1)

    def mid_product(i, a, b):
        return dot32(gate_backs[i][a:b], gate_rows) + dot32(up_backs[i][a:b], up_rows)

    def out_product(i, a, b):
        return dot32(acts[i][a:b], down_rows)

    down_low = weight_sum(acts, cot_sets)
    down_low, gate_backs[1], up_backs[1] = tie(down_low, gate_backs[1], up_backs[1])
    down_part = row_scatter(down_low)
    mid_from_core = near_sum(mid_product)
    mid_far_sum = far_sum(mid_product)
    mid_far_sum, gate_backs[0], up_backs[0] = tie(mid_far_sum, gate_backs[0], up_backs[0])
    mid_grad, (gate_backs[1],) = square_scatter(
        lambda first, last: mid_product(0, first, last) + wide(mid_from_core[first:last]),
        mid_far_sum,
        [gate_backs[1]],
    )
    gate_part = row_scatter(weight_sum(gate_backs, mid_sets))
    res_from_mid, second_gain_part = second_back(mid_grad)
    res_grad = wide(cotangent) + res_from_mid
    res_low, down_part, second_gain_part, *up_backs = tie(
        low(res_grad), down_part, second_gain_part, *up_backs
    )
    up_part = row_scatter(weight_sum(up_backs, mid_sets))
    second_gain_part = butterfly(second_gain_part.reshape(8, -1), ("grp", "row"))
    shard_rows = jnp.concatenate(col_gather(res_low), axis=0)
    down_over_y = swap(down_part, "grp", 2)
    shard_rows, gate_part, down_over_y, second_gain_part = tie(
        shard_rows, gate_part, down_over_y, second_gain_part
    )
    gate_part = gate_part.T
    gate_over_y = swap(gate_part, "grp", 2)

    mixed_low = low(dot_nt(shard_rows, output_weight))
    out_low = low(dot_tn(attn_low, shard_rows))
    mixed_low, out_low = tie(mixed_low, sum_cores(out_low, core))
    out_low = sum_y(out_low, ypos)
    query_back, key_back, value_back = attention_call(
        attend_back_kernel,
        "attend_back",
        first,
        [
            (query_low, group_cols, 0),
            (key_low, head_dim, 0),
            (value_low, head_dim, 0),
            (mixed_low, group_cols, 0),
        ],
        tables,
        (group_cols, head_dim, head_dim),
        (jnp.bfloat16, jnp.bfloat16, jnp.float32, jnp.float32),
        head_dim,
        (7 * score_flops, key_heads),
    )
    query_back, out_low = tie(query_back, out_low)
    out_part, up_part = tie(out_low, up_part)
    out_part = row_gather(row_scatter(out_part))
    pair_back = jnp.concatenate([key_back, value_back], axis=1)
    back_all = jnp.concatenate([query_back, pair_back], axis=1)
    query_low_grad = low(dot_tn(gathered_in, query_back))
    pair_low_grad = low(dot_tn(gathered_in, pair_back))
    query_part, pair_part, gate_over_y, *acts = tie(
        sum_cores(query_low_grad, core), sum_cores(pair_low_grad, core), gate_over_y, *acts
    )
    back_parts = blocks_of(back_all, 0, 2) if in_pairs else [back_all]
    in_grad = col_scatter(lambda i: dot_nt(back_parts[i], project_in))
    query_part, pair_part, out_part, up_part, in_grad = tie(
        sum_y(query_part, ypos), sum_y(pair_part, ypos), out_part, up_part, in_grad
    )
    both_part = row_scatter(jnp.concatenate([query_part, pair_part], axis=1))
    up_part = up_part.T
    up_over_y = swap(up_part, "grp", 2)
    out_over_y = swap(out_part, "grp", 2)
    out_from_core = near_sum(out_product)
    out_far = far_sum(out_product)

    def out_near(first, last):
        return out_product(0, first, last) + wide(out_from_core[first:last])

    if in_pairs:
        mid_row = packed_length // 2
        across = swap(out_far[mid_row:], "col", 1)
        out_far = low(wide(out_far[:mid_row]) + wide(across))
    both_part, up_over_y, out_over_y, out_far = tie(both_part, up_over_y, out_over_y, out_far)
    from_y = wide(swap(out_far, "grp", 2))
    if in_pairs:
        from_x = wide(swap(low(out_near(mid_row, packed_length)), "col", 1))
        layer_rows = out_near(0, mid_row) + from_x + from_y
    else:
        layer_rows = col_scatter(lambda i: out_near(0, packed_length) + from_y)
    layer_out = hidden_res + layer_rows
    res_from_in, _ = first_back(in_grad)
    input_grad = res_grad + res_from_in

    both_part, layer_out, input_grad = tie(row_gather(both_part), layer_out, input_grad)
    size = both_part.shape[0]
    project_rows = lax.dynamic_slice_in_dim(project_in, (2 * core + ypos) * size, size, 0)
    term = jnp.sum(wide(both_part) * wide(project_rows), axis=1)
    term = butterfly(term.reshape(8, -1), ("col",)).reshape(-1)
    term = ordered(ypos, term, swap(term, "grp", 2), 0)
    first_gain_grad = ordered(core, term, swap(term, "grp", 1), 0) / first_gain
    query_part, pair_part = both_part[:, :query_cols], both_part[:, query_cols:]
    down_grad = spread_quarters(down_part, down_over_y, core, ypos, 0)
    gate_grad = spread_quarters(gate_part, gate_over_y, core, ypos, 1)
    up_grad = spread_quarters(up_part, up_over_y, core, ypos, 1)
    out_wgrad = spread_quarters(out_part, out_over_y, core, ypos, 0)
    query_wgrad = spread_quarters(query_part, swap(query_part, "grp", 2), core, ypos, 0)
    if in_pairs:
        over_x, over_y = swap(pair_part, "col", 1), swap(pair_part, "grp", 2)
        half = pair_part.shape[0] // 2
        across = jnp.concatenate(
            [swap(over_x[:half], "grp", 2), swap(over_y[half:], "col", 1)], axis=0
        )
        pair_part = ordered(ypos, pair_part, over_y, 0)
        theirs = ordered(ypos, over_x, across, 0)
        key_part = ordered(col, pair_part[:, :key_cols], theirs[:, :key_cols], 1)
        value_part = ordered(col, pair_part[:, key_cols:], theirs[:, key_cols:], 1)
        key_full = wide(ordered(core, key_part, swap(key_part, "grp", 1), 0))
        value_full = wide(ordered(core, value_part, swap(value_part, "grp", 1), 0))
    else:
        pair_part = ordered(ypos, pair_part, swap(pair_part, "grp", 2), 0)
        pair_part = ordered(core, pair_part, swap(pair_part, "grp", 1), 0)
        pair_all = wide(lax.all_gather(pair_part, "col", axis=0))
        groups = lax.axis_size("col") // head_sharing

        def spread(piece):
            piece = jnp.sum(piece.reshape(groups, head_sharing, width, key_cols), axis=1)
            return jnp.swapaxes(piece, 0, 1).reshape(width, groups * key_cols)

        key_full = spread(pair_all[..., :key_cols])
        value_full = spread(pair_all[..., key_cols:])
    second_gain_grad = butterfly(second_gain_part, ("col",)).reshape(-1)
    return (
        layer_out,
        input_grad,
        first_gain_grad,
        query_wgrad,
        key_full,
        value_full,
        out_wgrad,
        second_gain_grad,
        gate_grad,
        up_grad,
        down_grad,
    )


def solution(mesh):
    return jax.shard_map(
        per_device,
        mesh=mesh,
        in_specs=(
            P(("grp", "row", "col"), None),
            P(("grp", "row", "col"), None),
            P(("grp", "row")),
            P(("grp", "row")),
            P(),
            P(None, "col"),
            P(),
            P(),
            P("col", None),
            P(),
            P(None, ("row", "col")),
            P(None, ("row", "col")),
            P(("row", "col"), None),
        ),
        out_specs=(
            P(("grp", "row", "col"), None),
            P(("grp", "row", "col"), None),
            P(),
            P(None, "col"),
            P(),
            P(),
            P("col", None),
            P(),
            P(None, ("row", "col")),
            P(None, ("row", "col")),
            P(("row", "col"), None),
        ),
        check_vma=False,
    )
```

```python
import math

import jax
import jax.numpy as jnp
from jax import lax
from jax.experimental import pallas as pl
from jax.experimental.pallas import tpu as pltpu
from jax.sharding import PartitionSpec as P

QUERY_HEADS = 8
KEY_VALUE_HEADS = 4
HEAD_SIZE = 256


NORM_EPSILON = 1e-06
ROPE_BASE = 1000042.0
MASKED_SCORE = -1e30


def normalize(values, gain):
    inverse = lax.rsqrt(jnp.mean(values * values, axis=-1, keepdims=True) + NORM_EPSILON)
    return values * inverse * gain


def rope_tables(positions, head_dim):
    half_dim = head_dim // 2
    exponent = jnp.arange(half_dim, dtype=jnp.float32) * (2.0 / head_dim)
    inverse_freq = jnp.exp(-math.log(ROPE_BASE) * exponent)
    angles = positions.astype(jnp.float32)[:, None] * inverse_freq[None, :]
    return (jnp.cos(angles), jnp.sin(angles))


def turn(value, cosine, sine):
    half = value.shape[-1] // 2
    first, second = value[:, :half], value[:, half:]
    return jnp.concatenate(
        [first * cosine - second * sine, second * cosine + first * sine], axis=-1
    )


def kernel_dot(left, right, left_dim, right_dim):
    return lax.dot_general(
        left, right, (((left_dim,), (right_dim,)), ((), ())), preferred_element_type=jnp.float32
    )


def query_spans(length):
    step = length // 4
    return [(i * step, step, (i + 1) * step) for i in range(4)]


def allowed_keys(place, start, size, keys):
    pos_row, pos_col, seg_row, seg_col = place
    key_seg = seg_row[:, :keys]
    return (pos_row[:, :keys] <= pos_col[start : start + size, :]) & (
        (key_seg == 0) | (key_seg == seg_col[start : start + size, :])
    )


def stored_rows(first_ref, length):
    half = length // 2
    offsets = [first_ref[0] * half, (1 - first_ref[0]) * half]

    def rows(start, size):
        offset = pl.multiple_of(offsets[start // half] + start % half, size)
        return pl.ds(offset, size)

    return rows


def attend_kernel(
    first_ref, q_ref, k_ref, v_ref, cos_ref, sin_ref, pr_ref, pc_ref, sr_ref, sc_ref,
    out_ref, q_low_ref, k_low_ref, v_low_ref, key_ref, value_ref,
):
    length, head_dim = k_ref.shape
    rows = stored_rows(first_ref, length)
    place = (pr_ref, pc_ref, sr_ref, sc_ref)
    for start, size, _ in query_spans(length):
        span = slice(start, start + size)
        key = turn(k_ref[rows(start, size), :], cos_ref[span, :], sin_ref[span, :])
        key = key.astype(jnp.bfloat16)
        value = v_ref[rows(start, size), :].astype(jnp.bfloat16)
        key_ref[span, :] = key
        value_ref[span, :] = value
        k_low_ref[rows(start, size), :] = key
        v_low_ref[rows(start, size), :] = value
    for start, size, keys in query_spans(length):
        span = slice(start, start + size)
        allowed = allowed_keys(place, start, size, keys)
        for head in range(q_ref.shape[1] // head_dim):
            cols = slice(head * head_dim, (head + 1) * head_dim)
            query = turn(q_ref[rows(start, size), cols], cos_ref[span, :], sin_ref[span, :])
            query = query.astype(jnp.bfloat16)
            q_low_ref[rows(start, size), cols] = query
            scores = kernel_dot(query, key_ref[:keys, :], 1, 1) * head_dim**-0.5
            scores = jnp.where(allowed, scores, MASKED_SCORE)
            weights = jnp.exp(scores - jnp.max(scores, axis=1, keepdims=True))
            weights = weights * (1 / jnp.sum(weights, axis=1, keepdims=True))
            mixed = kernel_dot(weights.astype(jnp.bfloat16), value_ref[:keys, :], 1, 0)
            out_ref[rows(start, size), cols] = mixed.astype(jnp.bfloat16)


def attend_back_kernel(
    first_ref, q_ref, k_ref, v_ref, m_ref, cos_ref, sin_ref, pr_ref, pc_ref, sr_ref, sc_ref,
    q_back_ref, k_back_ref, v_back_ref, key_ref, value_ref, key_sum, value_sum,
):
    length, head_dim = k_ref.shape
    scale = head_dim**-0.5
    rows = stored_rows(first_ref, length)
    place = (pr_ref, pc_ref, sr_ref, sc_ref)
    for start, size, _ in query_spans(length):
        span = slice(start, start + size)
        key_ref[span, :] = k_ref[rows(start, size), :]
        value_ref[span, :] = v_ref[rows(start, size), :]
    key_sum[...] = jnp.zeros_like(key_sum)
    value_sum[...] = jnp.zeros_like(value_sum)
    for start, size, keys in query_spans(length):
        span = slice(start, start + size)
        allowed = allowed_keys(place, start, size, keys)
        for head in range(q_ref.shape[1] // head_dim):
            cols = slice(head * head_dim, (head + 1) * head_dim)
            query = q_ref[rows(start, size), cols]
            mixed = m_ref[rows(start, size), cols]
            scores = kernel_dot(query, key_ref[:keys, :], 1, 1) * scale
            scores = jnp.where(allowed, scores, MASKED_SCORE)
            probs = jnp.exp(scores - jnp.max(scores, axis=1, keepdims=True))
            probs = probs * (1 / jnp.sum(probs, axis=1, keepdims=True))
            value_sum[:keys, :] += kernel_dot(probs.astype(jnp.bfloat16), mixed, 0, 0)
            prob_grad = kernel_dot(mixed, value_ref[:keys, :], 1, 1)
            row_dot = jnp.sum(probs * prob_grad, axis=1, keepdims=True)
            score_low = (probs * (prob_grad - row_dot)).astype(jnp.bfloat16)
            key_sum[:keys, :] += kernel_dot(score_low, query, 0, 0)
            query_grad = kernel_dot(score_low, key_ref[:keys, :], 1, 0) * scale
            query_grad = turn(query_grad, cos_ref[span, :], -sin_ref[span, :])
            q_back_ref[rows(start, size), cols] = query_grad.astype(jnp.bfloat16)
    for start, size, _ in query_spans(length):
        span = slice(start, start + size)
        key_grad = turn(key_sum[span, :] * scale, cos_ref[span, :], -sin_ref[span, :])
        k_back_ref[rows(start, size), :] = key_grad.astype(jnp.bfloat16)
        v_back_ref[rows(start, size), :] = value_sum[span, :].astype(jnp.bfloat16)


def attention_call(kernel, name, first, heads, tables, outs, scratch, head_dim, flops):
    length = heads[0][0].shape[0]
    key_heads = flops[1]

    def head_spec(width, start):
        return pl.BlockSpec((length, width), lambda g, first_ref: (0, start + g))

    def whole_spec(shape):
        return pl.BlockSpec(shape, lambda g, first_ref: (0, 0))

    return pl.pallas_call(
        kernel,
        grid_spec=pltpu.PrefetchScalarGridSpec(
            num_scalar_prefetch=1,
            grid=(key_heads,),
            in_specs=[head_spec(width, start) for _, width, start in heads]
            + [whole_spec(table.shape) for table in tables],
            out_specs=[head_spec(width, 0) for width in outs],
            scratch_shapes=[pltpu.VMEM((length, head_dim), kind) for kind in scratch],
        ),
        out_shape=[
            jax.ShapeDtypeStruct((length, width * key_heads), jnp.bfloat16) for width in outs
        ],
        cost_estimate=pl.CostEstimate(
            flops=flops[0], bytes_accessed=flops[0] // 200, transcendentals=length * length
        ),
        name=name,
    )(first, *[array for array, _, _ in heads], *tables)


def swap(value, axis, bit):
    count = lax.axis_size(axis)
    return lax.ppermute(value, axis, [(i, i ^ bit) for i in range(count)])


def shift(value, axis, step):
    count = lax.axis_size(axis)
    return lax.ppermute(value, axis, [(i, (i + step) % count) for i in range(count)])


def tie(*values):
    return lax.optimization_barrier(values)


def ordered(first_when_zero, mine, theirs, dim):
    keep = first_when_zero == 0
    return jnp.concatenate(
        [jnp.where(keep, mine, theirs), jnp.where(keep, theirs, mine)], axis=dim
    )


def dot32(left, right):
    return jnp.dot(left, right, preferred_element_type=jnp.float32)


def dot_nt(left, right):
    return jnp.einsum("td,fd->tf", left, right, preferred_element_type=jnp.float32)


def dot_tn(left, right):
    return jnp.einsum("td,tf->df", left, right, preferred_element_type=jnp.float32)


def low(value):
    return value.astype(jnp.bfloat16)


def wide(value):
    return value.astype(jnp.float32)


def col_gather(mine):
    if lax.axis_size("col") == 2:
        return [mine, swap(mine, "col", 1)]
    return [lax.all_gather(mine, "col", axis=0, tiled=True)]


def col_scatter(product):
    if lax.axis_size("col") == 2:
        theirs = swap(low(product(1)), "col", 1)
        return product(0) + wide(theirs)
    return wide(lax.psum_scatter(low(product(0)), "col", scatter_dimension=0, tiled=True))


def blocks_of(value, dim, count):
    size = value.shape[dim] // count
    return [lax.slice_in_dim(value, i * size, (i + 1) * size, axis=dim) for i in range(count)]


def square_gather(mine, beside_first, beside_second):
    if lax.axis_size("col") == 2:
        over_x, over_y, beside_first = tie(
            swap(mine, "col", 1), swap(mine, "grp", 2), beside_first
        )
        half = mine.shape[0] // 2
        across_first, across_second, beside_second = tie(
            swap(over_x[:half], "grp", 2), swap(over_y[half:], "col", 1), beside_second
        )
        near = jnp.concatenate([mine, over_x], axis=0)
        far = jnp.concatenate([over_y, across_first, across_second], axis=0)
        return near, far, beside_first, beside_second
    near = lax.all_gather(mine, "col", axis=0, tiled=True)
    return near, swap(near, "grp", 2), beside_first, beside_second


def with_core(pack):
    return jnp.concatenate([pack, swap(pack, "grp", 1)], axis=0)


def square_scatter(near, far, later):
    size = far.shape[0]
    if lax.axis_size("col") == 2:
        half, part = size // 2, size // 4
        across_first = swap(far[half : half + part], "grp", 2)
        across_second = swap(far[half + part :], "col", 1)
        rest = jnp.zeros_like(across_first)
        to_y = low(wide(far[:half]) + wide(jnp.concatenate([rest, across_second], axis=0)))
        to_x = low(near(half, size) + wide(jnp.concatenate([across_first, rest], axis=0)))
        to_y, to_x, *later = tie(to_y, to_x, *later)
        from_y = swap(to_y, "grp", 2)
        from_x = swap(to_x, "col", 1)
        return near(0, half) + wide(from_x) + wide(from_y), later
    total = low(near(0, size) + wide(swap(far, "grp", 2)))
    return wide(lax.psum_scatter(total, "col", scatter_dimension=0, tiled=True)), later


def butterfly(value, axes):
    for axis in axes:
        bit = 1
        while bit < lax.axis_size(axis):
            value = value + swap(value, axis, bit)
            bit *= 2
    return value


def half_rows(value, bit):
    size = value.shape[0] // 2
    return lax.dynamic_slice_in_dim(value, bit * size, size, 0)


def row_gather(value):
    return lax.all_gather(value, "row", axis=0, tiled=True)


def row_scatter(value):
    return lax.psum_scatter(value, "row", scatter_dimension=0, tiled=True)


def sum_cores(value, core):
    return low(wide(half_rows(value, core)) + wide(swap(half_rows(value, 1 - core), "grp", 1)))


def sum_y(part, ypos):
    part = low(wide(half_rows(part, ypos)) + wide(swap(half_rows(part, 1 - ypos), "grp", 2)))
    return part


def spread_y(part, ypos):
    return ordered(ypos, part, swap(part, "grp", 2), 0)


def spread_core(part, core):
    return ordered(core, part, swap(part, "grp", 1), 0)


def own_quarter(weight, core, ypos):
    size = weight.shape[0] // 4
    return lax.dynamic_slice_in_dim(weight, (2 * core + ypos) * size, size, 0)


def spread_quarters(part, over_y, core, ypos, dim):
    half = ordered(ypos, part, over_y, dim)
    return wide(ordered(core, half, swap(half, "grp", 1), dim))


def per_device(
    tokens,
    cotangent,
    segments,
    positions,
    first_gain,
    query_weight,
    key_matrix,
    value_matrix,
    output_weight,
    second_gain,
    gate_weight,
    up_weight,
    down_weight,
):
    head_dim = HEAD_SIZE
    query_heads = query_weight.shape[1] // head_dim
    heads_per_group = QUERY_HEADS // KEY_VALUE_HEADS
    key_heads = max(1, query_heads // heads_per_group)
    head_share = query_heads // key_heads
    head_sharing = max(1, heads_per_group // query_heads)
    col = lax.axis_index("col")
    key_first = col * query_heads // heads_per_group
    query_cols = query_heads * head_dim
    key_cols = key_heads * head_dim
    rows, width = tokens.shape
    grp, zpos = lax.axis_index("grp"), lax.axis_index("row")
    core, ypos = lax.rem(grp, 2), lax.div(grp, 2)
    in_pairs = lax.axis_size("col") == 2

    inputs = wide(tokens)
    normalized_input, first_back = jax.vjp(normalize, inputs, first_gain)
    gathered_in = jnp.concatenate(col_gather(low(normalized_input)), axis=0)
    packed_length = gathered_in.shape[0]

    down_rows, gate_rows, up_rows = [
        row_gather(own_quarter(weight, core, ypos))
        for weight in (down_weight, gate_weight.T, up_weight.T)
    ]

    gathered_in, cot_now = tie(gathered_in, cotangent)
    cot_near = col_gather(cot_now)
    cot_far = [swap(cotangent, "grp", 2)] if in_pairs else []
    cot_far.append(swap(cot_near[-1], "grp", 2))
    cot_sets = [with_core(jnp.concatenate(pack, axis=0)) for pack in (cot_near, cot_far)]

    key_slice = lax.dynamic_slice_in_dim(key_matrix, key_first * head_dim, key_cols, 1)
    value_slice = lax.dynamic_slice_in_dim(value_matrix, key_first * head_dim, key_cols, 1)
    project_in = jnp.concatenate([query_weight, key_slice, value_slice], axis=1)
    projected = dot32(gathered_in, project_in)
    cosine, sine = rope_tables(positions, head_dim)
    tables = (cosine, sine, positions[None], positions[:, None], segments[None], segments[:, None])
    first = (col if in_pairs else jnp.zeros_like(col)).astype(jnp.int32).reshape(1)
    group_cols = head_share * head_dim
    score_flops = query_cols * packed_length * packed_length
    attn_low, query_low, key_low, value_low = attention_call(
        attend_kernel,
        "attend",
        first,
        [
            (projected, group_cols, 0),
            (projected, head_dim, query_heads),
            (projected, head_dim, query_heads + key_heads),
        ],
        tables,
        (group_cols, group_cols, head_dim, head_dim),
        (jnp.bfloat16, jnp.bfloat16),
        head_dim,
        (3 * score_flops, key_heads),
    )
    attn_low, down_rows = tie(attn_low, down_rows)
    act_near = low(dot_nt(cot_sets[0], down_rows))
    act_far = low(dot_nt(cot_sets[1], down_rows))
    attn_parts = blocks_of(attn_low, 0, 2) if in_pairs else [attn_low]
    hidden_res = inputs + col_scatter(lambda i: dot32(attn_parts[i], output_weight))
    normed_mid, second_back = jax.vjp(normalize, hidden_res, second_gain)

    mid_near, mid_far, act_near, act_far = square_gather(low(normed_mid), act_near, act_far)
    mid_sets = [with_core(mid_near), with_core(mid_far)]
    gate_lins = [low(dot_nt(mid, gate_rows)) for mid in mid_sets]
    act_grads = [act_near, act_far]
    acts, gate_backs, up_backs = [], [], []
    for mid, act_grad, gate_lin in zip(mid_sets, act_grads, gate_lins):
        gate32 = wide(gate_lin)
        up_lin = dot_nt(mid, up_rows)
        sig = jax.nn.sigmoid(gate32)
        acts.append(low(gate32 * sig * up_lin))
        gate_backs.append(low(wide(act_grad) * up_lin * sig * (1 + gate32 * (1 - sig))))
        up_backs.append(low(wide(act_grad) * gate32 * sig))

    def weight_sum(lefts, rights):
        return low(sum(dot_tn(left, right) for left, right in zip(lefts, rights)))

    def far_sum(product):
        pack = packed_length
        theirs = swap(low(product(1, pack, 2 * pack)), "grp", 1)
        return low(product(1, 0, pack) + wide(theirs))

    def near_sum(product):
        pack = packed_length
        return swap(low(product(0, pack, 2 * pack)), "grp", 1)

    def mid_product(i, a, b):
        return dot32(gate_backs[i][a:b], gate_rows) + dot32(up_backs[i][a:b], up_rows)

    def out_product(i, a, b):
        return dot32(acts[i][a:b], down_rows)

    down_low = weight_sum(acts, cot_sets)
    down_low, gate_backs[1], up_backs[1] = tie(down_low, gate_backs[1], up_backs[1])
    down_part = row_scatter(down_low)
    mid_from_core = near_sum(mid_product)
    mid_far_sum = far_sum(mid_product)
    mid_far_sum, gate_backs[0], up_backs[0] = tie(mid_far_sum, gate_backs[0], up_backs[0])
    mid_grad, (gate_backs[1],) = square_scatter(
        lambda first, last: mid_product(0, first, last) + wide(mid_from_core[first:last]),
        mid_far_sum,
        [gate_backs[1]],
    )
    gate_part = row_scatter(weight_sum(gate_backs, mid_sets))
    res_from_mid, second_gain_part = second_back(mid_grad)
    res_grad = wide(cotangent) + res_from_mid
    res_low, down_part, second_gain_part, *up_backs = tie(
        low(res_grad), down_part, second_gain_part, *up_backs
    )
    up_part = row_scatter(weight_sum(up_backs, mid_sets))
    second_gain_part = butterfly(second_gain_part.reshape(8, -1), ("grp", "row"))
    shard_rows = jnp.concatenate(col_gather(res_low), axis=0)
    down_over_y = swap(down_part, "grp", 2)
    shard_rows, gate_part, down_over_y, second_gain_part = tie(
        shard_rows, gate_part, down_over_y, second_gain_part
    )
    gate_part = gate_part.T
    gate_over_y = swap(gate_part, "grp", 2)

    mixed_low = low(dot_nt(shard_rows, output_weight))
    out_low = low(dot_tn(attn_low, shard_rows))
    mixed_low, out_low = tie(mixed_low, sum_cores(out_low, core))
    out_low = sum_y(out_low, ypos)
    query_back, key_back, value_back = attention_call(
        attend_back_kernel,
        "attend_back",
        first,
        [
            (query_low, group_cols, 0),
            (key_low, head_dim, 0),
            (value_low, head_dim, 0),
            (mixed_low, group_cols, 0),
        ],
        tables,
        (group_cols, head_dim, head_dim),
        (jnp.bfloat16, jnp.bfloat16, jnp.float32, jnp.float32),
        head_dim,
        (7 * score_flops, key_heads),
    )
    query_back, out_low = tie(query_back, out_low)
    out_part, up_part = tie(out_low, up_part)
    out_part = row_gather(row_scatter(out_part))
    pair_back = jnp.concatenate([key_back, value_back], axis=1)
    back_all = jnp.concatenate([query_back, pair_back], axis=1)
    query_low_grad = low(dot_tn(gathered_in, query_back))
    pair_low_grad = low(dot_tn(gathered_in, pair_back))
    query_part, pair_part, gate_over_y, *acts = tie(
        sum_cores(query_low_grad, core), sum_cores(pair_low_grad, core), gate_over_y, *acts
    )
    back_parts = blocks_of(back_all, 0, 2) if in_pairs else [back_all]
    in_grad = col_scatter(lambda i: dot_nt(back_parts[i], project_in))
    query_part, pair_part, out_part, up_part, in_grad = tie(
        sum_y(query_part, ypos), sum_y(pair_part, ypos), out_part, up_part, in_grad
    )
    both_part = row_scatter(jnp.concatenate([query_part, pair_part], axis=1))
    up_part = up_part.T
    up_over_y = swap(up_part, "grp", 2)
    out_over_y = swap(out_part, "grp", 2)
    out_from_core = near_sum(out_product)
    out_far = far_sum(out_product)

    def out_near(first, last):
        return out_product(0, first, last) + wide(out_from_core[first:last])

    if in_pairs:
        mid_row = packed_length // 2
        across = swap(out_far[mid_row:], "col", 1)
        out_far = low(wide(out_far[:mid_row]) + wide(across))
    both_part, up_over_y, out_over_y, out_far = tie(both_part, up_over_y, out_over_y, out_far)
    from_y = swap(out_far, "grp", 2)
    gate_grad = spread_quarters(gate_part, gate_over_y, core, ypos, 1)
    up_grad = spread_quarters(up_part, up_over_y, core, ypos, 1)
    out_wgrad = spread_quarters(out_part, out_over_y, core, ypos, 0)
    both_part = row_gather(both_part)
    if in_pairs:
        both_part, from_x = tie(
            both_part, swap(low(out_near(mid_row, packed_length)), "col", 1)
        )
    both_part, from_y, gate_grad, up_grad, out_wgrad = tie(
        both_part, from_y, gate_grad, up_grad, out_wgrad
    )
    if in_pairs:
        layer_rows = out_near(0, mid_row) + wide(from_x) + wide(from_y)
    else:
        layer_rows = col_scatter(lambda i: out_near(0, packed_length) + wide(from_y))
    layer_out = hidden_res + layer_rows
    res_from_in, _ = first_back(in_grad)
    input_grad = res_grad + res_from_in

    size = both_part.shape[0]
    project_rows = lax.dynamic_slice_in_dim(project_in, (2 * core + ypos) * size, size, 0)
    term = jnp.sum(wide(both_part) * wide(project_rows), axis=1)
    term = butterfly(term.reshape(8, -1), ("col",)).reshape(-1)
    term = ordered(ypos, term, swap(term, "grp", 2), 0)
    first_gain_grad = ordered(core, term, swap(term, "grp", 1), 0) / first_gain
    query_part, pair_part = both_part[:, :query_cols], both_part[:, query_cols:]
    down_grad = spread_quarters(down_part, down_over_y, core, ypos, 0)
    query_wgrad = spread_quarters(query_part, swap(query_part, "grp", 2), core, ypos, 0)
    if in_pairs:
        over_x, over_y = tie(swap(pair_part, "col", 1), swap(pair_part, "grp", 2))
        across = swap(over_y, "col", 1)
        pair_part = ordered(ypos, pair_part, over_y, 0)
        theirs = ordered(ypos, over_x, across, 0)
        key_part = ordered(col, pair_part[:, :key_cols], theirs[:, :key_cols], 1)
        value_part = ordered(col, pair_part[:, key_cols:], theirs[:, key_cols:], 1)
        key_full = wide(ordered(core, key_part, swap(key_part, "grp", 1), 0))
        value_full = wide(ordered(core, value_part, swap(value_part, "grp", 1), 0))
    else:
        pair_part = ordered(ypos, pair_part, swap(pair_part, "grp", 2), 0)
        pair_part = ordered(core, pair_part, swap(pair_part, "grp", 1), 0)
        pair_all = wide(lax.all_gather(pair_part, "col", axis=0))
        groups = lax.axis_size("col") // head_sharing

        def spread(piece):
            piece = jnp.sum(piece.reshape(groups, head_sharing, width, key_cols), axis=1)
            return jnp.swapaxes(piece, 0, 1).reshape(width, groups * key_cols)

        key_full = spread(pair_all[..., :key_cols])
        value_full = spread(pair_all[..., key_cols:])
    second_gain_grad = butterfly(second_gain_part, ("col",)).reshape(-1)
    return (
        layer_out,
        input_grad,
        first_gain_grad,
        query_wgrad,
        key_full,
        value_full,
        out_wgrad,
        second_gain_grad,
        gate_grad,
        up_grad,
        down_grad,
    )


def solution(mesh):
    return jax.shard_map(
        per_device,
        mesh=mesh,
        in_specs=(
            P(("grp", "row", "col"), None),
            P(("grp", "row", "col"), None),
            P(("grp", "row")),
            P(("grp", "row")),
            P(),
            P(None, "col"),
            P(),
            P(),
            P("col", None),
            P(),
            P(None, ("row", "col")),
            P(None, ("row", "col")),
            P(("row", "col"), None),
        ),
        out_specs=(
            P(("grp", "row", "col"), None),
            P(("grp", "row", "col"), None),
            P(),
            P(None, "col"),
            P(),
            P(),
            P("col", None),
            P(),
            P(None, ("row", "col")),
            P(None, ("row", "col")),
            P(("row", "col"), None),
        ),
        check_vma=False,
    )
```

```python
import math

import jax
import jax.numpy as jnp
from jax import lax
from jax.experimental import pallas as pl
from jax.experimental.pallas import tpu as pltpu
from jax.sharding import PartitionSpec as P

QUERY_HEADS = 8
KEY_VALUE_HEADS = 4
HEAD_SIZE = 256


NORM_EPSILON = 1e-06
ROPE_BASE = 1000042.0
MASKED_SCORE = -1e30


def normalize(values, gain):
    inverse = lax.rsqrt(jnp.mean(values * values, axis=-1, keepdims=True) + NORM_EPSILON)
    return values * inverse * gain


def rope_tables(positions, head_dim):
    half_dim = head_dim // 2
    exponent = jnp.arange(half_dim, dtype=jnp.float32) * (2.0 / head_dim)
    inverse_freq = jnp.exp(-math.log(ROPE_BASE) * exponent)
    angles = positions.astype(jnp.float32)[:, None] * inverse_freq[None, :]
    return (jnp.cos(angles), jnp.sin(angles))


def turn(value, cosine, sine):
    half = value.shape[-1] // 2
    first, second = value[:, :half], value[:, half:]
    return jnp.concatenate(
        [first * cosine - second * sine, second * cosine + first * sine], axis=-1
    )


def kernel_dot(left, right, left_dim, right_dim):
    return lax.dot_general(
        left, right, (((left_dim,), (right_dim,)), ((), ())), preferred_element_type=jnp.float32
    )


def query_spans(length):
    step = length // 4
    return [(i * step, step, (i + 1) * step) for i in range(4)]


def allowed_keys(place, start, size, keys):
    pos_row, pos_col, seg_row, seg_col = place
    key_seg = seg_row[:, :keys]
    return (pos_row[:, :keys] <= pos_col[start : start + size, :]) & (
        (key_seg == 0) | (key_seg == seg_col[start : start + size, :])
    )


def stored_rows(first_ref, length):
    half = length // 2
    offsets = [first_ref[0] * half, (1 - first_ref[0]) * half]

    def rows(start, size):
        offset = pl.multiple_of(offsets[start // half] + start % half, size)
        return pl.ds(offset, size)

    return rows


def attend_kernel(
    first_ref, q_ref, k_ref, v_ref, cos_ref, sin_ref, pr_ref, pc_ref, sr_ref, sc_ref,
    out_ref, q_low_ref, k_low_ref, v_low_ref, key_ref, value_ref,
):
    length, head_dim = k_ref.shape
    rows = stored_rows(first_ref, length)
    place = (pr_ref, pc_ref, sr_ref, sc_ref)
    for start, size, _ in query_spans(length):
        span = slice(start, start + size)
        key = turn(k_ref[rows(start, size), :], cos_ref[span, :], sin_ref[span, :])
        key = key.astype(jnp.bfloat16)
        value = v_ref[rows(start, size), :].astype(jnp.bfloat16)
        key_ref[span, :] = key
        value_ref[span, :] = value
        k_low_ref[rows(start, size), :] = key
        v_low_ref[rows(start, size), :] = value
    for start, size, keys in query_spans(length):
        span = slice(start, start + size)
        allowed = allowed_keys(place, start, size, keys)
        for head in range(q_ref.shape[1] // head_dim):
            cols = slice(head * head_dim, (head + 1) * head_dim)
            query = turn(q_ref[rows(start, size), cols], cos_ref[span, :], sin_ref[span, :])
            query = query.astype(jnp.bfloat16)
            q_low_ref[rows(start, size), cols] = query
            scores = kernel_dot(query, key_ref[:keys, :], 1, 1) * head_dim**-0.5
            scores = jnp.where(allowed, scores, MASKED_SCORE)
            weights = jnp.exp(scores - jnp.max(scores, axis=1, keepdims=True))
            weights = weights * (1 / jnp.sum(weights, axis=1, keepdims=True))
            mixed = kernel_dot(weights.astype(jnp.bfloat16), value_ref[:keys, :], 1, 0)
            out_ref[rows(start, size), cols] = mixed.astype(jnp.bfloat16)


def attend_back_kernel(
    first_ref, q_ref, k_ref, v_ref, m_ref, cos_ref, sin_ref, pr_ref, pc_ref, sr_ref, sc_ref,
    q_back_ref, k_back_ref, v_back_ref, key_ref, value_ref, key_sum, value_sum,
):
    length, head_dim = k_ref.shape
    scale = head_dim**-0.5
    rows = stored_rows(first_ref, length)
    place = (pr_ref, pc_ref, sr_ref, sc_ref)
    for start, size, _ in query_spans(length):
        span = slice(start, start + size)
        key_ref[span, :] = k_ref[rows(start, size), :]
        value_ref[span, :] = v_ref[rows(start, size), :]
    key_sum[...] = jnp.zeros_like(key_sum)
    value_sum[...] = jnp.zeros_like(value_sum)
    for start, size, keys in query_spans(length):
        span = slice(start, start + size)
        allowed = allowed_keys(place, start, size, keys)
        for head in range(q_ref.shape[1] // head_dim):
            cols = slice(head * head_dim, (head + 1) * head_dim)
            query = q_ref[rows(start, size), cols]
            mixed = m_ref[rows(start, size), cols]
            scores = kernel_dot(query, key_ref[:keys, :], 1, 1) * scale
            scores = jnp.where(allowed, scores, MASKED_SCORE)
            probs = jnp.exp(scores - jnp.max(scores, axis=1, keepdims=True))
            probs = probs * (1 / jnp.sum(probs, axis=1, keepdims=True))
            value_sum[:keys, :] += kernel_dot(probs.astype(jnp.bfloat16), mixed, 0, 0)
            prob_grad = kernel_dot(mixed, value_ref[:keys, :], 1, 1)
            row_dot = jnp.sum(probs * prob_grad, axis=1, keepdims=True)
            score_low = (probs * (prob_grad - row_dot)).astype(jnp.bfloat16)
            key_sum[:keys, :] += kernel_dot(score_low, query, 0, 0)
            query_grad = kernel_dot(score_low, key_ref[:keys, :], 1, 0) * scale
            query_grad = turn(query_grad, cos_ref[span, :], -sin_ref[span, :])
            q_back_ref[rows(start, size), cols] = query_grad.astype(jnp.bfloat16)
    for start, size, _ in query_spans(length):
        span = slice(start, start + size)
        key_grad = turn(key_sum[span, :] * scale, cos_ref[span, :], -sin_ref[span, :])
        k_back_ref[rows(start, size), :] = key_grad.astype(jnp.bfloat16)
        v_back_ref[rows(start, size), :] = value_sum[span, :].astype(jnp.bfloat16)


def attention_call(kernel, name, first, heads, tables, outs, scratch, head_dim, flops):
    length = heads[0][0].shape[0]
    key_heads = flops[1]

    def head_spec(width, start):
        return pl.BlockSpec((length, width), lambda g, first_ref: (0, start + g))

    def whole_spec(shape):
        return pl.BlockSpec(shape, lambda g, first_ref: (0, 0))

    return pl.pallas_call(
        kernel,
        grid_spec=pltpu.PrefetchScalarGridSpec(
            num_scalar_prefetch=1,
            grid=(key_heads,),
            in_specs=[head_spec(width, start) for _, width, start in heads]
            + [whole_spec(table.shape) for table in tables],
            out_specs=[head_spec(width, 0) for width in outs],
            scratch_shapes=[pltpu.VMEM((length, head_dim), kind) for kind in scratch],
        ),
        out_shape=[
            jax.ShapeDtypeStruct((length, width * key_heads), jnp.bfloat16) for width in outs
        ],
        cost_estimate=pl.CostEstimate(
            flops=flops[0], bytes_accessed=flops[0] // 200, transcendentals=length * length
        ),
        name=name,
    )(first, *[array for array, _, _ in heads], *tables)


def swap(value, axis, bit):
    count = lax.axis_size(axis)
    return lax.ppermute(value, axis, [(i, i ^ bit) for i in range(count)])


def shift(value, axis, step):
    count = lax.axis_size(axis)
    return lax.ppermute(value, axis, [(i, (i + step) % count) for i in range(count)])


def tie(*values):
    return lax.optimization_barrier(values)


def ordered(first_when_zero, mine, theirs, dim):
    keep = first_when_zero == 0
    return jnp.concatenate(
        [jnp.where(keep, mine, theirs), jnp.where(keep, theirs, mine)], axis=dim
    )


def dot32(left, right):
    return jnp.dot(left, right, preferred_element_type=jnp.float32)


def dot_nt(left, right):
    return jnp.einsum("td,fd->tf", left, right, preferred_element_type=jnp.float32)


def dot_tn(left, right):
    return jnp.einsum("td,tf->df", left, right, preferred_element_type=jnp.float32)


def low(value):
    return value.astype(jnp.bfloat16)


def wide(value):
    return value.astype(jnp.float32)


def col_gather(mine):
    if lax.axis_size("col") == 2:
        return [mine, swap(mine, "col", 1)]
    return [lax.all_gather(mine, "col", axis=0, tiled=True)]


def col_scatter(product):
    if lax.axis_size("col") == 2:
        theirs = swap(low(product(1)), "col", 1)
        return product(0) + wide(theirs)
    return wide(lax.psum_scatter(low(product(0)), "col", scatter_dimension=0, tiled=True))


def blocks_of(value, dim, count):
    size = value.shape[dim] // count
    return [lax.slice_in_dim(value, i * size, (i + 1) * size, axis=dim) for i in range(count)]


def square_gather(mine, beside_first, beside_second):
    if lax.axis_size("col") == 2:
        over_x, over_y, beside_first = tie(
            swap(mine, "col", 1), swap(mine, "grp", 2), beside_first
        )
        half = mine.shape[0] // 2
        across_first, across_second, beside_second = tie(
            swap(over_x[:half], "grp", 2), swap(over_y[half:], "col", 1), beside_second
        )
        near = jnp.concatenate([mine, over_x], axis=0)
        far = jnp.concatenate([over_y, across_first, across_second], axis=0)
        return near, far, beside_first, beside_second
    near = lax.all_gather(mine, "col", axis=0, tiled=True)
    return near, swap(near, "grp", 2), beside_first, beside_second


def with_core(pack):
    return jnp.concatenate([pack, swap(pack, "grp", 1)], axis=0)


def square_scatter(near, far, later):
    size = far.shape[0]
    if lax.axis_size("col") == 2:
        half, part = size // 2, size // 4
        across_first = swap(far[half : half + part], "grp", 2)
        across_second = swap(far[half + part :], "col", 1)
        rest = jnp.zeros_like(across_first)
        to_y = low(wide(far[:half]) + wide(jnp.concatenate([rest, across_second], axis=0)))
        to_x = low(near(half, size) + wide(jnp.concatenate([across_first, rest], axis=0)))
        to_y, to_x, *later = tie(to_y, to_x, *later)
        from_y = swap(to_y, "grp", 2)
        from_x = swap(to_x, "col", 1)
        return near(0, half) + wide(from_x) + wide(from_y), later
    total = low(near(0, size) + wide(swap(far, "grp", 2)))
    return wide(lax.psum_scatter(total, "col", scatter_dimension=0, tiled=True)), later


def butterfly(value, axes):
    for axis in axes:
        bit = 1
        while bit < lax.axis_size(axis):
            value = value + swap(value, axis, bit)
            bit *= 2
    return value


def half_rows(value, bit):
    size = value.shape[0] // 2
    return lax.dynamic_slice_in_dim(value, bit * size, size, 0)


def row_gather(value):
    return lax.all_gather(value, "row", axis=0, tiled=True)


def row_scatter(value):
    return lax.psum_scatter(value, "row", scatter_dimension=0, tiled=True)


def sum_cores(value, core):
    return low(wide(half_rows(value, core)) + wide(swap(half_rows(value, 1 - core), "grp", 1)))


def sum_y(part, ypos):
    part = low(wide(half_rows(part, ypos)) + wide(swap(half_rows(part, 1 - ypos), "grp", 2)))
    return part


def spread_y(part, ypos):
    return ordered(ypos, part, swap(part, "grp", 2), 0)


def spread_core(part, core):
    return ordered(core, part, swap(part, "grp", 1), 0)


def own_quarter(weight, core, ypos):
    size = weight.shape[0] // 4
    return lax.dynamic_slice_in_dim(weight, (2 * core + ypos) * size, size, 0)


def spread_quarters(part, over_y, core, ypos, dim):
    half = ordered(ypos, part, over_y, dim)
    return wide(ordered(core, half, swap(half, "grp", 1), dim))


def per_device(
    tokens,
    cotangent,
    segments,
    positions,
    first_gain,
    query_weight,
    key_matrix,
    value_matrix,
    output_weight,
    second_gain,
    gate_weight,
    up_weight,
    down_weight,
):
    head_dim = HEAD_SIZE
    query_heads = query_weight.shape[1] // head_dim
    heads_per_group = QUERY_HEADS // KEY_VALUE_HEADS
    key_heads = max(1, query_heads // heads_per_group)
    head_share = query_heads // key_heads
    head_sharing = max(1, heads_per_group // query_heads)
    col = lax.axis_index("col")
    key_first = col * query_heads // heads_per_group
    query_cols = query_heads * head_dim
    key_cols = key_heads * head_dim
    rows, width = tokens.shape
    grp, zpos = lax.axis_index("grp"), lax.axis_index("row")
    core, ypos = lax.rem(grp, 2), lax.div(grp, 2)
    in_pairs = lax.axis_size("col") == 2

    inputs = wide(tokens)
    normalized_input, first_back = jax.vjp(normalize, inputs, first_gain)
    gathered_in = jnp.concatenate(col_gather(low(normalized_input)), axis=0)
    packed_length = gathered_in.shape[0]

    down_rows, gate_rows, up_rows = [
        row_gather(own_quarter(weight, core, ypos))
        for weight in (down_weight, gate_weight.T, up_weight.T)
    ]

    gathered_in, cot_now = tie(gathered_in, cotangent)
    cot_near = col_gather(cot_now)
    cot_far = [swap(cotangent, "grp", 2)] if in_pairs else []
    cot_far.append(swap(cot_near[-1], "grp", 2))
    cot_sets = [with_core(jnp.concatenate(pack, axis=0)) for pack in (cot_near, cot_far)]

    key_slice = lax.dynamic_slice_in_dim(key_matrix, key_first * head_dim, key_cols, 1)
    value_slice = lax.dynamic_slice_in_dim(value_matrix, key_first * head_dim, key_cols, 1)
    project_in = jnp.concatenate([query_weight, key_slice, value_slice], axis=1)
    projected = dot32(gathered_in, project_in)
    cosine, sine = rope_tables(positions, head_dim)
    tables = (cosine, sine, positions[None], positions[:, None], segments[None], segments[:, None])
    first = (col if in_pairs else jnp.zeros_like(col)).astype(jnp.int32).reshape(1)
    group_cols = head_share * head_dim
    score_flops = query_cols * packed_length * packed_length
    attn_low, query_low, key_low, value_low = attention_call(
        attend_kernel,
        "attend",
        first,
        [
            (projected, group_cols, 0),
            (projected, head_dim, query_heads),
            (projected, head_dim, query_heads + key_heads),
        ],
        tables,
        (group_cols, group_cols, head_dim, head_dim),
        (jnp.bfloat16, jnp.bfloat16),
        head_dim,
        (3 * score_flops, key_heads),
    )
    attn_low, down_rows = tie(attn_low, down_rows)
    act_near = low(dot_nt(cot_sets[0], down_rows))
    act_far = low(dot_nt(cot_sets[1], down_rows))
    attn_parts = blocks_of(attn_low, 0, 2) if in_pairs else [attn_low]
    hidden_res = inputs + col_scatter(lambda i: dot32(attn_parts[i], output_weight))
    normed_mid, second_back = jax.vjp(normalize, hidden_res, second_gain)

    mid_near, mid_far, act_near, act_far = square_gather(low(normed_mid), act_near, act_far)
    mid_sets = [with_core(mid_near), with_core(mid_far)]
    gate_lins = [low(dot_nt(mid, gate_rows)) for mid in mid_sets]
    act_grads = [act_near, act_far]
    acts, gate_backs, up_backs = [], [], []
    for mid, act_grad, gate_lin in zip(mid_sets, act_grads, gate_lins):
        gate32 = wide(gate_lin)
        up_lin = dot_nt(mid, up_rows)
        sig = jax.nn.sigmoid(gate32)
        acts.append(low(gate32 * sig * up_lin))
        gate_backs.append(low(wide(act_grad) * up_lin * sig * (1 + gate32 * (1 - sig))))
        up_backs.append(low(wide(act_grad) * gate32 * sig))

    def weight_sum(lefts, rights):
        return low(sum(dot_tn(left, right) for left, right in zip(lefts, rights)))

    def far_sum(product):
        pack = packed_length
        theirs = swap(low(product(1, pack, 2 * pack)), "grp", 1)
        return low(product(1, 0, pack) + wide(theirs))

    def near_sum(product):
        pack = packed_length
        return swap(low(product(0, pack, 2 * pack)), "grp", 1)

    def mid_product(i, a, b):
        return dot32(gate_backs[i][a:b], gate_rows) + dot32(up_backs[i][a:b], up_rows)

    def out_product(i, a, b):
        return dot32(acts[i][a:b], down_rows)

    down_low = weight_sum(acts, cot_sets)
    down_low, gate_backs[1], up_backs[1] = tie(down_low, gate_backs[1], up_backs[1])
    down_part = row_scatter(down_low)
    mid_from_core = near_sum(mid_product)
    mid_far_sum = far_sum(mid_product)
    mid_far_sum, gate_backs[0], up_backs[0] = tie(mid_far_sum, gate_backs[0], up_backs[0])
    mid_grad, (gate_backs[1],) = square_scatter(
        lambda first, last: mid_product(0, first, last) + wide(mid_from_core[first:last]),
        mid_far_sum,
        [gate_backs[1]],
    )
    gate_part = row_scatter(weight_sum(gate_backs, mid_sets))
    res_from_mid, second_gain_part = second_back(mid_grad)
    res_grad = wide(cotangent) + res_from_mid
    res_low, down_part, second_gain_part, *up_backs = tie(
        low(res_grad), down_part, second_gain_part, *up_backs
    )
    up_part = row_scatter(weight_sum(up_backs, mid_sets))
    second_gain_part = butterfly(second_gain_part.reshape(8, -1), ("grp", "row"))
    shard_rows = jnp.concatenate(col_gather(res_low), axis=0)
    down_over_y = swap(down_part, "grp", 2)
    shard_rows, gate_part, down_over_y, second_gain_part = tie(
        shard_rows, gate_part, down_over_y, second_gain_part
    )
    gate_part = gate_part.T
    gate_over_y = swap(gate_part, "grp", 2)

    mixed_low = low(dot_nt(shard_rows, output_weight))
    out_low = low(dot_tn(attn_low, shard_rows))
    mixed_low, out_low = tie(mixed_low, sum_cores(out_low, core))
    out_low = sum_y(out_low, ypos)
    query_back, key_back, value_back = attention_call(
        attend_back_kernel,
        "attend_back",
        first,
        [
            (query_low, group_cols, 0),
            (key_low, head_dim, 0),
            (value_low, head_dim, 0),
            (mixed_low, group_cols, 0),
        ],
        tables,
        (group_cols, head_dim, head_dim),
        (jnp.bfloat16, jnp.bfloat16, jnp.float32, jnp.float32),
        head_dim,
        (7 * score_flops, key_heads),
    )
    query_back, out_low = tie(query_back, out_low)
    out_part, up_part = tie(out_low, up_part)
    out_part = row_gather(row_scatter(out_part))
    pair_back = jnp.concatenate([key_back, value_back], axis=1)
    back_all = jnp.concatenate([query_back, pair_back], axis=1)
    query_low_grad = low(dot_tn(gathered_in, query_back))
    pair_low_grad = low(dot_tn(gathered_in, pair_back))
    query_part, pair_part, gate_over_y, *acts = tie(
        sum_cores(query_low_grad, core), sum_cores(pair_low_grad, core), gate_over_y, *acts
    )
    back_parts = blocks_of(back_all, 0, 2) if in_pairs else [back_all]
    in_grad = col_scatter(lambda i: dot_nt(back_parts[i], project_in))
    query_part, pair_part, out_part, up_part, in_grad = tie(
        sum_y(query_part, ypos), sum_y(pair_part, ypos), out_part, up_part, in_grad
    )
    both_part = row_scatter(jnp.concatenate([query_part, pair_part], axis=1))
    up_part = up_part.T
    up_over_y = swap(up_part, "grp", 2)
    out_over_y = swap(out_part, "grp", 2)
    out_from_core = near_sum(out_product)
    out_far = far_sum(out_product)

    def out_near(first, last):
        return out_product(0, first, last) + wide(out_from_core[first:last])

    if in_pairs:
        mid_row = packed_length // 2
        across = swap(out_far[mid_row:], "col", 1)
        out_far = low(wide(out_far[:mid_row]) + wide(across))
    both_part, up_over_y, out_over_y, out_far = tie(both_part, up_over_y, out_over_y, out_far)
    from_y = wide(swap(out_far, "grp", 2))
    if in_pairs:
        from_x = wide(swap(low(out_near(mid_row, packed_length)), "col", 1))
        layer_rows = out_near(0, mid_row) + from_x + from_y
    else:
        layer_rows = col_scatter(lambda i: out_near(0, packed_length) + from_y)
    layer_out = hidden_res + layer_rows
    res_from_in, _ = first_back(in_grad)
    input_grad = res_grad + res_from_in

    both_part, layer_out, input_grad = tie(row_gather(both_part), layer_out, input_grad)
    size = both_part.shape[0]
    project_rows = lax.dynamic_slice_in_dim(project_in, (2 * core + ypos) * size, size, 0)
    term = jnp.sum(wide(both_part) * wide(project_rows), axis=1)
    term = butterfly(term.reshape(8, -1), ("col",)).reshape(-1)
    term = ordered(ypos, term, swap(term, "grp", 2), 0)
    first_gain_grad = ordered(core, term, swap(term, "grp", 1), 0) / first_gain
    query_part, pair_part = both_part[:, :query_cols], both_part[:, query_cols:]
    down_grad = spread_quarters(down_part, down_over_y, core, ypos, 0)
    gate_grad = spread_quarters(gate_part, gate_over_y, core, ypos, 1)
    up_grad = spread_quarters(up_part, up_over_y, core, ypos, 1)
    out_wgrad = spread_quarters(out_part, out_over_y, core, ypos, 0)
    query_wgrad = spread_quarters(query_part, swap(query_part, "grp", 2), core, ypos, 0)
    if in_pairs:
        over_x, over_y = tie(swap(pair_part, "col", 1), swap(pair_part, "grp", 2))
        across = swap(over_y, "col", 1)
        pair_part = ordered(ypos, pair_part, over_y, 0)
        theirs = ordered(ypos, over_x, across, 0)
        key_part = ordered(col, pair_part[:, :key_cols], theirs[:, :key_cols], 1)
        value_part = ordered(col, pair_part[:, key_cols:], theirs[:, key_cols:], 1)
        key_full = wide(ordered(core, key_part, swap(key_part, "grp", 1), 0))
        value_full = wide(ordered(core, value_part, swap(value_part, "grp", 1), 0))
    else:
        pair_part = ordered(ypos, pair_part, swap(pair_part, "grp", 2), 0)
        pair_part = ordered(core, pair_part, swap(pair_part, "grp", 1), 0)
        pair_all = wide(lax.all_gather(pair_part, "col", axis=0))
        groups = lax.axis_size("col") // head_sharing

        def spread(piece):
            piece = jnp.sum(piece.reshape(groups, head_sharing, width, key_cols), axis=1)
            return jnp.swapaxes(piece, 0, 1).reshape(width, groups * key_cols)

        key_full = spread(pair_all[..., :key_cols])
        value_full = spread(pair_all[..., key_cols:])
    second_gain_grad = butterfly(second_gain_part, ("col",)).reshape(-1)
    return (
        layer_out,
        input_grad,
        first_gain_grad,
        query_wgrad,
        key_full,
        value_full,
        out_wgrad,
        second_gain_grad,
        gate_grad,
        up_grad,
        down_grad,
    )


def solution(mesh):
    return jax.shard_map(
        per_device,
        mesh=mesh,
        in_specs=(
            P(("grp", "row", "col"), None),
            P(("grp", "row", "col"), None),
            P(("grp", "row")),
            P(("grp", "row")),
            P(),
            P(None, "col"),
            P(),
            P(),
            P("col", None),
            P(),
            P(None, ("row", "col")),
            P(None, ("row", "col")),
            P(("row", "col"), None),
        ),
        out_specs=(
            P(("grp", "row", "col"), None),
            P(("grp", "row", "col"), None),
            P(),
            P(None, "col"),
            P(),
            P(),
            P("col", None),
            P(),
            P(None, ("row", "col")),
            P(None, ("row", "col")),
            P(("row", "col"), None),
        ),
        check_vma=False,
    )
```
